32 devices in a mesh: dp: 8 (over z, x), tensor: 4 (over y, core).
Axes of the slice: x: 2, y: 2, z: 4, core: 2. Of those that a mesh axis runs over, the one named last changes fastest.
Arguments:
- layer_input: bfloat16 [16, 512, 768], P('dp', 'tensor'), may hold values from -6 to 6
- doc_lengths: int32 [16, 8], P('dp'), may hold values from 1 to 256, 512 in all within a row
- norm1_gain: float32 [768], replicated, may hold values from 0.5 to 1.5
- alpha_raw: float32 [16, 768], replicated, may hold values from -4.5 to 0.5
- delta_raw: float32 [16, 768], replicated, may hold values from -4.5 to 0.5
- ema_beta: float32 [16, 768], replicated, may hold values from -5 to 5
- ema_eta: float32 [16, 768], replicated, may hold values from -1.5 to 1.5
- ema_omega: float32 [768], replicated, may hold values from -4 to 4
- w_z: bfloat16 [768, 128], replicated, may hold values from -0.21875 to 0.21875
- q_gain: float32 [128], replicated, may hold values from -3.2 to 3.2
- q_bias: float32 [128], replicated, may hold values from -4 to 4
- k_gain: float32 [128], replicated, may hold values from -3.2 to 3.2
- w_value: bfloat16 [768, 1536], P(None, 'tensor'), may hold values from -0.21875 to 0.21875
- w_reset: bfloat16 [768, 1536], P(None, 'tensor'), may hold values from -0.21875 to 0.21875
- w_update: bfloat16 [768, 768], replicated, may hold values from -0.21875 to 0.21875
- w_hidden: bfloat16 [768, 768], P('tensor'), may hold values from -0.21875 to 0.21875
- w_out: bfloat16 [1536, 768], P('tensor'), may hold values from -0.625 to 0.625
- norm2_gain: float32 [768], replicated, may hold values from 0.5 to 1.5
- w_ffn_in: bfloat16 [768, 1536], P(None, 'tensor'), may hold values from -0.21875 to 0.21875
- w_ffn_out: bfloat16 [1536, 768], P('tensor'), may hold values from -0.15625 to 0.15625
- cotangent: bfloat16 [16, 512, 768], P('dp', 'tensor'), may hold values from -6 to 6
Outputs:
- layer_output: bfloat16 [16, 512, 768], P('dp', 'tensor')
- input_grad: bfloat16 [16, 512, 768], P('dp', 'tensor')
- norm1_gain_grad: float32 [768], replicated
- alpha_raw_grad: float32 [16, 768], replicated
- delta_raw_grad: float32 [16, 768], replicated
- ema_beta_grad: float32 [16, 768], replicated
- ema_eta_grad: float32 [16, 768], replicated
- ema_omega_grad: float32 [768], replicated
- w_z_grad: float32 [768, 128], replicated
- q_gain_grad: float32 [128], replicated
- q_bias_grad: float32 [128], replicated
- k_gain_grad: float32 [128], replicated
- w_value_grad: float32 [768, 1536], P(None, 'tensor')
- w_reset_grad: float32 [768, 1536], P(None, 'tensor')
- w_update_grad: float32 [768, 768], replicated
- w_hidden_grad: float32 [768, 768], P('tensor')
- w_out_grad: float32 [1536, 768], P('tensor')
- norm2_gain_grad: float32 [768], replicated
- w_ffn_in_grad: float32 [768, 1536], P(None, 'tensor')
- w_ffn_out_grad: float32 [1536, 768], P('tensor')
The draws below stay inside these ranges and needn't reach their ends.
Inputs may be any that keep to these rules, and one draw needn't show every extreme that they name: `doc_lengths`: the 8 lengths of each row sum to 512, and the longest of each row is 256.
All inputs are finite; a program needn't handle non-finite values.
Results may differ from the reference program's by a relative error of at most 0.017.
Values may be sent and summed in bfloat16 or wider, within the bound.
No kernel may reach another device: no remote copies, remote signals or barrier semaphores. Data moves between devices by JAX's collectives and lax.ppermute only.
A program may use at most 256 MiB of HBM per device.

```python
import math
import jax
import jax.numpy as jnp
import numpy as np
from jax import lax

D = 768
ZD = 128
VD = 1536
NDIM = 16
FF = 1536
STRETCH = 128
NDOC = 8
LEN = 512
ROWS = 16


def block_levels(rng, extent, pieces, smallest, top_value):
    level, own = 1.0, jax.random.fold_in(rng, 6)
    for dim, shards_of in pieces:
        draws = jnp.exp(jax.random.uniform(jax.random.fold_in(own, dim), (shards_of,), jnp.float32, smallest / len(pieces), top_value / len(pieces)))
        level = level * jnp.repeat(draws, extent[dim] // shards_of).reshape([-1 if axis == dim else 1 for axis in range(len(extent))])
    return level


def split_up(number_of, total, bound, slope):
    loads = [(1 << 20) // math.isqrt(standing ** slope) + 1 for standing in range(2, number_of + 1)]
    spare, given = total - bound - (number_of - 1), [1] * (number_of - 1)
    while spare > 0:
        candidates = [i for i in range(number_of - 1) if given[i] < bound]
        whole, remaining = sum([loads[i] for i in candidates]), spare
        for i in candidates:
            extra = min(bound - given[i], max(1, remaining * loads[i] // whole), spare)
            given[i] = given[i] + extra
            spare = spare - extra
    return np.array([bound] + given)


def uneven(stream_key, amount, total, reach, slope):
    if amount == 2:
        one = jax.random.randint(stream_key, (), max(1, total - reach), min(reach, total - 1) + 1)
        return jnp.stack([one, total - one])
    tallies = jnp.asarray(split_up(amount, total, reach, slope), jnp.int32)
    twos = (amount - 1) // 2
    donor, taker = tallies[1:1 + 2 * twos:2], tallies[2:2 + 2 * twos:2]
    room = jnp.minimum(donor - 1, reach - taker)
    moved = jax.random.randint(jax.random.fold_in(stream_key, 1), (twos,), 0, 1 << 20) % (room + 1)
    tallies = tallies.at[1:1 + 2 * twos:2].set(donor - moved).at[2:2 + 2 * twos:2].set(taker + moved)
    return tallies[jax.random.permutation(jax.random.fold_in(stream_key, 2), amount)]


def bell_draw(own_key, dims, scale, reach, shards=(), held_as=jnp.bfloat16):
    level = block_levels(own_key, dims, shards, -0.22, 0.18) if shards else 1.0
    array = jax.random.normal(own_key, dims, jnp.float32) * scale * level
    return jnp.minimum(jnp.maximum(array, -reach), reach).astype(held_as)


def setup_inputs(seed: int = 0) -> dict:
    key_of = jax.random.split(jax.random.key(seed), 22)
    layer_input = bell_draw(key_of[0], (ROWS, LEN, D), 1.0, 6.0, ((0, 8), (1, 4)))
    doc_lengths = jax.vmap(lambda own: uneven(own, NDOC, LEN, LEN // 2, 2))(jax.random.split(key_of[1], ROWS)).reshape((ROWS, NDOC)).astype(jnp.int32)
    norm1_gain = jnp.clip(1.0 + 0.1 * jax.random.normal(key_of[2], (D,), jnp.float32), 0.5, 1.5)
    alpha_raw = jnp.clip(jax.random.uniform(key_of[3], (NDIM, D), jnp.float32, -4.5, 0.5), -4.5, 0.5)
    delta_raw = jnp.clip(jax.random.uniform(key_of[4], (NDIM, D), jnp.float32, -4.5, 0.5), -4.5, 0.5)
    ema_beta = bell_draw(key_of[5], (NDIM, D), 1.0, 5.0, (), jnp.float32)
    ema_eta = bell_draw(key_of[6], (NDIM, D), NDIM ** -0.5, 1.5, (), jnp.float32)
    ema_omega = bell_draw(key_of[7], (D,), 1.0, 4.0, (), jnp.float32)
    w_z = bell_draw(key_of[8], (D, ZD), D ** -0.5, 0.21875)
    q_gain = bell_draw(key_of[9], (ZD,), 0.8, 3.2, (), jnp.float32)
    q_bias = bell_draw(key_of[10], (ZD,), 1.0, 4.0, (), jnp.float32)
    k_gain = bell_draw(key_of[11], (ZD,), 0.8, 3.2, (), jnp.float32)
    w_value = bell_draw(key_of[12], (D, VD), D ** -0.5, 0.21875, ((1, 4),))
    w_reset = bell_draw(key_of[13], (D, VD), D ** -0.5, 0.21875, ((1, 4),))
    w_update = bell_draw(key_of[14], (D, D), D ** -0.5, 0.21875)
    w_hidden = bell_draw(key_of[15], (D, D), D ** -0.5, 0.21875, ((0, 4),))
    w_out = bell_draw(key_of[16], (VD, D), (VD // 16) ** -0.5, 0.625, ((0, 4),))
    norm2_gain = jnp.clip(1.0 + 0.1 * jax.random.normal(key_of[17], (D,), jnp.float32), 0.5, 1.5)
    w_ffn_in = bell_draw(key_of[18], (D, FF), D ** -0.5, 0.21875, ((1, 4),))
    w_ffn_out = bell_draw(key_of[19], (FF, D), FF ** -0.5, 0.15625, ((0, 4),))
    cotangent = bell_draw(key_of[20], (ROWS, LEN, D), 1.0, 6.0, ((0, 8), (1, 4)))
    return dict(layer_input=layer_input, doc_lengths=doc_lengths, norm1_gain=norm1_gain, alpha_raw=alpha_raw, delta_raw=delta_raw, ema_beta=ema_beta, ema_eta=ema_eta, ema_omega=ema_omega, w_z=w_z, q_gain=q_gain, q_bias=q_bias, k_gain=k_gain, w_value=w_value, w_reset=w_reset, w_update=w_update, w_hidden=w_hidden, w_out=w_out, norm2_gain=norm2_gain, w_ffn_in=w_ffn_in, w_ffn_out=w_ffn_out, cotangent=cotangent)


@jax.custom_vjp
def low(v):
    return lax.optimization_barrier(v.astype(jnp.bfloat16)).astype(jnp.float32)

@jax.custom_vjp
def low_back(v):
    return v

def low_keep(v):
    return (low(v), None)

def low_pass(kept, grad):
    return (grad,)

def back_keep(v):
    return (v, None)

def back_low(kept, grad):
    return (low(grad),)
low.defvjp(low_keep, low_pass)
low_back.defvjp(back_keep, back_low)
highest = lax.Precision.HIGHEST

def matmul(left, right):
    return jnp.dot(left, right, precision=highest, preferred_element_type=jnp.float32)

def silu(value):
    return value * jax.nn.sigmoid(value)

def layer_norm(value, gain):
    center = value - lax.optimization_barrier(jnp.mean(value, -1, keepdims=True))
    spread = lax.optimization_barrier(jnp.mean(center * center, -1, keepdims=True))
    return center * lax.rsqrt(spread + 1e-05) * gain

def doc_layout(lengths):
    sizes_int = lengths.astype(jnp.int32)
    ends = jnp.cumsum(sizes_int, dtype=jnp.int32).astype(jnp.int32)
    starts = (ends - sizes_int).astype(jnp.int32)
    places = jnp.arange(LEN, dtype=jnp.int32)
    docid = lax.optimization_barrier(jnp.sum((places[:, None] >= ends[None, :]).astype(jnp.int32), 1, dtype=jnp.int32)).astype(jnp.int32)
    fresh = jnp.any(places[:, None] == starts[None, :], 1)
    return (docid, 1.0 - fresh.astype(jnp.float32))

def row_forward(params, row_input, docid, keep):
    norm1_gain, alpha_raw, delta_raw, ema_beta, ema_eta, ema_omega, w_z, q_gain, q_bias, k_gain, w_value, w_reset, w_update, w_hidden, w_out, norm2_gain, w_ffn_in, w_ffn_out = params
    normed = layer_norm(row_input, norm1_gain)
    alpha = jax.nn.sigmoid(alpha_raw)
    decay = 1.0 - alpha * jax.nn.sigmoid(delta_raw)
    drive = alpha * ema_beta

    def advance(state, paired):
        token, kept = paired
        state = kept * decay * state + drive * token[None, :]
        return (state, lax.optimization_barrier(jnp.sum(ema_eta * state, 0)))
    start_state = jnp.zeros((NDIM, D), normed.dtype)
    _, smooth = lax.scan(jax.checkpoint(advance), start_state, (normed, keep.astype(normed.dtype)))
    mixed = silu(smooth + ema_omega * normed)
    normed_low = low(normed)
    mixed_low = low(mixed)
    z_low = low(silu(low_back(matmul(mixed_low, w_z))))
    queries = low(z_low * q_gain + q_bias)
    key_low = low(z_low * k_gain)
    values = low(silu(low_back(matmul(normed_low, w_value))))
    reset_gate = silu(low_back(matmul(mixed_low, w_reset)))
    gate_open = jax.nn.sigmoid(low_back(matmul(mixed_low, w_update)))
    blocks = LEN // STRETCH
    scores = jnp.einsum('cqz,ckz->cqk', queries.reshape(blocks, STRETCH, ZD), key_low.reshape(blocks, STRETCH, ZD), precision=highest) * ZD ** (-0.5)
    doc_blocks = docid.reshape(blocks, STRETCH)
    place_index = jnp.arange(STRETCH, dtype=jnp.int32)
    allowed = (place_index[None, :] <= place_index[:, None])[None] & (doc_blocks[:, :, None] == doc_blocks[:, None, :])
    scores = jnp.where(allowed, scores, -1e+30)
    shifted = jnp.exp(scores - lax.optimization_barrier(jnp.max(scores, -1, keepdims=True)))
    weights_low = low(shifted / lax.optimization_barrier(jnp.sum(shifted, -1, keepdims=True)))
    attended = low_back(jnp.einsum('cqk,ckv->cqv', weights_low, values.reshape(blocks, STRETCH, VD), precision=highest)).reshape(LEN, VD)
    united = low(reset_gate * attended)
    hidden = silu(low_back(matmul(mixed_low, w_hidden) + matmul(united, w_out)))
    blended = row_input + gate_open * (hidden - row_input)
    second = low(layer_norm(blended, norm2_gain))
    activated = low(silu(low_back(matmul(second, w_ffn_in))))
    return blended + low_back(matmul(activated, w_ffn_out))

def reference(layer_input, doc_lengths, norm1_gain, alpha_raw, delta_raw, ema_beta, ema_eta, ema_omega, w_z, q_gain, q_bias, k_gain, w_value, w_reset, w_update, w_hidden, w_out, norm2_gain, w_ffn_in, w_ffn_out, cotangent):
    params = tuple((weight_arg.astype(jnp.float32) for weight_arg in (norm1_gain, alpha_raw, delta_raw, ema_beta, ema_eta, ema_omega, w_z, q_gain, q_bias, k_gain, w_value, w_reset, w_update, w_hidden, w_out, norm2_gain, w_ffn_in, w_ffn_out)))

    def per_row(totals, row_items):
        row_input, lengths, row_cot = row_items
        docid, keep = doc_layout(lengths)

        def forward(weights, inputs):
            return row_forward(weights, inputs, docid, keep)
        result, backward = jax.vjp(forward, params, row_input.astype(jnp.float32))
        weight_grads, row_grad = backward(row_cot.astype(jnp.float32))
        totals = jax.tree.map(lambda left, right: left + right, totals, weight_grads)
        return (totals, (result.astype(jnp.bfloat16), row_grad.astype(jnp.bfloat16)))
    start = jax.tree.map(jnp.zeros_like, params)
    grads, (outputs, input_grads) = lax.scan(per_row, start, (layer_input, doc_lengths.astype(jnp.int32), cotangent))
    return (outputs, input_grads, grads[0], grads[1], grads[2], grads[3], grads[4], grads[5], grads[6], grads[7], grads[8], grads[9], grads[10], grads[11], grads[12], grads[13], grads[14], grads[15], grads[16], grads[17])
```

```python
import functools

import jax
import jax.numpy as jnp
from jax import lax
from jax.experimental import pallas as pl
from jax.experimental.pallas import tpu as pltpu
from jax.sharding import PartitionSpec as P

STRETCH = 128
LANES = 128
CHUNKS = 8
F32 = jnp.float32
LOW = jnp.bfloat16


def silu(v):
    return v * jax.nn.sigmoid(v)


def silu_slope(v):
    s = jax.nn.sigmoid(v)
    return s * (1.0 + v * (1.0 - s))


def dot(a, b):
    return jnp.dot(a, b, preferred_element_type=F32)


def dot_rows(a, b):
    return lax.dot_general(a, b, (((0,), (0,)), ((), ())), preferred_element_type=F32)


def dot_cols(a, b):
    return lax.dot_general(a, b, (((1,), (1,)), ((), ())), preferred_element_type=F32)


def norm_parts(v):
    center = v - jnp.mean(v, -1, keepdims=True)
    scale = lax.rsqrt(jnp.mean(center * center, -1, keepdims=True) + 1e-05)
    return center * scale, scale


def norm_back(grad, hat, scale):
    return scale * (
        grad - jnp.mean(grad, -1, keepdims=True) - hat * jnp.mean(grad * hat, -1, keepdims=True)
    )


def call(kernel, outs, args, flops, scratch=(), smem=(), limit=48 << 20):
    specs = [
        pl.BlockSpec(memory_space=pltpu.SMEM if i in smem else pltpu.VMEM)
        for i in range(len(args))
    ]
    outs = [jax.ShapeDtypeStruct(s, d) for s, d in outs]
    size = sum(a.size * a.dtype.itemsize for a in args) + sum(
        o.size * o.dtype.itemsize for o in outs
    )
    return pl.pallas_call(
        kernel,
        out_shape=outs,
        in_specs=specs,
        out_specs=[pl.BlockSpec(memory_space=pltpu.VMEM) for _ in outs],
        scratch_shapes=list(scratch),
        compiler_params=pltpu.CompilerParams(vmem_limit_bytes=limit),
        cost_estimate=pl.CostEstimate(flops=int(flops), bytes_accessed=int(size), transcendentals=0),
    )(*args)


def bcast(ref, row, lanes):
    return jnp.broadcast_to(ref[pl.ds(row, 1), lanes], (CHUNKS, LANES))


def shifted(v, by, fill):
    place = lax.broadcasted_iota(jnp.int32, v.shape, 0)
    if by > 0:
        return jnp.where(place >= by, pltpu.roll(v, by, 0), fill)
    return jnp.where(place < CHUNKS + by, pltpu.roll(v, CHUNKS + by, 0), fill)


def power(v, n):
    out = None
    while n:
        if n & 1:
            out = v if out is None else out * v
        n >>= 1
        if n:
            v = v * v
    return out


def chunk_powers(base, order):
    place = lax.broadcasted_iota(jnp.int32, base.shape, 0)
    place = place if order > 0 else (CHUNKS - 1) - place
    out = jnp.where(place & 1 == 1, base, 1.0)
    base = base * base
    out = out * jnp.where(place & 2 == 2, base, 1.0)
    base = base * base
    return out * jnp.where(place & 4 == 4, base, 1.0)


def rate_tables(al_ref, de_ref, be_ref, dec_ref, drv_ref):
    alpha = jax.nn.sigmoid(al_ref[...])
    dec_ref[...] = 1.0 - alpha * jax.nn.sigmoid(de_ref[...])
    drv_ref[...] = alpha * be_ref[...]


def steps_of(ref, base, steps):
    return [ref[pl.ds(base + k, CHUNKS, stride=steps), :] for k in range(steps)]


def into_slabs(ref, v):
    tokens = v.shape[0]
    for j in range(v.shape[1] // LANES):
        ref[j * tokens : (j + 1) * tokens, :] = v[:, j * LANES : (j + 1) * LANES]


def from_slabs(v, tokens):
    return jnp.concatenate(
        [v[at : at + tokens] for at in range(0, v.shape[0], tokens)], 1
    )


def product(values):
    out = values[0]
    for v in values[1:]:
        out = out * v
    return out


def first_pass(rows, x_ref, g_ref, al_ref, de_ref, be_ref, keep_ref, normed_ref, low_ref, init_ref, last_ref, dec_ref, drv_ref):
    hat, _ = norm_parts(x_ref[...].astype(F32))
    normed = hat * g_ref[...]
    into_slabs(normed_ref, normed)
    low_ref[...] = normed.astype(LOW)
    rate_tables(al_ref, de_ref, be_ref, dec_ref, drv_ref)
    dims, width = al_ref.shape
    tokens = x_ref.shape[0]
    length = tokens // rows
    steps = length // CHUNKS

    def lane(j, carry):
        lanes = pl.ds(pl.multiple_of(j * LANES, LANES), LANES)
        for row in range(rows):
            token = steps_of(normed_ref, j * tokens + row * length, steps)
            kept = steps_of(keep_ref, row * length, steps)
            whole = product(kept)
            for n in range(dims):
                d, b = bcast(dec_ref, n, lanes), bcast(drv_ref, n, lanes)
                s = b * token[0]
                for k in range(1, steps):
                    s = (kept[k] * d) * s + b * token[k]
                a = power(d, steps) * whole
                for by in (1, 2, 4):
                    s = s + a * shifted(s, by, 0.0)
                    a = a * shifted(a, by, 1.0)
                init_ref[pl.ds((row * dims + n) * CHUNKS, CHUNKS), lanes] = shifted(s, 1, 0.0)
                last_ref[pl.ds(row * dims + n, 1), lanes] = s[CHUNKS - 1 :, :]
        return carry

    lax.fori_loop(0, width // LANES, lane, 0)


def second_pass(rows, normed_ref, init_ref, f1_ref, f2_ref, keep_ref, flag_ref, al_ref, de_ref, be_ref, eta_ref, om_ref, wz_ref, wu_ref, qg_ref, qb_ref, kg_ref, mask_ref, pre_ref, mixed_ref, zpre_ref, gate_ref, probs_ref, dec_ref, drv_ref):
    rate_tables(al_ref, de_ref, be_ref, dec_ref, drv_ref)
    dims, width = al_ref.shape
    tokens = keep_ref.shape[0]
    length = tokens // rows
    steps = length // CHUNKS

    def lane(j, carry):
        lanes = pl.ds(pl.multiple_of(j * LANES, LANES), LANES)
        omega = bcast(om_ref, 0, lanes)
        for row in range(rows):
            base = j * tokens + row * length
            token = steps_of(normed_ref, base, steps)
            kept = steps_of(keep_ref, row * length, steps)
            reach = shifted(product(kept), 1, 1.0)
            for by in (1, 2, 4):
                reach = reach * shifted(reach, by, 1.0)
            flag = bcast(flag_ref, row, pl.ds(0, LANES))
            total = [omega * t for t in token]
            for n in range(dims):
                d, b, e = bcast(dec_ref, n, lanes), bcast(drv_ref, n, lanes), bcast(eta_ref, n, lanes)
                chunk = power(d, steps)
                entering = bcast(f1_ref, row * dims + n, lanes) + (
                    power(chunk, CHUNKS) * flag
                ) * bcast(f2_ref, row * dims + n, lanes)
                s = (
                    init_ref[pl.ds((row * dims + n) * CHUNKS, CHUNKS), lanes]
                    + reach * chunk_powers(chunk, 1) * entering
                )
                for k in range(steps):
                    s = (kept[k] * d) * s + b * token[k]
                    total[k] = total[k] + e * s
            for k in range(steps):
                pre_ref[pl.ds(base + k, CHUNKS, stride=steps), :] = total[k]
        return carry

    lax.fori_loop(0, width // LANES, lane, 0)
    mixed_low = from_slabs(silu(pre_ref[...]).astype(LOW), tokens)
    mixed_ref[...] = mixed_low
    z_pre = dot(mixed_low, wz_ref[...])
    zpre_ref[...] = z_pre
    gate_ref[...] = jax.nn.sigmoid(dot(mixed_low, wu_ref[...]))
    z_low = silu(z_pre).astype(LOW).astype(F32)
    queries = (z_low * qg_ref[...] + qb_ref[...]).astype(LOW)
    keys = (z_low * kg_ref[...]).astype(LOW)
    for start in range(0, z_low.shape[0], STRETCH):
        block = slice(start, start + STRETCH)
        scores = dot_cols(queries[block], keys[block]) * z_low.shape[1] ** (-0.5)
        scores = jnp.where(mask_ref[block, :] > 0.5, scores, -1e30)
        shift = jnp.exp(scores - jnp.max(scores, -1, keepdims=True))
        probs_ref[block, :] = shift / jnp.sum(shift, -1, keepdims=True)


def value_part(normed_ref, mixed_ref, probs_ref, wa_ref, wb_ref, vpre_ref, rpre_ref, att_ref, united_ref):
    depth = normed_ref.shape[1]
    tokens = normed_ref.shape[0]
    for i, w_ref in enumerate((wa_ref, wb_ref)):
        value_pre = dot(normed_ref[...], w_ref[:depth, :])
        reset_pre = dot(mixed_ref[...], w_ref[depth:, :])
        vpre_ref[i] = value_pre
        rpre_ref[i] = reset_pre
        values = silu(value_pre).astype(LOW)
        for start in range(0, tokens, STRETCH):
            block = slice(start, start + STRETCH)
            att_ref[i, block, :] = dot(probs_ref[block, :].astype(LOW), values[block])
        united_ref[i] = (silu(reset_pre) * att_ref[i]).astype(LOW)


def blend_part(offs_ref, x_ref, mixed_ref, gate_ref, u0_ref, u1_ref, g0_ref, g1_ref, g2_ref, g3_ref, gain_ref, hpre_ref, blended_ref, second_ref, whid_ref):
    cols = whid_ref.shape[0] // 4
    packs = (g0_ref, g1_ref, g2_ref, g3_ref)
    for r, g_ref in enumerate(packs):
        whid_ref[pl.ds(pl.multiple_of(offs_ref[r], 64), cols), :] = g_ref[:cols, :]
    hidden_pre = dot(mixed_ref[...], whid_ref[...])
    for r, g_ref in enumerate(packs):
        united = (u0_ref, u1_ref)[r // 2][r % 2]
        hidden_pre = hidden_pre + dot(united, g_ref[cols:, :])
    hpre_ref[...] = hidden_pre
    x = x_ref[...].astype(F32)
    blended = x + gate_ref[...] * (silu(hidden_pre) - x)
    blended_ref[...] = blended
    hat, _ = norm_parts(blended)
    second_ref[...] = (hat * gain_ref[...]).astype(LOW)


def ffn_part(second_ref, cot_ref, ia_ref, ib_ref, oa_ref, ob_ref, out_ref, sg_ref, keep_ref, send_ref):
    second, cot = second_ref[...], cot_ref[...]
    depth, units = ia_ref.shape
    half = depth // 2
    for i, (in_ref, fo_ref, pack_ref) in enumerate(
        ((ia_ref, oa_ref, keep_ref), (ib_ref, ob_ref, send_ref))
    ):
        up_pre = dot(second, in_ref[...])
        activated = silu(up_pre).astype(LOW)
        up_grad = (dot_cols(cot, fo_ref[...]) * silu_slope(up_pre)).astype(LOW)
        out = dot(activated, fo_ref[...])
        back = dot_cols(up_grad, in_ref[...])
        out_ref[...] = out if i == 0 else out_ref[...] + out
        sg_ref[...] = back if i == 0 else sg_ref[...] + back
        kind = pack_ref.dtype
        pack_ref[:depth, :] = dot_rows(second, up_grad).astype(kind)
        for h in range(2):
            pack_ref[depth + h * units : depth + (h + 1) * units, :] = dot_rows(
                activated, cot[:, h * half : (h + 1) * half]
            ).astype(kind)


def blend_back(offs_ref, x_ref, cot_ref, blended_ref, s0_ref, s1_ref, o0_ref, o1_ref, hpre_ref, gate_ref, mixed_ref, gain_ref, wu_ref, whid_ref, y_ref, direct_ref, hidden_ref, mg_ref, gg_ref, keep_ref, send_ref, full_ref):
    blended = blended_ref[...]
    y_ref[...] = (blended + (o0_ref[...] + o1_ref[...])).astype(LOW)
    second_grad = s0_ref[...] + s1_ref[...]
    hat, scale = norm_parts(blended)
    gg_ref[...] = jnp.sum(second_grad * hat, 0, keepdims=True)
    grad = cot_ref[...].astype(F32) + norm_back(second_grad * gain_ref[...], hat, scale)
    gate, hidden_pre, x = gate_ref[...], hpre_ref[...], x_ref[...].astype(F32)
    direct_ref[...] = grad * (1.0 - gate)
    hidden_low = (grad * gate * silu_slope(hidden_pre)).astype(LOW)
    gate_low = (grad * (silu(hidden_pre) - x) * gate * (1.0 - gate)).astype(LOW)
    hidden_ref[...] = hidden_low
    mg_ref[...] = dot_cols(gate_low, wu_ref[...]) + dot_cols(hidden_low, whid_ref[...])
    width = x.shape[1]
    cols, half = width // 4, width // 2
    for i, low in enumerate((gate_low, hidden_low)):
        full_ref[...] = dot_rows(mixed_ref[...], low)
        for r in range(4):
            pack_ref = (keep_ref, send_ref)[r % 2]
            rows = pl.ds(pl.multiple_of(offs_ref[r], 64), cols)
            for h in range(2):
                at = (2 * i + h) * cols
                pack_ref[r // 2, at : at + cols, :] = full_ref[
                    rows, h * half : (h + 1) * half
                ].astype(pack_ref.dtype)


def value_back(hidden_ref, normed_ref, mixed_ref, probs_ref, vpre_ref, rpre_ref, att_ref, united_ref, ga_ref, gb_ref, wa_ref, wb_ref, ng_ref, mg_ref, pg_ref, keep_ref, send_ref):
    hidden, normed, mixed = hidden_ref[...], normed_ref[...], mixed_ref[...]
    tokens, depth = hidden.shape
    units = wa_ref.shape[1]
    cols = ga_ref.shape[0] - units
    half = depth // 2
    for i, (g_ref, w_ref, pack_ref) in enumerate(
        ((ga_ref, wa_ref, keep_ref), (gb_ref, wb_ref, send_ref))
    ):
        kind = pack_ref.dtype
        united_grad = dot_cols(hidden, g_ref[cols:, :])
        reset_pre, value_pre = rpre_ref[i], vpre_ref[i]
        reset_low = (united_grad * att_ref[i] * silu_slope(reset_pre)).astype(LOW)
        attended_low = (united_grad * silu(reset_pre)).astype(LOW)
        values = silu(value_pre).astype(LOW)
        parts = []
        for start in range(0, tokens, STRETCH):
            block = slice(start, start + STRETCH)
            parts.append(dot_rows(probs_ref[block, :].astype(LOW), attended_low[block]))
            back = dot_cols(attended_low[block], values[block])
            pg_ref[block, :] = back if i == 0 else pg_ref[block, :] + back
        value_low = (jnp.concatenate(parts, 0) * silu_slope(value_pre)).astype(LOW)
        into_normed = dot_cols(value_low, w_ref[:depth, :])
        into_mixed = dot_cols(reset_low, w_ref[depth:, :])
        ng_ref[...] = into_normed if i == 0 else ng_ref[...] + into_normed
        mg_ref[...] = into_mixed if i == 0 else mg_ref[...] + into_mixed
        pack_ref[:depth, :] = dot_rows(mixed, reset_low).astype(kind)
        for h in range(2):
            pack_ref[depth + h * units : depth + (h + 1) * units, :] = dot_rows(
                united_ref[i], hidden[:, h * half : (h + 1) * half]
            ).astype(kind)
        pack_ref[2 * depth :, :] = dot_rows(normed, value_low).astype(kind)


def third_pass(rows, zpre_ref, probs_ref, p0_ref, p1_ref, qg_ref, qb_ref, kg_ref, wz_ref, mixed_ref, m0_ref, m1_ref, m2_ref, pre_ref, keep_ref, al_ref, de_ref, pg_ref, dz_ref, small_ref, im_ref, iv_ref, lm_ref, lv_ref, qk_ref):
    z_pre = zpre_ref[...]
    z_low = silu(z_pre).astype(LOW).astype(F32)
    queries = (z_low * qg_ref[...] + qb_ref[...]).astype(LOW)
    keys = (z_low * kg_ref[...]).astype(LOW)
    for start in range(0, z_low.shape[0], STRETCH):
        block = slice(start, start + STRETCH)
        probs = probs_ref[block, :]
        grad = p0_ref[block, :] + p1_ref[block, :]
        grad = probs * (grad - jnp.sum(probs * grad, -1, keepdims=True)) * z_low.shape[1] ** (-0.5)
        high = grad.astype(LOW)
        rest = (grad - high.astype(F32)).astype(LOW)
        qk_ref[0, block, :] = dot(high, keys[block]) + dot(rest, keys[block])
        qk_ref[1, block, :] = dot_rows(high, queries[block]) + dot_rows(rest, queries[block])
    query_grad, key_grad = qk_ref[0], qk_ref[1]
    small_ref[...] = jnp.zeros_like(small_ref)
    small_ref[0:1, :] = jnp.sum(query_grad * z_low, 0, keepdims=True)
    small_ref[1:2, :] = jnp.sum(query_grad, 0, keepdims=True)
    small_ref[2:3, :] = jnp.sum(key_grad * z_low, 0, keepdims=True)
    z_grad = ((query_grad * qg_ref[...] + key_grad * kg_ref[...]) * silu_slope(z_pre)).astype(LOW)
    dz_ref[...] = dot_rows(mixed_ref[...], z_grad)
    mixed_grad = m0_ref[...] + m1_ref[...] + m2_ref[...] + dot_cols(z_grad, wz_ref[...])
    into_slabs(pg_ref, mixed_grad)
    pg_ref[...] = pg_ref[...] * silu_slope(pre_ref[...])
    dims, width = al_ref.shape
    tokens = z_pre.shape[0]
    length = tokens // rows
    steps = length // CHUNKS

    def lane(j, carry):
        lanes = pl.ds(pl.multiple_of(j * LANES, LANES), LANES)
        for row in range(rows):
            token = steps_of(pg_ref, j * tokens + row * length, steps)
            kept = steps_of(keep_ref, row * length, steps)
            whole = product(kept)
            for n in range(dims):
                alpha = jax.nn.sigmoid(bcast(al_ref, n, lanes))
                d = 1.0 - alpha * jax.nn.sigmoid(bcast(de_ref, n, lanes))
                mu = token[steps - 1]
                m = (kept[steps - 1] * d) * mu
                v = kept[steps - 1] * mu
                for k in range(steps - 2, -1, -1):
                    mu = token[k] + m
                    rate = kept[k] * d
                    m = rate * mu
                    v = kept[k] * mu + rate * v
                a = power(d, steps) * whole
                b = steps * power(d, steps - 1) * whole
                for by in (-1, -2, -4):
                    mp, vp = shifted(m, by, 0.0), shifted(v, by, 0.0)
                    ap, bp = shifted(a, by, 1.0), shifted(b, by, 0.0)
                    v = v + a * vp + b * mp
                    m = m + a * mp
                    b = a * bp + b * ap
                    a = a * ap
                at = pl.ds((row * dims + n) * CHUNKS, CHUNKS)
                im_ref[at, lanes] = shifted(m, -1, 0.0)
                iv_ref[at, lanes] = shifted(v, -1, 0.0)
                lm_ref[pl.ds(row * dims + n, 1), lanes] = m[0:1, :]
                lv_ref[pl.ds(row * dims + n, 1), lanes] = v[0:1, :]
        return carry

    lax.fori_loop(0, width // LANES, lane, 0)


def fourth_pass(rows, pg_ref, normed_ref, im_ref, iv_ref, near_ref, far_ref, keep_ref, flag_ref, al_ref, de_ref, be_ref, eta_ref, om_ref, n0_ref, n1_ref, x_ref, g_ref, direct_ref, gg_ref, qk_ref, xg_ref, sums_ref, dec_ref, drv_ref, ng_ref):
    rate_tables(al_ref, de_ref, be_ref, dec_ref, drv_ref)
    dims, width = al_ref.shape
    tokens = keep_ref.shape[0]
    length = tokens // rows
    steps = length // CHUNKS
    span = rows * dims
    sums_ref[...] = jnp.zeros_like(sums_ref)

    def lane(j, carry):
        lanes = pl.ds(pl.multiple_of(j * LANES, LANES), LANES)
        omega = bcast(om_ref, 0, lanes)
        for row in range(rows):
            base = j * tokens + row * length
            grad = steps_of(pg_ref, base, steps)
            token = steps_of(normed_ref, base, steps)
            kept = steps_of(keep_ref, row * length, steps)
            reach = shifted(product(kept), -1, 1.0)
            for by in (-1, -2, -4):
                reach = reach * shifted(reach, by, 1.0)
            place = lax.broadcasted_iota(jnp.int32, (CHUNKS, LANES), 0)
            later = (steps * (CHUNKS - 1 - place)).astype(F32)
            flag = bcast(flag_ref, row, pl.ds(0, LANES))
            total = [omega * t for t in grad]
            for n in range(dims):
                d, b, e = bcast(dec_ref, n, lanes), bcast(drv_ref, n, lanes), bcast(eta_ref, n, lanes)
                chunk = power(d, steps)
                inverse = 1.0 / d
                part = power(chunk, CHUNKS) * flag
                slope = (float(length) * part) * inverse
                at = row * dims + n
                m2 = bcast(far_ref, at, lanes)
                m_in = bcast(near_ref, at, lanes) + part * m2
                v_in = bcast(near_ref, span + at, lanes) + part * bcast(far_ref, span + at, lanes) + slope * m2
                through = reach * chunk_powers(chunk, -1)
                at = pl.ds(at * CHUNKS, CHUNKS)
                m = im_ref[at, lanes] + through * m_in
                v = iv_ref[at, lanes] + through * v_in + (later * through * inverse) * m_in
                coef = e * b
                sum_m = jnp.zeros((CHUNKS, LANES), F32)
                sum_v = jnp.zeros((CHUNKS, LANES), F32)
                for k in range(steps - 1, -1, -1):
                    mu = grad[k] + m
                    sum_m = sum_m + token[k] * mu
                    sum_v = sum_v + token[k] * v
                    total[k] = total[k] + coef * mu
                    rate = kept[k] * d
                    m = rate * mu
                    v = kept[k] * mu + rate * v
                sums_ref[pl.ds(n, 1), lanes] += jnp.sum(sum_m, 0, keepdims=True)
                sums_ref[pl.ds(dims + n, 1), lanes] += jnp.sum(sum_v, 0, keepdims=True)
            for k in range(steps):
                ng_ref[pl.ds(base + k, CHUNKS, stride=steps), :] = total[k]
        return carry

    lax.fori_loop(0, width // LANES, lane, 0)
    normed_grad = from_slabs(ng_ref[...], tokens) + n0_ref[...] + n1_ref[...]
    hat, scale = norm_parts(x_ref[...].astype(F32))
    at = 2 * dims
    for j in range(width // LANES):
        slab = slice(j * tokens, (j + 1) * tokens)
        sums_ref[at : at + 1, j * LANES : (j + 1) * LANES] = jnp.sum(
            pg_ref[slab, :] * normed_ref[slab, :], 0, keepdims=True
        )
    sums_ref[at + 1 : at + 2, :] = jnp.sum(normed_grad * hat, 0, keepdims=True)
    sums_ref[at + 2 : at + 3, :] = gg_ref[...]
    zd = qk_ref.shape[1]
    for i in range(3):
        sums_ref[at + 3 : at + 4, i * zd : (i + 1) * zd] = qk_ref[i : i + 1, :]
    xg_ref[...] = (direct_ref[...] + norm_back(normed_grad * g_ref[...], hat, scale)).astype(LOW)


def swap(x, axis, bit):
    size = lax.axis_size(axis)
    return lax.ppermute(x, axis, [(i, i ^ bit) for i in range(size)])


def shift(x, by):
    size = lax.axis_size("tensor")
    return lax.ppermute(
        x, "tensor", [(i, i + by) for i in range(size) if 0 <= i + by < size]
    )


def rounded(v):
    return lax.reduce_precision(v, 8, 7)


def sum_over_rows(s):
    size, index = lax.axis_size("dp"), lax.axis_index("dp")
    bits = size.bit_length() - 1
    halvings = min(2, bits - 1)
    for b in range(halvings):
        bit, half = (index >> b) & 1, s.shape[0] // 2
        away = lax.dynamic_slice_in_dim(s, (1 - bit) * half, half).astype(LOW)
        mine = lax.dynamic_slice_in_dim(s, bit * half, half)
        s = mine + swap(away, "dp", 1 << b).astype(F32)
    s = rounded(s)
    for b in range(halvings, bits):
        s = rounded(s + swap(s.astype(LOW), "dp", 1 << b).astype(F32))
    low = s.astype(LOW)
    for b in reversed(range(halvings)):
        bit = (index >> b) & 1
        got = swap(low, "dp", 1 << b)
        low = jnp.where(
            bit == 0, jnp.concatenate([low, got], 0), jnp.concatenate([got, low], 0)
        )
    return low


def reduced(keep0, send0, keep1, send1):
    got1 = swap(send1, "tensor", 1)
    across = (keep1 + got1.astype(F32)).astype(LOW)
    got0 = swap(send0, "tensor", 1)
    over = swap(across, "tensor", 2)
    return sum_over_rows(keep0 + got0.astype(F32) + over.astype(F32))


def side_by_side(pack):
    half = pack.shape[0] // 2
    return jnp.concatenate([pack[:half], pack[half:]], 1)


def butterfly(v, low):
    for axis in ("tensor", "dp"):
        size = lax.axis_size(axis)
        for b in range(size.bit_length() - 1):
            if low:
                v = rounded(v)
                v = v + swap(v.astype(LOW), axis, 1 << b).astype(F32)
            else:
                v = v + swap(v, axis, 1 << b)
    return v


def shards(
    layer_input,
    doc_lengths,
    norm1_gain,
    alpha_raw,
    delta_raw,
    ema_beta,
    ema_eta,
    ema_omega,
    w_z,
    q_gain,
    q_bias,
    k_gain,
    w_value,
    w_reset,
    w_update,
    w_hidden,
    w_out,
    norm2_gain,
    w_ffn_in,
    w_ffn_out,
    cotangent,
):
    member = lax.axis_index("tensor")
    rows, length, width = layer_input.shape
    tokens = rows * length
    dims = alpha_raw.shape[0]
    zd = w_z.shape[1]
    units = w_value.shape[1]
    cols = w_hidden.shape[0]
    x = layer_input.reshape(tokens, width)
    cot = cotangent.reshape(tokens, width)
    g1, g2, om = norm1_gain[None], norm2_gain[None], ema_omega[None]
    qg, qb, kg = q_gain[None], q_bias[None], k_gain[None]

    pack_a = jnp.concatenate([w_value, w_reset], 0)
    pack_g = jnp.concatenate([w_hidden, w_out], 0)
    shares = (pack_a, pack_g, w_ffn_in, w_ffn_out)
    over = [swap(w, "tensor", 2) for w in shares]
    beside = [swap(w, "tensor", 1) for w in shares]
    both = [swap(w, "tensor", 1) for w in over]
    wa, wg, wi, wo = (
        (own, b, o, d) for own, b, o, d in zip(shares, beside, over, both, strict=True)
    )

    docs = doc_lengths.shape[1]
    order = jnp.arange(docs)
    ends = jnp.sum(
        jnp.where(order[:, None] <= order[None, :], doc_lengths[:, :, None], 0), 1
    ).astype(jnp.int32)
    starts = ends - doc_lengths
    places = member * length + jnp.arange(length, dtype=jnp.int32)
    docid = jnp.sum((places[None, :, None] >= ends[:, None, :]).astype(jnp.int32), 2)
    keep = 1.0 - jnp.any(places[None, :, None] == starts[:, None, :], 2).astype(F32)
    keep = jnp.broadcast_to(keep.reshape(tokens, 1), (tokens, LANES))
    blocks = docid.reshape(tokens // STRETCH, STRETCH)
    spot = jnp.arange(STRETCH)
    mask = (spot[None, :] <= spot[:, None])[None] & (blocks[:, :, None] == blocks[:, None, :])
    mask = mask.astype(F32).reshape(tokens, STRETCH)

    def unbroken(part):
        low, high = part * length, (part + 1) * length
        inside = jnp.any((starts >= low) & (starts < high), 1)
        return jnp.broadcast_to(1.0 - inside.astype(F32)[:, None], (rows, LANES))

    offs = (member ^ jnp.arange(4, dtype=jnp.int32)) * cols

    vm = lambda shape: pltpu.VMEM(shape, F32)
    tab = (dims, width)
    wide = (tokens, width)
    mat = 2.0 * tokens * width
    ema = 8.0 * tokens * width * dims
    chunked = (rows * dims * CHUNKS, width)
    finals = (rows * dims, width)
    slabs = (tokens * width // LANES, LANES)

    normed, normed_low, init, last = call(
        functools.partial(first_pass, rows),
        [(slabs, F32), (wide, LOW), (chunked, F32), (finals, F32)],
        (x, g1, alpha_raw, delta_raw, ema_beta, keep),
        ema,
        [vm(tab), vm(tab)],
    )
    f1, f2 = shift(last, 1), shift(last, 2)
    pre, mixed_low, z_pre, gate, probs = call(
        functools.partial(second_pass, rows),
        [(slabs, F32), (wide, LOW), ((tokens, zd), F32), (wide, F32), ((tokens, STRETCH), F32)],
        (normed, init, f1, f2, keep, unbroken(member - 1), alpha_raw, delta_raw, ema_beta,
         ema_eta, om, w_z, w_update, qg, qb, kg, mask),
        ema + mat * width,
        [vm(tab), vm(tab)],
    )
    split = (2, tokens, units)
    kept_parts = []
    for p in range(2):
        kept_parts.append(
            call(
                value_part,
                [(split, F32), (split, F32), (split, F32), (split, LOW)],
                (normed_low, mixed_low, probs, wa[2 * p], wa[2 * p + 1]),
                4 * mat * units,
            )
        )
    hidden_pre, blended, second, whid = call(
        blend_part,
        [(wide, F32), (wide, F32), (wide, LOW), ((width, width), LOW)],
        (offs, x, mixed_low, gate, kept_parts[0][3], kept_parts[1][3], *wg, g2),
        mat * (width + 4 * units),
        smem=(0,),
    )
    ffn_rows = width + 2 * units
    ffn = [None, None]
    for p in (1, 0):
        ffn[p] = call(
            ffn_part,
            [(wide, F32), (wide, F32), ((ffn_rows, units), F32), ((ffn_rows, units), LOW)],
            (second, cot, wi[2 * p], wi[2 * p + 1], wo[2 * p], wo[2 * p + 1]),
            12 * mat * units,
        )
    ffn_sum = reduced(ffn[0][2], ffn[0][3], ffn[1][2], ffn[1][3])
    own = (2, 4 * cols, width // 2)
    output, direct, hidden_low, mixed0, gain2, keep_u, send_u = call(
        blend_back,
        [(wide, LOW), (wide, F32), (wide, LOW), (wide, F32), ((1, width), F32), (own, F32), (own, LOW)],
        (offs, x, cot, blended, ffn[0][1], ffn[1][1], ffn[0][0], ffn[1][0], hidden_pre, gate,
         mixed_low, g2, w_update, whid),
        4 * mat * width,
        [vm((width, width))],
        smem=(0,),
    )
    pair_sum = reduced(keep_u[0], send_u[0], keep_u[1], send_u[1])
    rest = [None, None]
    pack_rows = 2 * width + 2 * units
    for p in (1, 0):
        rest[p] = call(
            value_back,
            [(wide, F32), (wide, F32), ((tokens, STRETCH), F32), ((pack_rows, units), F32), ((pack_rows, units), LOW)],
            (hidden_low, normed_low, mixed_low, probs, *kept_parts[p], wg[2 * p], wg[2 * p + 1],
             wa[2 * p], wa[2 * p + 1]),
            14 * mat * units,
        )
    cut = width + 2 * units
    sums_c = reduced(*(rest[p][i][:cut] for p in range(2) for i in (3, 4)))
    sums_d = reduced(*(rest[p][i][cut:] for p in range(2) for i in (3, 4)))
    pre_grad, dz, small, im, iv, lm, lv = call(
        functools.partial(third_pass, rows),
        [(slabs, F32), ((width, zd), F32), ((8, zd), F32), (chunked, F32), (chunked, F32), (finals, F32), (finals, F32)],
        (z_pre, probs, rest[0][2], rest[1][2], qg, qb, kg, w_z, mixed_low, mixed0, rest[0][1],
         rest[1][1], pre, keep, alpha_raw, delta_raw),
        2 * ema,
        [vm((2, tokens, zd))],
    )
    dz_sum = butterfly(dz, True)
    back = jnp.concatenate([lm, lv], 0)
    near, far = shift(back, -1), shift(back, -2)
    input_grad, sums = call(
        functools.partial(fourth_pass, rows),
        [(wide, LOW), ((2 * dims + 8, width), F32)],
        (pre_grad, normed, im, iv, near, far, keep, unbroken(member + 1), alpha_raw, delta_raw,
         ema_beta, ema_eta, om, rest[0][0], rest[1][0], x, g1, direct, gain2, small),
        2 * ema,
        [vm(tab), vm(tab), vm(slabs)],
    )
    sums = butterfly(sums, False)

    alpha, sigma = jax.nn.sigmoid(alpha_raw), jax.nn.sigmoid(delta_raw)
    with_mu, with_nu = sums[:dims], sums[dims : 2 * dims]
    drive_grad = ema_eta * with_mu
    decay_grad = ema_eta * (alpha * ema_beta) * with_nu
    at = 2 * dims
    quarter = side_by_side(pair_sum[: 2 * cols])
    pair = jnp.stack([quarter, swap(quarter, "tensor", 2)])
    quarters = jnp.stack([pair, swap(pair, "tensor", 1)], 1).reshape(4, cols, width)
    update_grad = jnp.concatenate(
        [lax.dynamic_index_in_dim(quarters, g ^ member, 0, False) for g in range(4)], 0
    )
    return (
        output.reshape(layer_input.shape),
        input_grad.reshape(layer_input.shape),
        sums[at + 1],
        (ema_beta * drive_grad - sigma * decay_grad) * alpha * (1.0 - alpha),
        -alpha * decay_grad * sigma * (1.0 - sigma),
        alpha * drive_grad,
        (alpha * ema_beta) * with_mu,
        sums[at],
        dz_sum,
        sums[at + 3, :zd],
        sums[at + 3, zd : 2 * zd],
        sums[at + 3, 2 * zd : 3 * zd],
        sums_d.astype(F32),
        sums_c[:width].astype(F32),
        update_grad.astype(F32),
        side_by_side(pair_sum[2 * cols :]).astype(F32),
        side_by_side(sums_c[width:]).astype(F32),
        sums[at + 2],
        ffn_sum[:width].astype(F32),
        side_by_side(ffn_sum[width:]).astype(F32),
    )


def solution(mesh):
    whole, by_row = P(), P("dp", "tensor", None)
    by_col, by_unit = P(None, "tensor"), P("tensor", None)
    return jax.shard_map(
        shards,
        mesh=mesh,
        in_specs=(by_row, P("dp", None), *(whole,) * 10, by_col, by_col, whole, by_unit, by_unit, whole, by_col, by_unit, by_row),
        out_specs=(by_row, by_row, *(whole,) * 10, by_col, by_col, whole, by_unit, by_unit, whole, by_col, by_unit),
        check_vma=False,
    )
```

```python
import functools

import jax
import jax.numpy as jnp
from jax import lax
from jax.experimental import pallas as pl
from jax.experimental.pallas import tpu as pltpu
from jax.sharding import PartitionSpec as P

STRETCH = 128
LANES = 128
CHUNKS = 8
F32 = jnp.float32
LOW = jnp.bfloat16
KINDS = {"F": "w", "P": "x", "R": "x", "O": "z", "N": "x"}
ORDER = (
    "+F0", "+F1", "Kbb", "-F0", "-F1", "+P0", "Kv1", "-P0", "+V1", "+F",
    "+P", "Kv0", "-V1", "+V0", "Kt3", "-V0", "+dz", "+E", "-P", "+R",
    "-dz", "+O", "-F", "+N", "-R", "+P", "-O", "+F", "-E", "Kt4",
    "-P", "+R", "+sm", "-N", "+P", "-sm", "+N", "-F", "+F", "-P",
    "+P", "-R", "+dz", "+R", "-F", "+sm", "-N", "+F", "-R", "+O",
    "-P", "-dz", "+N", "+dz", "-sm", "+P", "-dz", "-O", "-N", "+R",
    "+sm", "+dz", "-P", "+O", "-F", "+P", "-sm", "+N", "-O", "+sm",
    "-dz", "+O", "-R", "+F", "-P", "+R", "-sm", "+dz", "-N", "+N",
    "-F", "-R", "+R", "+F", "-O", "+O", "-N", "+N", "-dz", "-R",
    "-O", "+sm", "+O", "-F", "-N", "-sm", "-O",
)


def silu(v):
    return v * jax.nn.sigmoid(v)


def silu_slope(v):
    s = jax.nn.sigmoid(v)
    return s * (1.0 + v * (1.0 - s))


def dot(a, b):
    return jnp.dot(a, b, preferred_element_type=F32)


def dot_rows(a, b):
    return lax.dot_general(a, b, (((0,), (0,)), ((), ())), preferred_element_type=F32)


def dot_cols(a, b):
    return lax.dot_general(a, b, (((1,), (1,)), ((), ())), preferred_element_type=F32)


def norm_parts(v):
    center = v - jnp.mean(v, -1, keepdims=True)
    scale = lax.rsqrt(jnp.mean(center * center, -1, keepdims=True) + 1e-05)
    return center * scale, scale


def norm_back(grad, hat, scale):
    return scale * (
        grad - jnp.mean(grad, -1, keepdims=True) - hat * jnp.mean(grad * hat, -1, keepdims=True)
    )


def call(kernel, outs, args, flops, scratch=(), smem=(), limit=48 << 20):
    specs = [
        pl.BlockSpec(memory_space=pltpu.SMEM if i in smem else pltpu.VMEM)
        for i in range(len(args))
    ]
    outs = [jax.ShapeDtypeStruct(s, d) for s, d in outs]
    size = sum(a.size * a.dtype.itemsize for a in args) + sum(
        o.size * o.dtype.itemsize for o in outs
    )
    return pl.pallas_call(
        kernel,
        out_shape=outs,
        in_specs=specs,
        out_specs=[pl.BlockSpec(memory_space=pltpu.VMEM) for _ in outs],
        scratch_shapes=list(scratch),
        compiler_params=pltpu.CompilerParams(vmem_limit_bytes=limit),
        cost_estimate=pl.CostEstimate(flops=int(flops), bytes_accessed=int(size), transcendentals=0),
    )(*args)


def bcast(ref, row, lanes):
    return jnp.broadcast_to(ref[pl.ds(row, 1), lanes], (CHUNKS, LANES))


def shifted(v, by, fill):
    place = lax.broadcasted_iota(jnp.int32, v.shape, 0)
    if by > 0:
        return jnp.where(place >= by, pltpu.roll(v, by, 0), fill)
    return jnp.where(place < CHUNKS + by, pltpu.roll(v, CHUNKS + by, 0), fill)


def power(v, n):
    out = None
    while n:
        if n & 1:
            out = v if out is None else out * v
        n >>= 1
        if n:
            v = v * v
    return out


def chunk_powers(base, order):
    place = lax.broadcasted_iota(jnp.int32, base.shape, 0)
    place = place if order > 0 else (CHUNKS - 1) - place
    out = jnp.where(place & 1 == 1, base, 1.0)
    base = base * base
    out = out * jnp.where(place & 2 == 2, base, 1.0)
    base = base * base
    return out * jnp.where(place & 4 == 4, base, 1.0)


def rate_tables(al_ref, de_ref, be_ref, dec_ref, drv_ref):
    alpha = jax.nn.sigmoid(al_ref[...])
    dec_ref[...] = 1.0 - alpha * jax.nn.sigmoid(de_ref[...])
    drv_ref[...] = alpha * be_ref[...]


def steps_of(ref, base, steps):
    return [ref[pl.ds(base + k, CHUNKS, stride=steps), :] for k in range(steps)]


def into_slabs(ref, v):
    tokens = v.shape[0]
    for j in range(v.shape[1] // LANES):
        ref[j * tokens : (j + 1) * tokens, :] = v[:, j * LANES : (j + 1) * LANES]


def from_slabs(v, tokens):
    return jnp.concatenate(
        [v[at : at + tokens] for at in range(0, v.shape[0], tokens)], 1
    )


def product(values):
    out = values[0]
    for v in values[1:]:
        out = out * v
    return out


def first_pass(rows, x_ref, g_ref, al_ref, de_ref, be_ref, keep_ref, normed_ref, low_ref, init_ref, last_ref, dec_ref, drv_ref):
    hat, _ = norm_parts(x_ref[...].astype(F32))
    normed = hat * g_ref[...]
    into_slabs(normed_ref, normed)
    low_ref[...] = normed.astype(LOW)
    rate_tables(al_ref, de_ref, be_ref, dec_ref, drv_ref)
    dims, width = al_ref.shape
    tokens = x_ref.shape[0]
    length = tokens // rows
    steps = length // CHUNKS

    def lane(j, carry):
        lanes = pl.ds(pl.multiple_of(j * LANES, LANES), LANES)
        for row in range(rows):
            token = steps_of(normed_ref, j * tokens + row * length, steps)
            kept = steps_of(keep_ref, row * length, steps)
            whole = product(kept)
            for n in range(dims):
                d, b = bcast(dec_ref, n, lanes), bcast(drv_ref, n, lanes)
                s = b * token[0]
                for k in range(1, steps):
                    s = (kept[k] * d) * s + b * token[k]
                a = power(d, steps) * whole
                for by in (1, 2, 4):
                    s = s + a * shifted(s, by, 0.0)
                    a = a * shifted(a, by, 1.0)
                init_ref[pl.ds((row * dims + n) * CHUNKS, CHUNKS), lanes] = shifted(s, 1, 0.0)
                last_ref[pl.ds(row * dims + n, 1), lanes] = s[CHUNKS - 1 :, :]
        return carry

    lax.fori_loop(0, width // LANES, lane, 0)


def second_pass(rows, normed_ref, init_ref, f1_ref, f2_ref, keep_ref, flag_ref, al_ref, de_ref, be_ref, eta_ref, om_ref, wz_ref, wu_ref, qg_ref, qb_ref, kg_ref, mask_ref, pre_ref, mixed_ref, zpre_ref, gate_ref, probs_ref, dec_ref, drv_ref):
    rate_tables(al_ref, de_ref, be_ref, dec_ref, drv_ref)
    dims, width = al_ref.shape
    tokens = keep_ref.shape[0]
    length = tokens // rows
    steps = length // CHUNKS

    def lane(j, carry):
        lanes = pl.ds(pl.multiple_of(j * LANES, LANES), LANES)
        omega = bcast(om_ref, 0, lanes)
        for row in range(rows):
            base = j * tokens + row * length
            token = steps_of(normed_ref, base, steps)
            kept = steps_of(keep_ref, row * length, steps)
            reach = shifted(product(kept), 1, 1.0)
            for by in (1, 2, 4):
                reach = reach * shifted(reach, by, 1.0)
            flag = bcast(flag_ref, row, pl.ds(0, LANES))
            total = [omega * t for t in token]
            for n in range(dims):
                d, b, e = bcast(dec_ref, n, lanes), bcast(drv_ref, n, lanes), bcast(eta_ref, n, lanes)
                chunk = power(d, steps)
                entering = bcast(f1_ref, row * dims + n, lanes) + (
                    power(chunk, CHUNKS) * flag
                ) * bcast(f2_ref, row * dims + n, lanes)
                s = (
                    init_ref[pl.ds((row * dims + n) * CHUNKS, CHUNKS), lanes]
                    + reach * chunk_powers(chunk, 1) * entering
                )
                for k in range(steps):
                    s = (kept[k] * d) * s + b * token[k]
                    total[k] = total[k] + e * s
            for k in range(steps):
                pre_ref[pl.ds(base + k, CHUNKS, stride=steps), :] = total[k]
        return carry

    lax.fori_loop(0, width // LANES, lane, 0)
    mixed_low = from_slabs(silu(pre_ref[...]).astype(LOW), tokens)
    mixed_ref[...] = mixed_low
    z_pre = dot(mixed_low, wz_ref[...])
    zpre_ref[...] = z_pre
    gate_ref[...] = jax.nn.sigmoid(dot(mixed_low, wu_ref[...]))
    z_low = silu(z_pre).astype(LOW).astype(F32)
    queries = (z_low * qg_ref[...] + qb_ref[...]).astype(LOW)
    keys = (z_low * kg_ref[...]).astype(LOW)
    for start in range(0, z_low.shape[0], STRETCH):
        block = slice(start, start + STRETCH)
        scores = dot_cols(queries[block], keys[block]) * z_low.shape[1] ** (-0.5)
        scores = jnp.where(mask_ref[block, :] > 0.5, scores, -1e30)
        shift = jnp.exp(scores - jnp.max(scores, -1, keepdims=True))
        probs_ref[block, :] = shift / jnp.sum(shift, -1, keepdims=True)


def value_part(normed_ref, mixed_ref, probs_ref, va_ref, ra_ref, vb_ref, rb_ref, vpre_ref, rpre_ref, att_ref, united_ref):
    tokens = normed_ref.shape[0]
    for i, (v_ref, r_ref) in enumerate(((va_ref, ra_ref), (vb_ref, rb_ref))):
        value_pre = dot(normed_ref[...], v_ref[...])
        reset_pre = dot(mixed_ref[...], r_ref[...])
        vpre_ref[i] = value_pre
        rpre_ref[i] = reset_pre
        values = silu(value_pre).astype(LOW)
        for start in range(0, tokens, STRETCH):
            block = slice(start, start + STRETCH)
            att_ref[i, block, :] = dot(probs_ref[block, :].astype(LOW), values[block])
        united_ref[i] = (silu(reset_pre) * att_ref[i]).astype(LOW)


def blend_part(offs_ref, x_ref, mixed_ref, gate_ref, u0_ref, u1_ref, ga_ref, gb_ref, gain_ref, hpre_ref, blended_ref, second_ref, whid_ref):
    cols = whid_ref.shape[0] // 4
    for r in range(4):
        whid_ref[pl.ds(pl.multiple_of(offs_ref[r], 64), cols), :] = (ga_ref, gb_ref)[r % 2][r // 2, :cols, :]
    hidden_pre = dot(mixed_ref[...], whid_ref[...])
    for r in range(4):
        united = (u0_ref, u1_ref)[r // 2][r % 2]
        hidden_pre = hidden_pre + dot(united, (ga_ref, gb_ref)[r % 2][r // 2, cols:, :])
    hpre_ref[...] = hidden_pre
    x = x_ref[...].astype(F32)
    blended = x + gate_ref[...] * (silu(hidden_pre) - x)
    blended_ref[...] = blended
    hat, _ = norm_parts(blended)
    second_ref[...] = (hat * gain_ref[...]).astype(LOW)


def ffn_part(second_ref, cot_ref, ia_ref, ib_ref, oa_ref, ob_ref, out_ref, sg_ref, keep_ref, send_ref):
    second, cot = second_ref[...], cot_ref[...]
    depth, units = ia_ref.shape
    half = depth // 2
    for i, (in_ref, fo_ref, pack_ref) in enumerate(
        ((ia_ref, oa_ref, keep_ref), (ib_ref, ob_ref, send_ref))
    ):
        up_pre = dot(second, in_ref[...])
        activated = silu(up_pre).astype(LOW)
        up_grad = (dot_cols(cot, fo_ref[...]) * silu_slope(up_pre)).astype(LOW)
        out = dot(activated, fo_ref[...])
        back = dot_cols(up_grad, in_ref[...])
        out_ref[...] = out if i == 0 else out_ref[...] + out
        sg_ref[...] = back if i == 0 else sg_ref[...] + back
        kind = pack_ref.dtype
        pack_ref[:depth, :] = dot_rows(second, up_grad).astype(kind)
        for h in range(2):
            pack_ref[depth + h * units : depth + (h + 1) * units, :] = dot_rows(
                activated, cot[:, h * half : (h + 1) * half]
            ).astype(kind)


def blend_back(offs_ref, x_ref, cot_ref, blended_ref, s0_ref, s1_ref, o0_ref, o1_ref, hpre_ref, gate_ref, mixed_ref, gain_ref, wu_ref, whid_ref, y_ref, direct_ref, hidden_ref, mg_ref, gg_ref, keep_ref, send_ref, full_ref):
    blended = blended_ref[...]
    y_ref[...] = (blended + (o0_ref[...] + o1_ref[...])).astype(LOW)
    second_grad = s0_ref[...] + s1_ref[...]
    hat, scale = norm_parts(blended)
    gg_ref[...] = jnp.sum(second_grad * hat, 0, keepdims=True)
    grad = cot_ref[...].astype(F32) + norm_back(second_grad * gain_ref[...], hat, scale)
    gate, hidden_pre, x = gate_ref[...], hpre_ref[...], x_ref[...].astype(F32)
    direct_ref[...] = grad * (1.0 - gate)
    hidden_low = (grad * gate * silu_slope(hidden_pre)).astype(LOW)
    gate_low = (grad * (silu(hidden_pre) - x) * gate * (1.0 - gate)).astype(LOW)
    hidden_ref[...] = hidden_low
    mg_ref[...] = dot_cols(gate_low, wu_ref[...]) + dot_cols(hidden_low, whid_ref[...])
    width = x.shape[1]
    cols, half = width // 4, width // 2
    for i, low in enumerate((gate_low, hidden_low)):
        full_ref[...] = dot_rows(mixed_ref[...], low)
        for r in range(4):
            pack_ref = (keep_ref, send_ref)[r % 2]
            rows = pl.ds(pl.multiple_of(offs_ref[r], 64), cols)
            for h in range(2):
                at = (2 * i + h) * cols
                pack_ref[r // 2, at : at + cols, :] = full_ref[
                    rows, h * half : (h + 1) * half
                ].astype(pack_ref.dtype)


def value_back(part, hidden_ref, normed_ref, mixed_ref, probs_ref, vpre_ref, rpre_ref, att_ref, united_ref, ga_ref, gb_ref, va_ref, ra_ref, vb_ref, rb_ref, ng_ref, mg_ref, pg_ref, keep_ref, send_ref):
    hidden, normed, mixed = hidden_ref[...], normed_ref[...], mixed_ref[...]
    tokens, depth = hidden.shape
    units = va_ref.shape[1]
    cols = ga_ref.shape[1] - units
    half = depth // 2
    for i, (g_ref, v_ref, r_ref, pack_ref) in enumerate(
        ((ga_ref, va_ref, ra_ref, keep_ref), (gb_ref, vb_ref, rb_ref, send_ref))
    ):
        kind = pack_ref.dtype
        united_grad = dot_cols(hidden, g_ref[part, cols:, :])
        reset_pre, value_pre = rpre_ref[i], vpre_ref[i]
        reset_low = (united_grad * att_ref[i] * silu_slope(reset_pre)).astype(LOW)
        attended_low = (united_grad * silu(reset_pre)).astype(LOW)
        values = silu(value_pre).astype(LOW)
        parts = []
        for start in range(0, tokens, STRETCH):
            block = slice(start, start + STRETCH)
            parts.append(dot_rows(probs_ref[block, :].astype(LOW), attended_low[block]))
            back = dot_cols(attended_low[block], values[block])
            pg_ref[block, :] = back if i == 0 else pg_ref[block, :] + back
        value_low = (jnp.concatenate(parts, 0) * silu_slope(value_pre)).astype(LOW)
        into_normed = dot_cols(value_low, v_ref[...])
        into_mixed = dot_cols(reset_low, r_ref[...])
        ng_ref[...] = into_normed if i == 0 else ng_ref[...] + into_normed
        mg_ref[...] = into_mixed if i == 0 else mg_ref[...] + into_mixed
        pack_ref[:depth, :] = dot_rows(mixed, reset_low).astype(kind)
        for h in range(2):
            pack_ref[depth + h * units : depth + (h + 1) * units, :] = dot_rows(
                united_ref[i], hidden[:, h * half : (h + 1) * half]
            ).astype(kind)
        pack_ref[2 * depth :, :] = dot_rows(normed, value_low).astype(kind)


def third_pass(rows, zpre_ref, probs_ref, p0_ref, p1_ref, qg_ref, qb_ref, kg_ref, wz_ref, mixed_ref, m0_ref, m1_ref, m2_ref, pre_ref, keep_ref, al_ref, de_ref, pg_ref, dz_ref, small_ref, im_ref, iv_ref, lm_ref, lv_ref, qk_ref):
    z_pre = zpre_ref[...]
    z_low = silu(z_pre).astype(LOW).astype(F32)
    queries = (z_low * qg_ref[...] + qb_ref[...]).astype(LOW)
    keys = (z_low * kg_ref[...]).astype(LOW)
    for start in range(0, z_low.shape[0], STRETCH):
        block = slice(start, start + STRETCH)
        probs = probs_ref[block, :]
        grad = p0_ref[block, :] + p1_ref[block, :]
        grad = probs * (grad - jnp.sum(probs * grad, -1, keepdims=True)) * z_low.shape[1] ** (-0.5)
        high = grad.astype(LOW)
        rest = (grad - high.astype(F32)).astype(LOW)
        qk_ref[0, block, :] = dot(high, keys[block]) + dot(rest, keys[block])
        qk_ref[1, block, :] = dot_rows(high, queries[block]) + dot_rows(rest, queries[block])
    query_grad, key_grad = qk_ref[0], qk_ref[1]
    small_ref[...] = jnp.zeros_like(small_ref)
    small_ref[0:1, :] = jnp.sum(query_grad * z_low, 0, keepdims=True)
    small_ref[1:2, :] = jnp.sum(query_grad, 0, keepdims=True)
    small_ref[2:3, :] = jnp.sum(key_grad * z_low, 0, keepdims=True)
    z_grad = ((query_grad * qg_ref[...] + key_grad * kg_ref[...]) * silu_slope(z_pre)).astype(LOW)
    dz_ref[...] = dot_rows(mixed_ref[...], z_grad)
    mixed_grad = m0_ref[...] + m1_ref[...] + m2_ref[...] + dot_cols(z_grad, wz_ref[...])
    into_slabs(pg_ref, mixed_grad)
    pg_ref[...] = pg_ref[...] * silu_slope(pre_ref[...])
    dims, width = al_ref.shape
    tokens = z_pre.shape[0]
    length = tokens // rows
    steps = length // CHUNKS

    def lane(j, carry):
        lanes = pl.ds(pl.multiple_of(j * LANES, LANES), LANES)
        for row in range(rows):
            token = steps_of(pg_ref, j * tokens + row * length, steps)
            kept = steps_of(keep_ref, row * length, steps)
            whole = product(kept)
            for n in range(dims):
                alpha = jax.nn.sigmoid(bcast(al_ref, n, lanes))
                d = 1.0 - alpha * jax.nn.sigmoid(bcast(de_ref, n, lanes))
                mu = token[steps - 1]
                m = (kept[steps - 1] * d) * mu
                v = kept[steps - 1] * mu
                for k in range(steps - 2, -1, -1):
                    mu = token[k] + m
                    rate = kept[k] * d
                    m = rate * mu
                    v = kept[k] * mu + rate * v
                a = power(d, steps) * whole
                b = steps * power(d, steps - 1) * whole
                for by in (-1, -2, -4):
                    mp, vp = shifted(m, by, 0.0), shifted(v, by, 0.0)
                    ap, bp = shifted(a, by, 1.0), shifted(b, by, 0.0)
                    v = v + a * vp + b * mp
                    m = m + a * mp
                    b = a * bp + b * ap
                    a = a * ap
                at = pl.ds((row * dims + n) * CHUNKS, CHUNKS)
                im_ref[at, lanes] = shifted(m, -1, 0.0)
                iv_ref[at, lanes] = shifted(v, -1, 0.0)
                lm_ref[pl.ds(row * dims + n, 1), lanes] = m[0:1, :]
                lv_ref[pl.ds(row * dims + n, 1), lanes] = v[0:1, :]
        return carry

    lax.fori_loop(0, width // LANES, lane, 0)


def fourth_pass(rows, pg_ref, normed_ref, im_ref, iv_ref, near_ref, far_ref, keep_ref, flag_ref, al_ref, de_ref, be_ref, eta_ref, om_ref, n0_ref, n1_ref, x_ref, g_ref, direct_ref, gg_ref, qk_ref, xg_ref, sums_ref, dec_ref, drv_ref, ng_ref):
    rate_tables(al_ref, de_ref, be_ref, dec_ref, drv_ref)
    dims, width = al_ref.shape
    tokens = keep_ref.shape[0]
    length = tokens // rows
    steps = length // CHUNKS
    span = rows * dims
    sums_ref[...] = jnp.zeros_like(sums_ref)

    def lane(j, carry):
        lanes = pl.ds(pl.multiple_of(j * LANES, LANES), LANES)
        omega = bcast(om_ref, 0, lanes)
        for row in range(rows):
            base = j * tokens + row * length
            grad = steps_of(pg_ref, base, steps)
            token = steps_of(normed_ref, base, steps)
            kept = steps_of(keep_ref, row * length, steps)
            reach = shifted(product(kept), -1, 1.0)
            for by in (-1, -2, -4):
                reach = reach * shifted(reach, by, 1.0)
            place = lax.broadcasted_iota(jnp.int32, (CHUNKS, LANES), 0)
            later = (steps * (CHUNKS - 1 - place)).astype(F32)
            flag = bcast(flag_ref, row, pl.ds(0, LANES))
            total = [omega * t for t in grad]
            for n in range(dims):
                d, b, e = bcast(dec_ref, n, lanes), bcast(drv_ref, n, lanes), bcast(eta_ref, n, lanes)
                chunk = power(d, steps)
                inverse = 1.0 / d
                part = power(chunk, CHUNKS) * flag
                slope = (float(length) * part) * inverse
                at = row * dims + n
                m2 = bcast(far_ref, at, lanes)
                m_in = bcast(near_ref, at, lanes) + part * m2
                v_in = bcast(near_ref, span + at, lanes) + part * bcast(far_ref, span + at, lanes) + slope * m2
                through = reach * chunk_powers(chunk, -1)
                at = pl.ds(at * CHUNKS, CHUNKS)
                m = im_ref[at, lanes] + through * m_in
                v = iv_ref[at, lanes] + through * v_in + (later * through * inverse) * m_in
                coef = e * b
                sum_m = jnp.zeros((CHUNKS, LANES), F32)
                sum_v = jnp.zeros((CHUNKS, LANES), F32)
                for k in range(steps - 1, -1, -1):
                    mu = grad[k] + m
                    sum_m = sum_m + token[k] * mu
                    sum_v = sum_v + token[k] * v
                    total[k] = total[k] + coef * mu
                    rate = kept[k] * d
                    m = rate * mu
                    v = kept[k] * mu + rate * v
                sums_ref[pl.ds(n, 1), lanes] += jnp.sum(sum_m, 0, keepdims=True)
                sums_ref[pl.ds(dims + n, 1), lanes] += jnp.sum(sum_v, 0, keepdims=True)
            for k in range(steps):
                ng_ref[pl.ds(base + k, CHUNKS, stride=steps), :] = total[k]
        return carry

    lax.fori_loop(0, width // LANES, lane, 0)
    normed_grad = from_slabs(ng_ref[...], tokens) + n0_ref[...] + n1_ref[...]
    hat, scale = norm_parts(x_ref[...].astype(F32))
    at = 2 * dims
    for j in range(width // LANES):
        slab = slice(j * tokens, (j + 1) * tokens)
        sums_ref[at : at + 1, j * LANES : (j + 1) * LANES] = jnp.sum(
            pg_ref[slab, :] * normed_ref[slab, :], 0, keepdims=True
        )
    sums_ref[at + 1 : at + 2, :] = jnp.sum(normed_grad * hat, 0, keepdims=True)
    sums_ref[at + 2 : at + 3, :] = gg_ref[...]
    zd = qk_ref.shape[1]
    for i in range(3):
        sums_ref[at + 3 : at + 4, i * zd : (i + 1) * zd] = qk_ref[i : i + 1, :]
    xg_ref[...] = (direct_ref[...] + norm_back(normed_grad * g_ref[...], hat, scale)).astype(LOW)


def swap(x, axis, bit):
    size = lax.axis_size(axis)
    return lax.ppermute(x, axis, [(i, i ^ bit) for i in range(size)])


def shift(x, by):
    size = lax.axis_size("tensor")
    return lax.ppermute(
        x, "tensor", [(i, i + by) for i in range(size) if 0 <= i + by < size]
    )


def parity_of(bit):
    return (lax.axis_index("dp") // bit) & 1


def half_of(share, bit):
    half = share.shape[0] // 2
    return lax.dynamic_slice_in_dim(share, parity_of(bit) * half, half)


def joined(mine, other, bit):
    return jnp.where(
        parity_of(bit) == 0,
        jnp.concatenate([mine, other], 0),
        jnp.concatenate([other, mine], 0),
    )


tied = lax.optimization_barrier


def rounded(v):
    return lax.reduce_precision(v, 8, 7)


def halves(v, bit):
    half, parity = v.shape[0] // 2, parity_of(bit)
    return (
        lax.dynamic_slice_in_dim(v, parity * half, half),
        lax.dynamic_slice_in_dim(v, (1 - parity) * half, half).astype(LOW),
    )


def reduction(kind, near, far):
    bits = [1 << b for b in range(lax.axis_size("dp").bit_length() - 1)]
    lead = {"x": [1], "z": [2]}.get(kind, [])
    spread = {"x": [2], "z": [1], "y": [1, 2], "w": [2, 1]}[kind]
    near, far = near(), far()
    for bit in lead:
        near, away = halves(near, bit)
        far, far_away = halves(far, bit)
        got = yield "dp", bit, jnp.concatenate([away, far_away], 0)
        got = got.astype(F32)
        near, far = near + got[: near.shape[0]], far + got[near.shape[0] :]
    got = yield "tensor", 2, far.astype(LOW)
    total = near + got.astype(F32)
    for bit in spread:
        total, away = halves(total, bit)
        got = yield "dp", bit, away
        total = total + got.astype(F32)
    for bit in bits[2:]:
        total = rounded(total)
        got = yield "dp", bit, total.astype(LOW)
        total = total + got.astype(F32)
    low = total.astype(LOW)
    for bit in reversed(lead + spread):
        got = yield "dp", bit, low
        low = joined(low, got, bit)
    return low


def one_swap(axis, bit, v):
    got = yield axis, bit, v
    return got


def everywhere(v, kind):
    for axis in ("tensor", "dp"):
        for b in range(lax.axis_size(axis).bit_length() - 1):
            v = lax.reduce_precision(v, 8, 7) if kind == LOW else v
            got = yield axis, 1 << b, v.astype(kind)
            v = v + got.astype(F32)
    return v


class Pump:
    def __init__(self, token):
        self.token = token
        self.flows, self.ready, self.flying, self.done = {}, {}, {}, {}

    def gate(self, v):
        v, self.token = tied((v, self.token))
        return v

    def add(self, name, flow):
        self.flows[name] = flow
        self.ready[name] = next(flow)

    def issue(self, name):
        axis, bit, v = self.ready.pop(name)
        self.flying[name] = swap(self.gate(v), axis, bit)

    def finish(self, name):
        got = self.gate(self.flying.pop(name))
        try:
            self.ready[name] = self.flows[name].send(got)
        except StopIteration as end:
            self.done[name] = end.value

    def drain(self):
        while self.ready or self.flying:
            for name in list(self.ready):
                self.issue(name)
            for name in list(self.flying):
                self.finish(name)


def side_by_side(pack):
    half = pack.shape[0] // 2
    return jnp.concatenate([pack[:half], pack[half:]], 1)


def shards(
    layer_input,
    doc_lengths,
    norm1_gain,
    alpha_raw,
    delta_raw,
    ema_beta,
    ema_eta,
    ema_omega,
    w_z,
    q_gain,
    q_bias,
    k_gain,
    w_value,
    w_reset,
    w_update,
    w_hidden,
    w_out,
    norm2_gain,
    w_ffn_in,
    w_ffn_out,
    cotangent,
):
    member = lax.axis_index("tensor")
    rows, length, width = layer_input.shape
    tokens = rows * length
    dims = alpha_raw.shape[0]
    zd = w_z.shape[1]
    units = w_value.shape[1]
    cols = w_hidden.shape[0]
    x = layer_input.reshape(tokens, width)
    cot = cotangent.reshape(tokens, width)
    g1, g2, om = norm1_gain[None], norm2_gain[None], ema_omega[None]
    qg, qb, kg = q_gain[None], q_bias[None], k_gain[None]

    docs = doc_lengths.shape[1]
    order = jnp.arange(docs)
    ends = jnp.sum(
        jnp.where(order[:, None] <= order[None, :], doc_lengths[:, :, None], 0), 1
    ).astype(jnp.int32)
    starts = ends - doc_lengths
    places = member * length + jnp.arange(length, dtype=jnp.int32)
    docid = jnp.sum((places[None, :, None] >= ends[:, None, :]).astype(jnp.int32), 2)
    keep = 1.0 - jnp.any(places[None, :, None] == starts[:, None, :], 2).astype(F32)
    keep = jnp.broadcast_to(keep.reshape(tokens, 1), (tokens, LANES))
    blocks = docid.reshape(tokens // STRETCH, STRETCH)
    spot = jnp.arange(STRETCH)
    mask = (spot[None, :] <= spot[:, None])[None] & (blocks[:, :, None] == blocks[:, None, :])
    mask = mask.astype(F32).reshape(tokens, STRETCH)

    def unbroken(part):
        low, high = part * length, (part + 1) * length
        inside = jnp.any((starts >= low) & (starts < high), 1)
        return jnp.broadcast_to(1.0 - inside.astype(F32)[:, None], (rows, LANES))

    offs = (member ^ jnp.arange(4, dtype=jnp.int32)) * cols

    vm = lambda shape: pltpu.VMEM(shape, F32)
    tab = (dims, width)
    wide = (tokens, width)
    mat = 2.0 * tokens * width
    ema = 8.0 * tokens * width * dims
    chunked = (rows * dims * CHUNKS, width)
    finals = (rows * dims, width)
    slabs = (tokens * width // LANES, LANES)

    w_join = jnp.concatenate([w_hidden, w_out], 0)
    shares = (w_value, w_reset, w_join, w_ffn_in, w_ffn_out)
    bits = (1, 1, 2, 1, 1)
    pump = Pump(offs)
    beside = [swap(w_value, "tensor", 1), swap(w_reset, "tensor", 1)]
    half_v, half_r, half_g, half_i, half_o = (
        half_of(w, bit) for w, bit in zip(shares, bits, strict=True)
    )

    over_v = swap(half_v, "tensor", 2)

    normed, normed_low, init, last = call(
        functools.partial(first_pass, rows),
        [(slabs, F32), (wide, LOW), (chunked, F32), (finals, F32)],
        (x, g1, alpha_raw, delta_raw, ema_beta, keep),
        ema,
        [vm(tab), vm(tab)],
    )
    f1, f2 = shift(last, 1), shift(last, 2)
    f1, f2 = pump.gate(f1), pump.gate(f2)
    beside = [pump.gate(w) for w in beside]
    over_r = swap(pump.gate(half_r), "tensor", 2)
    beside += [swap(pump.gate(w), "tensor", 1) for w in (w_ffn_in, w_ffn_out)]
    pre, mixed_low, z_pre, gate, probs = call(
        functools.partial(second_pass, rows),
        [(slabs, F32), (wide, LOW), ((tokens, zd), F32), (wide, F32), ((tokens, STRETCH), F32)],
        (normed, init, f1, f2, keep, unbroken(member - 1), alpha_raw, delta_raw, ema_beta,
         ema_eta, om, w_z, w_update, qg, qb, kg, mask),
        ema + mat * width,
        [vm(tab), vm(tab)],
    )
    split = (2, tokens, units)
    mixed_low = pump.gate(mixed_low)
    over_v = pump.gate(over_v)
    other_v = swap(over_v, "dp", 1)
    over_g = swap(pump.gate(half_g), "tensor", 2)
    beside = [pump.gate(w) for w in beside]
    mixed_low = pump.gate(mixed_low)

    def values(weights):
        return call(
            value_part,
            [(split, F32), (split, F32), (split, F32), (split, LOW)],
            (normed_low, mixed_low, probs, *weights),
            4 * mat * units,
        )

    own_part = values((w_value, w_reset, beside[0], beside[1]))
    united0 = pump.gate(own_part[3])
    over_r = pump.gate(over_r)
    other_r = swap(over_r, "dp", 1)
    over_i = swap(pump.gate(half_i), "tensor", 2)
    other_v = pump.gate(other_v)
    full_v = pump.gate(joined(over_v, other_v, 1))
    both_v = swap(full_v, "tensor", 1)
    over_g = pump.gate(over_g)
    other_g = swap(over_g, "dp", 2)
    over_o = swap(pump.gate(half_o), "tensor", 2)
    other_r = pump.gate(other_r)
    full_r = pump.gate(joined(over_r, other_r, 1))
    both_r = swap(full_r, "tensor", 1)
    both_v, both_r = pump.gate(both_v), pump.gate(both_r)
    over_i = pump.gate(over_i)
    full_v = pump.gate(full_v)
    far_part = values((full_v, full_r, both_v, both_r))
    united1 = pump.gate(far_part[3])
    other_i = swap(over_i, "dp", 1)
    over_o = pump.gate(over_o)
    other_o = swap(over_o, "dp", 1)
    other_g = pump.gate(other_g)
    near_g = pump.gate(jnp.stack([w_join, joined(over_g, other_g, 2)]))
    beside_g = swap(near_g, "tensor", 1)
    other_i = pump.gate(other_i)
    full_i = pump.gate(joined(over_i, other_i, 1))
    both_i = swap(full_i, "tensor", 1)
    beside_g = pump.gate(beside_g)
    wg = (near_g, beside_g)
    wv, wr = (w_value, beside[0], full_v, both_v), (w_reset, beside[1], full_r, both_r)
    kept_parts = ((*own_part[:3], united0), (*far_part[:3], united1))
    hidden_pre, blended, second, whid = call(
        blend_part,
        [(wide, F32), (wide, F32), (wide, LOW), ((width, width), LOW)],
        (offs, x, mixed_low, gate, united0, united1, *wg, g2),
        mat * (width + 4 * units),
        smem=(0,),
    )
    second = pump.gate(second)
    ffn_rows = width + 2 * units

    def ffn_of(weights):
        return call(
            ffn_part,
            [(wide, F32), (wide, F32), ((ffn_rows, units), F32), ((ffn_rows, units), LOW)],
            (second, cot, *weights),
            12 * mat * units,
        )

    ffn0 = ffn_of((w_ffn_in, beside[2], w_ffn_out, beside[3]))
    back0 = pump.gate(ffn0[1])
    other_o = pump.gate(other_o)
    full_o = pump.gate(joined(over_o, other_o, 1))
    both_o = swap(full_o, "tensor", 1)
    both_i, both_o = pump.gate(both_i), pump.gate(both_o)
    ffn1 = ffn_of((full_i, both_i, full_o, both_o))
    pump.add("F0", one_swap("tensor", 1, ffn0[3]))
    pump.add("F1", one_swap("tensor", 1, ffn1[3]))
    own = (2, 4 * cols, width // 2)
    pack_rows = 2 * width + 2 * units
    held = {}

    def run_blend():
        held["bb"] = call(
            blend_back,
            [(wide, LOW), (wide, F32), (wide, LOW), (wide, F32), ((1, width), F32), (own, F32), (own, LOW)],
            (offs, x, cot, pump.gate(blended), ffn1[1], back0, ffn0[0], ffn1[0], hidden_pre, gate,
             mixed_low, g2, w_update, whid),
            4 * mat * width,
            [vm((width, width))],
            smem=(0,),
        )
        held["hidden"] = pump.gate(held["bb"][2])
        pump.add("P0", one_swap("tensor", 1, held["bb"][6]))

    def run_values(p):
        held[p] = [*call(
            functools.partial(value_back, p),
            [(wide, F32), (wide, F32), ((tokens, STRETCH), F32), ((pack_rows, units), F32), ((pack_rows, units), LOW)],
            (pump.gate(held["hidden"]), normed_low, mixed_low, probs, *kept_parts[p], *wg,
             wv[2 * p], wr[2 * p], wv[2 * p + 1], wr[2 * p + 1]),
            14 * mat * units,
        )]
        pump.token, held[p][2] = tied((pump.token, held[p][2]))
        pump.add(f"V{p}", one_swap("tensor", 1, held[p][4]))

    def run_third():
        held["t3"] = call(
            functools.partial(third_pass, rows),
            [(slabs, F32), ((width, zd), F32), ((8, zd), F32), (chunked, F32), (chunked, F32), (finals, F32), (finals, F32)],
            (pump.gate(z_pre), probs, held[0][2], held[1][2], qg, qb, kg, w_z, mixed_low, held["bb"][3],
             held[0][1], held[1][1], pre, keep, alpha_raw, delta_raw),
            2 * ema,
            [vm((2, tokens, zd))],
        )
        pump.add("dz", everywhere(held["t3"][1], LOW))

    def send_back():
        back = pump.gate(jnp.concatenate([held["t3"][5], held["t3"][6]], 0))
        held["back"] = shift(back, -1), shift(back, -2)

    def take_back():
        held["back"] = [pump.gate(v) for v in held["back"]]

    def run_fourth():
        t3 = held["t3"]
        held["t4"] = call(
            functools.partial(fourth_pass, rows),
            [(wide, LOW), ((2 * dims + 8, width), F32)],
            (t3[0], normed, t3[3], t3[4], *held["back"], keep, unbroken(member + 1), alpha_raw,
             delta_raw, ema_beta, ema_eta, om, held[0][0], held[1][0], x, g1, held["bb"][1],
             held["bb"][4], t3[2]),
            2 * ema,
            [vm(tab), vm(tab), vm(slabs)],
        )
        pump.add("sm", everywhere(pump.gate(held["t4"][1]), F32))

    def pack(p, source, at, end):
        kept = (ffn0, ffn1)[p][2] if source == "F" else held[p][3]
        return kept[at:end] + pump.done[f"{source}{p}"][at:end].astype(F32)

    def add_flow(name):
        if name == "P":
            kept, got = held["bb"][5], pump.done["P0"].astype(F32)
            near, far = (lambda: kept[0] + got[0]), (lambda: kept[1] + got[1])
        else:
            source = "F" if name == "F" else "V"
            at, end = {"F": (0, 2 * width), "R": (0, width), "O": (width, 2 * width), "N": (2 * width, 3 * width)}[name]
            near, far = (lambda: pack(0, source, at, end)), (lambda: pack(1, source, at, end))
        pump.add(name, reduction(KINDS[name], near, far))

    kernels = {
        "bb": run_blend,
        "v1": lambda: run_values(1),
        "v0": lambda: run_values(0),
        "t3": run_third,
        "t4": run_fourth,
    }
    for word in ORDER:
        sign, name = word[0], word[1:]
        if sign == "K":
            kernels[name]()
        elif name == "E":
            (send_back if sign == "+" else take_back)()
        elif sign == "+":
            if name in KINDS and name not in pump.flows:
                add_flow(name)
            pump.issue(name)
        else:
            pump.finish(name)
    pump.drain()
    output, input_grad = held["bb"][0], held["t4"][0]
    sums, dz_sum, pair_sum, ffn_sum = (pump.done[n] for n in ("sm", "dz", "P", "F"))
    reset_sum, out_sum, value_sum = (pump.done[n] for n in "RON")

    alpha, sigma = jax.nn.sigmoid(alpha_raw), jax.nn.sigmoid(delta_raw)
    with_mu, with_nu = sums[:dims], sums[dims : 2 * dims]
    drive_grad = ema_eta * with_mu
    decay_grad = ema_eta * (alpha * ema_beta) * with_nu
    at = 2 * dims
    quarter = side_by_side(pair_sum[: 2 * cols])
    pair = jnp.stack([quarter, swap(quarter, "tensor", 2)])
    quarters = jnp.stack([pair, swap(pair, "tensor", 1)], 1).reshape(4, cols, width)
    update_grad = jnp.concatenate(
        [lax.dynamic_index_in_dim(quarters, g ^ member, 0, False) for g in range(4)], 0
    )
    return (
        output.reshape(layer_input.shape),
        input_grad.reshape(layer_input.shape),
        sums[at + 1],
        (ema_beta * drive_grad - sigma * decay_grad) * alpha * (1.0 - alpha),
        -alpha * decay_grad * sigma * (1.0 - sigma),
        alpha * drive_grad,
        (alpha * ema_beta) * with_mu,
        sums[at],
        dz_sum,
        sums[at + 3, :zd],
        sums[at + 3, zd : 2 * zd],
        sums[at + 3, 2 * zd : 3 * zd],
        value_sum.astype(F32),
        reset_sum.astype(F32),
        update_grad.astype(F32),
        side_by_side(pair_sum[2 * cols :]).astype(F32),
        side_by_side(out_sum).astype(F32),
        sums[at + 2],
        ffn_sum[:width].astype(F32),
        side_by_side(ffn_sum[width:]).astype(F32),
    )


def solution(mesh):
    whole, by_row = P(), P("dp", "tensor", None)
    by_col, by_unit = P(None, "tensor"), P("tensor", None)
    return jax.shard_map(
        shards,
        mesh=mesh,
        in_specs=(by_row, P("dp", None), *(whole,) * 10, by_col, by_col, whole, by_unit, by_unit, whole, by_col, by_unit, by_row),
        out_specs=(by_row, by_row, *(whole,) * 10, by_col, by_col, whole, by_unit, by_unit, whole, by_col, by_unit),
        check_vma=False,
    )
```

```python
import functools

import jax
import jax.numpy as jnp
from jax import lax
from jax.experimental import pallas as pl
from jax.experimental.pallas import tpu as pltpu
from jax.sharding import PartitionSpec as P

STRETCH = 128
LANES = 128
CHUNKS = 8
F32 = jnp.float32
LOW = jnp.bfloat16
KINDS = {"F": "w", "P": "x", "R": "x", "O": "z", "N": "x"}
ORDER = (
    "+F0", "+F1", "Kbb", "-F0", "-F1", "+P0", "Kv1", "-P0", "+V1", "+F",
    "+P", "Kv0", "-V1", "+V0", "Kt3", "-V0", "+dz", "+E", "-P", "+R",
    "-dz", "+O", "-F", "+N", "-R", "+P", "-O", "+F", "-E", "Kt4",
    "-P", "+R", "+sm", "-N", "+P", "-sm", "+N", "-F", "+F", "-P",
    "+P", "-R", "+dz", "+R", "-F", "+sm", "-N", "+F", "-R", "+O",
    "-P", "-dz", "+N", "+dz", "-sm", "+P", "-dz", "-O", "-N", "+R",
    "+sm", "+dz", "-P", "+O", "-F", "+P", "-sm", "+N", "-O", "+sm",
    "-dz", "+O", "-R", "+F", "-P", "+R", "-sm", "+dz", "-N", "+N",
    "-F", "-R", "+R", "+F", "-O", "+O", "-N", "+N", "-dz", "-R",
    "-O", "+sm", "+O", "-F", "-N", "-sm", "-O",
)


def silu(v):
    return v * jax.nn.sigmoid(v)


def silu_slope(v):
    s = jax.nn.sigmoid(v)
    return s * (1.0 + v * (1.0 - s))


def dot(a, b):
    return jnp.dot(a, b, preferred_element_type=F32)


def dot_rows(a, b):
    return lax.dot_general(a, b, (((0,), (0,)), ((), ())), preferred_element_type=F32)


def dot_cols(a, b):
    return lax.dot_general(a, b, (((1,), (1,)), ((), ())), preferred_element_type=F32)


def norm_parts(v):
    center = v - jnp.mean(v, -1, keepdims=True)
    scale = lax.rsqrt(jnp.mean(center * center, -1, keepdims=True) + 1e-05)
    return center * scale, scale


def norm_back(grad, hat, scale):
    return scale * (
        grad - jnp.mean(grad, -1, keepdims=True) - hat * jnp.mean(grad * hat, -1, keepdims=True)
    )


def call(kernel, outs, args, flops, scratch=(), smem=(), limit=12 << 20):
    specs = [
        pl.BlockSpec(memory_space=pltpu.SMEM if i in smem else pltpu.VMEM)
        for i in range(len(args))
    ]
    outs = [jax.ShapeDtypeStruct(s, d) for s, d in outs]
    size = sum(a.size * a.dtype.itemsize for a in args) + sum(
        o.size * o.dtype.itemsize for o in outs
    )
    return pl.pallas_call(
        kernel,
        out_shape=outs,
        in_specs=specs,
        out_specs=[pl.BlockSpec(memory_space=pltpu.VMEM) for _ in outs],
        scratch_shapes=list(scratch),
        compiler_params=pltpu.CompilerParams(vmem_limit_bytes=limit),
        cost_estimate=pl.CostEstimate(flops=int(flops), bytes_accessed=int(size), transcendentals=0),
    )(*args)


def bcast(ref, row, lanes):
    return jnp.broadcast_to(ref[pl.ds(row, 1), lanes], (CHUNKS, LANES))


def shifted(v, by, fill):
    place = lax.broadcasted_iota(jnp.int32, v.shape, 0)
    if by > 0:
        return jnp.where(place >= by, pltpu.roll(v, by, 0), fill)
    return jnp.where(place < CHUNKS + by, pltpu.roll(v, CHUNKS + by, 0), fill)


def power(v, n):
    out = None
    while n:
        if n & 1:
            out = v if out is None else out * v
        n >>= 1
        if n:
            v = v * v
    return out


def chunk_powers(base, order):
    place = lax.broadcasted_iota(jnp.int32, base.shape, 0)
    place = place if order > 0 else (CHUNKS - 1) - place
    out = jnp.where(place & 1 == 1, base, 1.0)
    base = base * base
    out = out * jnp.where(place & 2 == 2, base, 1.0)
    base = base * base
    return out * jnp.where(place & 4 == 4, base, 1.0)


def rate_tables(al_ref, de_ref, be_ref, dec_ref, drv_ref):
    alpha = jax.nn.sigmoid(al_ref[...])
    dec_ref[...] = 1.0 - alpha * jax.nn.sigmoid(de_ref[...])
    drv_ref[...] = alpha * be_ref[...]


def steps_of(ref, base, steps):
    return [ref[pl.ds(base + k, CHUNKS, stride=steps), :] for k in range(steps)]


def into_slabs(ref, v):
    tokens = v.shape[0]
    for j in range(v.shape[1] // LANES):
        ref[j * tokens : (j + 1) * tokens, :] = v[:, j * LANES : (j + 1) * LANES]


def from_slabs(v, tokens):
    return jnp.concatenate(
        [v[at : at + tokens] for at in range(0, v.shape[0], tokens)], 1
    )


def product(values):
    out = values[0]
    for v in values[1:]:
        out = out * v
    return out


def first_pass(rows, x_ref, g_ref, al_ref, de_ref, be_ref, keep_ref, normed_ref, low_ref, init_ref, last_ref, dec_ref, drv_ref):
    hat, _ = norm_parts(x_ref[...].astype(F32))
    normed = hat * g_ref[...]
    into_slabs(normed_ref, normed)
    low_ref[...] = normed.astype(LOW)
    rate_tables(al_ref, de_ref, be_ref, dec_ref, drv_ref)
    dims, width = al_ref.shape
    tokens = x_ref.shape[0]
    length = tokens // rows
    steps = length // CHUNKS

    def lane(j, carry):
        lanes = pl.ds(pl.multiple_of(j * LANES, LANES), LANES)
        for row in range(rows):
            token = steps_of(normed_ref, j * tokens + row * length, steps)
            kept = steps_of(keep_ref, row * length, steps)
            whole = product(kept)
            for n in range(dims):
                d, b = bcast(dec_ref, n, lanes), bcast(drv_ref, n, lanes)
                s = b * token[0]
                for k in range(1, steps):
                    s = (kept[k] * d) * s + b * token[k]
                a = power(d, steps) * whole
                for by in (1, 2, 4):
                    s = s + a * shifted(s, by, 0.0)
                    a = a * shifted(a, by, 1.0)
                init_ref[pl.ds((row * dims + n) * CHUNKS, CHUNKS), lanes] = shifted(s, 1, 0.0)
                last_ref[pl.ds(row * dims + n, 1), lanes] = s[CHUNKS - 1 :, :]
        return carry

    lax.fori_loop(0, width // LANES, lane, 0)


def second_pass(rows, normed_ref, init_ref, f1_ref, f2_ref, keep_ref, flag_ref, al_ref, de_ref, be_ref, eta_ref, om_ref, wz_ref, wu_ref, qg_ref, qb_ref, kg_ref, mask_ref, pre_ref, mixed_ref, zpre_ref, gate_ref, probs_ref, dec_ref, drv_ref):
    rate_tables(al_ref, de_ref, be_ref, dec_ref, drv_ref)
    dims, width = al_ref.shape
    tokens = keep_ref.shape[0]
    length = tokens // rows
    steps = length // CHUNKS

    def lane(j, carry):
        lanes = pl.ds(pl.multiple_of(j * LANES, LANES), LANES)
        omega = bcast(om_ref, 0, lanes)
        for row in range(rows):
            base = j * tokens + row * length
            token = steps_of(normed_ref, base, steps)
            kept = steps_of(keep_ref, row * length, steps)
            reach = shifted(product(kept), 1, 1.0)
            for by in (1, 2, 4):
                reach = reach * shifted(reach, by, 1.0)
            flag = bcast(flag_ref, row, pl.ds(0, LANES))
            total = [omega * t for t in token]
            for n in range(dims):
                d, b, e = bcast(dec_ref, n, lanes), bcast(drv_ref, n, lanes), bcast(eta_ref, n, lanes)
                chunk = power(d, steps)
                entering = bcast(f1_ref, row * dims + n, lanes) + (
                    power(chunk, CHUNKS) * flag
                ) * bcast(f2_ref, row * dims + n, lanes)
                s = (
                    init_ref[pl.ds((row * dims + n) * CHUNKS, CHUNKS), lanes]
                    + reach * chunk_powers(chunk, 1) * entering
                )
                for k in range(steps):
                    s = (kept[k] * d) * s + b * token[k]
                    total[k] = total[k] + e * s
            for k in range(steps):
                pre_ref[pl.ds(base + k, CHUNKS, stride=steps), :] = total[k]
        return carry

    lax.fori_loop(0, width // LANES, lane, 0)
    mixed_low = from_slabs(silu(pre_ref[...]).astype(LOW), tokens)
    mixed_ref[...] = mixed_low
    z_pre = dot(mixed_low, wz_ref[...])
    zpre_ref[...] = z_pre
    gate_ref[...] = jax.nn.sigmoid(dot(mixed_low, wu_ref[...]))
    z_low = silu(z_pre).astype(LOW).astype(F32)
    queries = (z_low * qg_ref[...] + qb_ref[...]).astype(LOW)
    keys = (z_low * kg_ref[...]).astype(LOW)
    for start in range(0, z_low.shape[0], STRETCH):
        block = slice(start, start + STRETCH)
        scores = dot_cols(queries[block], keys[block]) * z_low.shape[1] ** (-0.5)
        scores = jnp.where(mask_ref[block, :] > 0.5, scores, -1e30)
        shift = jnp.exp(scores - jnp.max(scores, -1, keepdims=True))
        probs_ref[block, :] = shift / jnp.sum(shift, -1, keepdims=True)


def value_part(normed_ref, mixed_ref, probs_ref, va_ref, ra_ref, vb_ref, rb_ref, vpre_ref, rpre_ref, att_ref, united_ref):
    tokens = normed_ref.shape[0]
    for i, (v_ref, r_ref) in enumerate(((va_ref, ra_ref), (vb_ref, rb_ref))):
        value_pre = dot(normed_ref[...], v_ref[...])
        reset_pre = dot(mixed_ref[...], r_ref[...])
        vpre_ref[i] = value_pre
        rpre_ref[i] = reset_pre
        values = silu(value_pre).astype(LOW)
        for start in range(0, tokens, STRETCH):
            block = slice(start, start + STRETCH)
            att_ref[i, block, :] = dot(probs_ref[block, :].astype(LOW), values[block])
        united_ref[i] = (silu(reset_pre) * att_ref[i]).astype(LOW)


def blend_part(offs_ref, x_ref, mixed_ref, gate_ref, u0_ref, u1_ref, ga_ref, gb_ref, gain_ref, hpre_ref, blended_ref, second_ref, whid_ref):
    cols = whid_ref.shape[0] // 4
    for r in range(4):
        whid_ref[pl.ds(pl.multiple_of(offs_ref[r], 64), cols), :] = (ga_ref, gb_ref)[r % 2][r // 2, :cols, :]
    hidden_pre = dot(mixed_ref[...], whid_ref[...])
    for r in range(4):
        united = (u0_ref, u1_ref)[r // 2][r % 2]
        hidden_pre = hidden_pre + dot(united, (ga_ref, gb_ref)[r % 2][r // 2, cols:, :])
    hpre_ref[...] = hidden_pre
    x = x_ref[...].astype(F32)
    blended = x + gate_ref[...] * (silu(hidden_pre) - x)
    blended_ref[...] = blended
    hat, _ = norm_parts(blended)
    second_ref[...] = (hat * gain_ref[...]).astype(LOW)


def ffn_part(second_ref, cot_ref, ia_ref, ib_ref, oa_ref, ob_ref, out_ref, sg_ref, keep_ref, send_ref):
    second, cot = second_ref[...], cot_ref[...]
    depth, units = ia_ref.shape
    half = depth // 2
    for i, (in_ref, fo_ref, pack_ref) in enumerate(
        ((ia_ref, oa_ref, keep_ref), (ib_ref, ob_ref, send_ref))
    ):
        up_pre = dot(second, in_ref[...])
        activated = silu(up_pre).astype(LOW)
        up_grad = (dot_cols(cot, fo_ref[...]) * silu_slope(up_pre)).astype(LOW)
        out = dot(activated, fo_ref[...])
        back = dot_cols(up_grad, in_ref[...])
        out_ref[...] = out if i == 0 else out_ref[...] + out
        sg_ref[...] = back if i == 0 else sg_ref[...] + back
        kind = pack_ref.dtype
        pack_ref[:depth, :] = dot_rows(second, up_grad).astype(kind)
        for h in range(2):
            pack_ref[depth + h * units : depth + (h + 1) * units, :] = dot_rows(
                activated, cot[:, h * half : (h + 1) * half]
            ).astype(kind)


def blend_back(offs_ref, x_ref, cot_ref, blended_ref, s0_ref, s1_ref, o0_ref, o1_ref, hpre_ref, gate_ref, mixed_ref, gain_ref, wu_ref, whid_ref, y_ref, direct_ref, hidden_ref, mg_ref, gg_ref, keep_ref, send_ref, full_ref):
    blended = blended_ref[...]
    y_ref[...] = (blended + (o0_ref[...] + o1_ref[...])).astype(LOW)
    second_grad = s0_ref[...] + s1_ref[...]
    hat, scale = norm_parts(blended)
    gg_ref[...] = jnp.sum(second_grad * hat, 0, keepdims=True)
    grad = cot_ref[...].astype(F32) + norm_back(second_grad * gain_ref[...], hat, scale)
    gate, hidden_pre, x = gate_ref[...], hpre_ref[...], x_ref[...].astype(F32)
    direct_ref[...] = grad * (1.0 - gate)
    hidden_low = (grad * gate * silu_slope(hidden_pre)).astype(LOW)
    gate_low = (grad * (silu(hidden_pre) - x) * gate * (1.0 - gate)).astype(LOW)
    hidden_ref[...] = hidden_low
    mg_ref[...] = dot_cols(gate_low, wu_ref[...]) + dot_cols(hidden_low, whid_ref[...])
    width = x.shape[1]
    cols, half = width // 4, width // 2
    for i, low in enumerate((gate_low, hidden_low)):
        full_ref[...] = dot_rows(mixed_ref[...], low)
        for r in range(4):
            pack_ref = (keep_ref, send_ref)[r % 2]
            rows = pl.ds(pl.multiple_of(offs_ref[r], 64), cols)
            for h in range(2):
                at = (2 * i + h) * cols
                pack_ref[r // 2, at : at + cols, :] = full_ref[
                    rows, h * half : (h + 1) * half
                ].astype(pack_ref.dtype)


def value_back(part, hidden_ref, normed_ref, mixed_ref, probs_ref, vpre_ref, rpre_ref, att_ref, united_ref, ga_ref, gb_ref, va_ref, ra_ref, vb_ref, rb_ref, ng_ref, mg_ref, pg_ref, keep_ref, send_ref):
    hidden, normed, mixed = hidden_ref[...], normed_ref[...], mixed_ref[...]
    tokens, depth = hidden.shape
    units = va_ref.shape[1]
    cols = ga_ref.shape[1] - units
    half = depth // 2
    for i, (g_ref, v_ref, r_ref, pack_ref) in enumerate(
        ((ga_ref, va_ref, ra_ref, keep_ref), (gb_ref, vb_ref, rb_ref, send_ref))
    ):
        kind = pack_ref.dtype
        united_grad = dot_cols(hidden, g_ref[part, cols:, :])
        reset_pre, value_pre = rpre_ref[i], vpre_ref[i]
        reset_low = (united_grad * att_ref[i] * silu_slope(reset_pre)).astype(LOW)
        attended_low = (united_grad * silu(reset_pre)).astype(LOW)
        values = silu(value_pre).astype(LOW)
        parts = []
        for start in range(0, tokens, STRETCH):
            block = slice(start, start + STRETCH)
            parts.append(dot_rows(probs_ref[block, :].astype(LOW), attended_low[block]))
            back = dot_cols(attended_low[block], values[block])
            pg_ref[block, :] = back if i == 0 else pg_ref[block, :] + back
        value_low = (jnp.concatenate(parts, 0) * silu_slope(value_pre)).astype(LOW)
        into_normed = dot_cols(value_low, v_ref[...])
        into_mixed = dot_cols(reset_low, r_ref[...])
        ng_ref[...] = into_normed if i == 0 else ng_ref[...] + into_normed
        mg_ref[...] = into_mixed if i == 0 else mg_ref[...] + into_mixed
        pack_ref[:depth, :] = dot_rows(mixed, reset_low).astype(kind)
        for h in range(2):
            pack_ref[depth + h * units : depth + (h + 1) * units, :] = dot_rows(
                united_ref[i], hidden[:, h * half : (h + 1) * half]
            ).astype(kind)
        pack_ref[2 * depth :, :] = dot_rows(normed, value_low).astype(kind)


def third_pass(rows, zpre_ref, probs_ref, p0_ref, p1_ref, qg_ref, qb_ref, kg_ref, wz_ref, mixed_ref, m0_ref, m1_ref, m2_ref, pre_ref, keep_ref, al_ref, de_ref, pg_ref, dz_ref, small_ref, im_ref, iv_ref, lm_ref, lv_ref, qk_ref):
    z_pre = zpre_ref[...]
    z_low = silu(z_pre).astype(LOW).astype(F32)
    queries = (z_low * qg_ref[...] + qb_ref[...]).astype(LOW)
    keys = (z_low * kg_ref[...]).astype(LOW)
    for start in range(0, z_low.shape[0], STRETCH):
        block = slice(start, start + STRETCH)
        probs = probs_ref[block, :]
        grad = p0_ref[block, :] + p1_ref[block, :]
        grad = probs * (grad - jnp.sum(probs * grad, -1, keepdims=True)) * z_low.shape[1] ** (-0.5)
        high = grad.astype(LOW)
        rest = (grad - high.astype(F32)).astype(LOW)
        qk_ref[0, block, :] = dot(high, keys[block]) + dot(rest, keys[block])
        qk_ref[1, block, :] = dot_rows(high, queries[block]) + dot_rows(rest, queries[block])
    query_grad, key_grad = qk_ref[0], qk_ref[1]
    small_ref[...] = jnp.zeros_like(small_ref)
    small_ref[0:1, :] = jnp.sum(query_grad * z_low, 0, keepdims=True)
    small_ref[1:2, :] = jnp.sum(query_grad, 0, keepdims=True)
    small_ref[2:3, :] = jnp.sum(key_grad * z_low, 0, keepdims=True)
    z_grad = ((query_grad * qg_ref[...] + key_grad * kg_ref[...]) * silu_slope(z_pre)).astype(LOW)
    dz_ref[...] = dot_rows(mixed_ref[...], z_grad)
    mixed_grad = m0_ref[...] + m1_ref[...] + m2_ref[...] + dot_cols(z_grad, wz_ref[...])
    into_slabs(pg_ref, mixed_grad)
    pg_ref[...] = pg_ref[...] * silu_slope(pre_ref[...])
    dims, width = al_ref.shape
    tokens = z_pre.shape[0]
    length = tokens // rows
    steps = length // CHUNKS

    def lane(j, carry):
        lanes = pl.ds(pl.multiple_of(j * LANES, LANES), LANES)
        for row in range(rows):
            token = steps_of(pg_ref, j * tokens + row * length, steps)
            kept = steps_of(keep_ref, row * length, steps)
            whole = product(kept)
            for n in range(dims):
                alpha = jax.nn.sigmoid(bcast(al_ref, n, lanes))
                d = 1.0 - alpha * jax.nn.sigmoid(bcast(de_ref, n, lanes))
                mu = token[steps - 1]
                m = (kept[steps - 1] * d) * mu
                v = kept[steps - 1] * mu
                for k in range(steps - 2, -1, -1):
                    mu = token[k] + m
                    rate = kept[k] * d
                    m = rate * mu
                    v = kept[k] * mu + rate * v
                a = power(d, steps) * whole
                b = steps * power(d, steps - 1) * whole
                for by in (-1, -2, -4):
                    mp, vp = shifted(m, by, 0.0), shifted(v, by, 0.0)
                    ap, bp = shifted(a, by, 1.0), shifted(b, by, 0.0)
                    v = v + a * vp + b * mp
                    m = m + a * mp
                    b = a * bp + b * ap
                    a = a * ap
                at = pl.ds((row * dims + n) * CHUNKS, CHUNKS)
                im_ref[at, lanes] = shifted(m, -1, 0.0)
                iv_ref[at, lanes] = shifted(v, -1, 0.0)
                lm_ref[pl.ds(row * dims + n, 1), lanes] = m[0:1, :]
                lv_ref[pl.ds(row * dims + n, 1), lanes] = v[0:1, :]
        return carry

    lax.fori_loop(0, width // LANES, lane, 0)


def fourth_pass(rows, pg_ref, normed_ref, im_ref, iv_ref, near_ref, far_ref, keep_ref, flag_ref, al_ref, de_ref, be_ref, eta_ref, om_ref, n0_ref, n1_ref, x_ref, g_ref, direct_ref, gg_ref, qk_ref, xg_ref, sums_ref, dec_ref, drv_ref, ng_ref):
    rate_tables(al_ref, de_ref, be_ref, dec_ref, drv_ref)
    dims, width = al_ref.shape
    tokens = keep_ref.shape[0]
    length = tokens // rows
    steps = length // CHUNKS
    span = rows * dims
    sums_ref[...] = jnp.zeros_like(sums_ref)

    def lane(j, carry):
        lanes = pl.ds(pl.multiple_of(j * LANES, LANES), LANES)
        omega = bcast(om_ref, 0, lanes)
        for row in range(rows):
            base = j * tokens + row * length
            grad = steps_of(pg_ref, base, steps)
            token = steps_of(normed_ref, base, steps)
            kept = steps_of(keep_ref, row * length, steps)
            reach = shifted(product(kept), -1, 1.0)
            for by in (-1, -2, -4):
                reach = reach * shifted(reach, by, 1.0)
            place = lax.broadcasted_iota(jnp.int32, (CHUNKS, LANES), 0)
            later = (steps * (CHUNKS - 1 - place)).astype(F32)
            flag = bcast(flag_ref, row, pl.ds(0, LANES))
            total = [omega * t for t in grad]
            for n in range(dims):
                d, b, e = bcast(dec_ref, n, lanes), bcast(drv_ref, n, lanes), bcast(eta_ref, n, lanes)
                chunk = power(d, steps)
                inverse = 1.0 / d
                part = power(chunk, CHUNKS) * flag
                slope = (float(length) * part) * inverse
                at = row * dims + n
                m2 = bcast(far_ref, at, lanes)
                m_in = bcast(near_ref, at, lanes) + part * m2
                v_in = bcast(near_ref, span + at, lanes) + part * bcast(far_ref, span + at, lanes) + slope * m2
                through = reach * chunk_powers(chunk, -1)
                at = pl.ds(at * CHUNKS, CHUNKS)
                m = im_ref[at, lanes] + through * m_in
                v = iv_ref[at, lanes] + through * v_in + (later * through * inverse) * m_in
                coef = e * b
                sum_m = jnp.zeros((CHUNKS, LANES), F32)
                sum_v = jnp.zeros((CHUNKS, LANES), F32)
                for k in range(steps - 1, -1, -1):
                    mu = grad[k] + m
                    sum_m = sum_m + token[k] * mu
                    sum_v = sum_v + token[k] * v
                    total[k] = total[k] + coef * mu
                    rate = kept[k] * d
                    m = rate * mu
                    v = kept[k] * mu + rate * v
                sums_ref[pl.ds(n, 1), lanes] += jnp.sum(sum_m, 0, keepdims=True)
                sums_ref[pl.ds(dims + n, 1), lanes] += jnp.sum(sum_v, 0, keepdims=True)
            for k in range(steps):
                ng_ref[pl.ds(base + k, CHUNKS, stride=steps), :] = total[k]
        return carry

    lax.fori_loop(0, width // LANES, lane, 0)
    normed_grad = from_slabs(ng_ref[...], tokens) + n0_ref[...] + n1_ref[...]
    hat, scale = norm_parts(x_ref[...].astype(F32))
    at = 2 * dims
    for j in range(width // LANES):
        slab = slice(j * tokens, (j + 1) * tokens)
        sums_ref[at : at + 1, j * LANES : (j + 1) * LANES] = jnp.sum(
            pg_ref[slab, :] * normed_ref[slab, :], 0, keepdims=True
        )
    sums_ref[at + 1 : at + 2, :] = jnp.sum(normed_grad * hat, 0, keepdims=True)
    sums_ref[at + 2 : at + 3, :] = gg_ref[...]
    zd = qk_ref.shape[1]
    for i in range(3):
        sums_ref[at + 3 : at + 4, i * zd : (i + 1) * zd] = qk_ref[i : i + 1, :]
    xg_ref[...] = (direct_ref[...] + norm_back(normed_grad * g_ref[...], hat, scale)).astype(LOW)


def swap(x, axis, bit):
    size = lax.axis_size(axis)
    return lax.ppermute(x, axis, [(i, i ^ bit) for i in range(size)])


def shift(x, by):
    size = lax.axis_size("tensor")
    return lax.ppermute(
        x, "tensor", [(i, i + by) for i in range(size) if 0 <= i + by < size]
    )


def pick(first, pair):
    return jnp.where(first, *pair)


def split_rows(v):
    half = v.shape[0] // 2
    return v[:half], v[half:]


def joined(mine, other, first):
    return pick(
        first, (jnp.concatenate([mine, other], 0), jnp.concatenate([other, mine], 0))
    )


tied = lax.optimization_barrier


def rounded(v):
    return lax.reduce_precision(v, 8, 7)


def halves(v, first):
    low, high = split_rows(v)
    return pick(first, (low, high)), pick(first, (high, low)).astype(LOW)


def reduction(kind, near, far, firsts):
    bits = [1 << b for b in range(lax.axis_size("dp").bit_length() - 1)]
    lead = {"x": [1], "z": [2]}.get(kind, [])
    spread = {"x": [2], "z": [1], "y": [1, 2], "w": [2, 1]}[kind]
    near, far = near(), far()
    for bit in lead:
        near, away = halves(near, firsts[bit])
        far, far_away = halves(far, firsts[bit])
        got = yield "dp", bit, jnp.concatenate([away, far_away], 0)
        got = got.astype(F32)
        near, far = near + got[: near.shape[0]], far + got[near.shape[0] :]
    got = yield "tensor", 2, far.astype(LOW)
    total = near + got.astype(F32)
    for bit in spread:
        total, away = halves(total, firsts[bit])
        got = yield "dp", bit, away
        total = total + got.astype(F32)
    for bit in bits[2:]:
        total = rounded(total)
        got = yield "dp", bit, total.astype(LOW)
        total = total + got.astype(F32)
    low = total.astype(LOW)
    for bit in reversed(lead + spread):
        got = yield "dp", bit, low
        low = joined(low, got, firsts[bit])
    return low


def one_swap(axis, bit, v):
    got = yield axis, bit, v
    return got


def everywhere(v, kind):
    for axis in ("tensor", "dp"):
        for b in range(lax.axis_size(axis).bit_length() - 1):
            v = lax.reduce_precision(v, 8, 7) if kind == LOW else v
            got = yield axis, 1 << b, v.astype(kind)
            v = v + got.astype(F32)
    return v


class Pump:
    def __init__(self, token):
        self.token = token
        self.flows, self.ready, self.flying, self.done = {}, {}, {}, {}

    def gate(self, v):
        v, self.token = tied((v, self.token))
        return v

    def add(self, name, flow):
        self.flows[name] = flow
        self.ready[name] = next(flow)

    def issue(self, name):
        axis, bit, v = self.ready.pop(name)
        self.flying[name] = swap(self.gate(v), axis, bit)

    def finish(self, name):
        got = self.gate(self.flying.pop(name))
        try:
            self.ready[name] = self.flows[name].send(got)
        except StopIteration as end:
            self.done[name] = end.value

    def drain(self):
        while self.ready or self.flying:
            for name in list(self.ready):
                self.issue(name)
            for name in list(self.flying):
                self.finish(name)


def side_by_side(pack):
    half = pack.shape[0] // 2
    return jnp.concatenate([pack[:half], pack[half:]], 1)


def shards(
    layer_input,
    doc_lengths,
    norm1_gain,
    alpha_raw,
    delta_raw,
    ema_beta,
    ema_eta,
    ema_omega,
    w_z,
    q_gain,
    q_bias,
    k_gain,
    w_value,
    w_reset,
    w_update,
    w_hidden,
    w_out,
    norm2_gain,
    w_ffn_in,
    w_ffn_out,
    cotangent,
):
    member = lax.axis_index("tensor")
    place = lax.axis_index("dp")
    layer_input, begin, offs, *firsts = tied(
        (
            layer_input,
            member * layer_input.shape[1],
            (member ^ jnp.arange(4, dtype=jnp.int32)) * w_hidden.shape[0],
            (place & 1) == 0,
            (place & 2) == 0,
            (member & 1) == 0,
            (member & 2) == 0,
        )
    )
    first_core, first_chip = firsts[2:]
    firsts = dict(zip((1, 2), firsts[:2], strict=True))
    rows, length, width = layer_input.shape
    tokens = rows * length
    dims = alpha_raw.shape[0]
    zd = w_z.shape[1]
    units = w_value.shape[1]
    cols = w_hidden.shape[0]
    x = layer_input.reshape(tokens, width)
    cot = cotangent.reshape(tokens, width)
    g1, g2, om = norm1_gain[None], norm2_gain[None], ema_omega[None]
    qg, qb, kg = q_gain[None], q_bias[None], k_gain[None]

    docs = doc_lengths.shape[1]
    order = jnp.arange(docs)
    ends = jnp.sum(
        jnp.where(order[:, None] <= order[None, :], doc_lengths[:, :, None], 0), 1
    ).astype(jnp.int32)
    starts = ends - doc_lengths
    starts, ends = starts - begin, ends - begin
    places = jnp.arange(length, dtype=jnp.int32)
    docid = jnp.sum((places[None, :, None] >= ends[:, None, :]).astype(jnp.int32), 2)
    keep = 1.0 - jnp.any(places[None, :, None] == starts[:, None, :], 2).astype(F32)
    keep = jnp.broadcast_to(keep.reshape(tokens, 1), (tokens, LANES))
    blocks = docid.reshape(tokens // STRETCH, STRETCH)
    spot = jnp.arange(STRETCH)
    mask = (spot[None, :] <= spot[:, None])[None] & (blocks[:, :, None] == blocks[:, None, :])
    mask = mask.astype(F32).reshape(tokens, STRETCH)

    def unbroken(part):
        low, high = part * length, (part + 1) * length
        inside = jnp.any((starts >= low) & (starts < high), 1)
        return jnp.broadcast_to(1.0 - inside.astype(F32)[:, None], (rows, LANES))

    vm = lambda shape: pltpu.VMEM(shape, F32)
    tab = (dims, width)
    wide = (tokens, width)
    mat = 2.0 * tokens * width
    ema = 8.0 * tokens * width * dims
    chunked = (rows * dims * CHUNKS, width)
    finals = (rows * dims, width)
    slabs = (tokens * width // LANES, LANES)

    w_join = jnp.concatenate([w_hidden, w_out], 0)
    shares = (w_value, w_reset, w_join, w_ffn_in, w_ffn_out)
    bits = (1, 1, 2, 1, 1)
    pump = Pump(offs)
    beside = [swap(w_value, "tensor", 1), swap(w_reset, "tensor", 1)]
    half_v, half_r, half_g, half_i, half_o = (
        pick(firsts[bit], split_rows(w)) for w, bit in zip(shares, bits, strict=True)
    )

    over_v = swap(half_v, "tensor", 2)

    normed, normed_low, init, last = call(
        functools.partial(first_pass, rows),
        [(slabs, F32), (wide, LOW), (chunked, F32), (finals, F32)],
        (x, g1, alpha_raw, delta_raw, ema_beta, keep),
        ema,
        [vm(tab), vm(tab)],
    )
    f1, f2 = shift(last, 1), shift(last, 2)
    f1, f2 = pump.gate(f1), pump.gate(f2)
    beside = [pump.gate(w) for w in beside]
    over_r = swap(pump.gate(half_r), "tensor", 2)
    beside += [swap(pump.gate(w), "tensor", 1) for w in (w_ffn_in, w_ffn_out)]
    pre, mixed_low, z_pre, gate, probs = call(
        functools.partial(second_pass, rows),
        [(slabs, F32), (wide, LOW), ((tokens, zd), F32), (wide, F32), ((tokens, STRETCH), F32)],
        (normed, init, f1, f2, keep, unbroken(-1), alpha_raw, delta_raw, ema_beta,
         ema_eta, om, w_z, w_update, qg, qb, kg, mask),
        ema + mat * width,
        [vm(tab), vm(tab)],
    )
    split = (2, tokens, units)
    mixed_low = pump.gate(mixed_low)
    over_v = pump.gate(over_v)
    other_v = swap(over_v, "dp", 1)
    over_g = swap(pump.gate(half_g), "tensor", 2)
    beside = [pump.gate(w) for w in beside]
    mixed_low = pump.gate(mixed_low)

    def values(weights):
        return call(
            value_part,
            [(split, F32), (split, F32), (split, F32), (split, LOW)],
            (normed_low, mixed_low, probs, *weights),
            4 * mat * units,
        )

    own_part = values((w_value, w_reset, beside[0], beside[1]))
    united0 = pump.gate(own_part[3])
    over_r = pump.gate(over_r)
    other_r = swap(over_r, "dp", 1)
    over_i = swap(pump.gate(half_i), "tensor", 2)
    other_v = pump.gate(other_v)
    full_v = pump.gate(joined(over_v, other_v, firsts[1]))
    both_v = swap(full_v, "tensor", 1)
    over_g = pump.gate(over_g)
    other_g = swap(over_g, "dp", 2)
    over_o = swap(pump.gate(half_o), "tensor", 2)
    other_r = pump.gate(other_r)
    full_r = pump.gate(joined(over_r, other_r, firsts[1]))
    both_r = swap(full_r, "tensor", 1)
    both_v, both_r = pump.gate(both_v), pump.gate(both_r)
    over_i = pump.gate(over_i)
    full_v = pump.gate(full_v)
    far_part = values((full_v, full_r, both_v, both_r))
    united1 = pump.gate(far_part[3])
    other_i = swap(over_i, "dp", 1)
    over_o = pump.gate(over_o)
    other_o = swap(over_o, "dp", 1)
    other_g = pump.gate(other_g)
    near_g = pump.gate(jnp.stack([w_join, joined(over_g, other_g, firsts[2])]))
    beside_g = swap(near_g, "tensor", 1)
    other_i = pump.gate(other_i)
    full_i = pump.gate(joined(over_i, other_i, firsts[1]))
    both_i = swap(full_i, "tensor", 1)
    beside_g = pump.gate(beside_g)
    wg = (near_g, beside_g)
    wv, wr = (w_value, beside[0], full_v, both_v), (w_reset, beside[1], full_r, both_r)
    kept_parts = ((*own_part[:3], united0), (*far_part[:3], united1))
    hidden_pre, blended, second, whid = call(
        blend_part,
        [(wide, F32), (wide, F32), (wide, LOW), ((width, width), LOW)],
        (offs, x, mixed_low, gate, united0, united1, *wg, g2),
        mat * (width + 4 * units),
        smem=(0,),
    )
    second = pump.gate(second)
    ffn_rows = width + 2 * units

    def ffn_of(weights):
        return call(
            ffn_part,
            [(wide, F32), (wide, F32), ((ffn_rows, units), F32), ((ffn_rows, units), LOW)],
            (second, cot, *weights),
            12 * mat * units,
        )

    ffn0 = ffn_of((w_ffn_in, beside[2], w_ffn_out, beside[3]))
    back0 = pump.gate(ffn0[1])
    other_o = pump.gate(other_o)
    full_o = pump.gate(joined(over_o, other_o, firsts[1]))
    both_o = swap(full_o, "tensor", 1)
    both_i, both_o = pump.gate(both_i), pump.gate(both_o)
    ffn1 = ffn_of((full_i, both_i, full_o, both_o))
    pump.add("F0", one_swap("tensor", 1, ffn0[3]))
    pump.add("F1", one_swap("tensor", 1, ffn1[3]))
    own = (2, 4 * cols, width // 2)
    pack_rows = 2 * width + 2 * units
    held = {}

    def run_blend():
        held["bb"] = call(
            blend_back,
            [(wide, LOW), (wide, F32), (wide, LOW), (wide, F32), ((1, width), F32), (own, F32), (own, LOW)],
            (offs, x, cot, pump.gate(blended), ffn1[1], back0, ffn0[0], ffn1[0], hidden_pre, gate,
             mixed_low, g2, w_update, whid),
            4 * mat * width,
            [vm((width, width))],
            smem=(0,),
        )
        held["hidden"] = pump.gate(held["bb"][2])
        pump.add("P0", one_swap("tensor", 1, held["bb"][6]))

    def run_values(p):
        held[p] = [*call(
            functools.partial(value_back, p),
            [(wide, F32), (wide, F32), ((tokens, STRETCH), F32), ((pack_rows, units), F32), ((pack_rows, units), LOW)],
            (pump.gate(held["hidden"]), normed_low, mixed_low, probs, *kept_parts[p], *wg,
             wv[2 * p], wr[2 * p], wv[2 * p + 1], wr[2 * p + 1]),
            14 * mat * units,
        )]
        pump.token, held[p][2] = tied((pump.token, held[p][2]))
        pump.add(f"V{p}", one_swap("tensor", 1, held[p][4]))

    def run_third():
        held["t3"] = call(
            functools.partial(third_pass, rows),
            [(slabs, F32), ((width, zd), F32), ((8, zd), F32), (chunked, F32), (chunked, F32), (finals, F32), (finals, F32)],
            (pump.gate(z_pre), probs, held[0][2], held[1][2], qg, qb, kg, w_z, mixed_low, held["bb"][3],
             held[0][1], held[1][1], pre, keep, alpha_raw, delta_raw),
            2 * ema,
            [vm((2, tokens, zd))],
        )
        pump.add("dz", everywhere(held["t3"][1], LOW))

    def send_back():
        back = pump.gate(jnp.concatenate([held["t3"][5], held["t3"][6]], 0))
        held["back"] = shift(back, -1), shift(back, -2)

    def take_back():
        held["back"] = [pump.gate(v) for v in held["back"]]

    def run_fourth():
        t3 = held["t3"]
        held["t4"] = call(
            functools.partial(fourth_pass, rows),
            [(wide, LOW), ((2 * dims + 8, width), F32)],
            (t3[0], normed, t3[3], t3[4], *held["back"], keep, unbroken(1), alpha_raw,
             delta_raw, ema_beta, ema_eta, om, held[0][0], held[1][0], x, g1, held["bb"][1],
             held["bb"][4], t3[2]),
            2 * ema,
            [vm(tab), vm(tab), vm(slabs)],
        )
        pump.add("sm", everywhere(pump.gate(held["t4"][1]), F32))

    def pack(p, source, at, end):
        kept = (ffn0, ffn1)[p][2] if source == "F" else held[p][3]
        return kept[at:end] + pump.done[f"{source}{p}"][at:end].astype(F32)

    def add_flow(name):
        if name == "P":
            kept, got = held["bb"][5], pump.done["P0"].astype(F32)
            near, far = (lambda: kept[0] + got[0]), (lambda: kept[1] + got[1])
        else:
            source = "F" if name == "F" else "V"
            at, end = {"F": (0, 2 * width), "R": (0, width), "O": (width, 2 * width), "N": (2 * width, 3 * width)}[name]
            near, far = (lambda: pack(0, source, at, end)), (lambda: pack(1, source, at, end))
        pump.add(name, reduction(KINDS[name], near, far, firsts))

    kernels = {
        "bb": run_blend,
        "v1": lambda: run_values(1),
        "v0": lambda: run_values(0),
        "t3": run_third,
        "t4": run_fourth,
    }
    for word in ORDER:
        sign, name = word[0], word[1:]
        if sign == "K":
            kernels[name]()
        elif name == "E":
            (send_back if sign == "+" else take_back)()
        elif sign == "+":
            if name in KINDS and name not in pump.flows:
                add_flow(name)
            pump.issue(name)
        else:
            pump.finish(name)
    pump.drain()
    output, input_grad = held["bb"][0], held["t4"][0]
    sums, dz_sum, pair_sum, ffn_sum = (pump.done[n] for n in ("sm", "dz", "P", "F"))
    reset_sum, out_sum, value_sum = (pump.done[n] for n in "RON")

    alpha, sigma = jax.nn.sigmoid(alpha_raw), jax.nn.sigmoid(delta_raw)
    with_mu, with_nu = sums[:dims], sums[dims : 2 * dims]
    drive_grad = ema_eta * with_mu
    decay_grad = ema_eta * (alpha * ema_beta) * with_nu
    at = 2 * dims
    quarter = side_by_side(pair_sum[: 2 * cols])
    update_grad = joined(quarter, swap(quarter, "tensor", 1), first_core)
    update_grad = joined(update_grad, swap(update_grad, "tensor", 2), first_chip)
    return (
        output.reshape(layer_input.shape),
        input_grad.reshape(layer_input.shape),
        sums[at + 1],
        (ema_beta * drive_grad - sigma * decay_grad) * alpha * (1.0 - alpha),
        -alpha * decay_grad * sigma * (1.0 - sigma),
        alpha * drive_grad,
        (alpha * ema_beta) * with_mu,
        sums[at],
        dz_sum,
        sums[at + 3, :zd],
        sums[at + 3, zd : 2 * zd],
        sums[at + 3, 2 * zd : 3 * zd],
        value_sum.astype(F32),
        reset_sum.astype(F32),
        update_grad.astype(F32),
        side_by_side(pair_sum[2 * cols :]).astype(F32),
        side_by_side(out_sum).astype(F32),
        sums[at + 2],
        ffn_sum[:width].astype(F32),
        side_by_side(ffn_sum[width:]).astype(F32),
    )


def solution(mesh):
    whole, by_row = P(), P("dp", "tensor", None)
    by_col, by_unit = P(None, "tensor"), P("tensor", None)
    return jax.shard_map(
        shards,
        mesh=mesh,
        in_specs=(by_row, P("dp", None), *(whole,) * 10, by_col, by_col, whole, by_unit, by_unit, whole, by_col, by_unit, by_row),
        out_specs=(by_row, by_row, *(whole,) * 10, by_col, by_col, whole, by_unit, by_unit, whole, by_col, by_unit),
        check_vma=False,
    )
```

```python
import functools

import jax
import jax.numpy as jnp
from jax import lax
from jax.experimental import pallas as pl
from jax.experimental.pallas import tpu as pltpu
from jax.sharding import PartitionSpec as P

STRETCH = 128
LANES = 128
CHUNKS = 8
F32 = jnp.float32
LOW = jnp.bfloat16
KINDS = {"I": "x", "U": "y", "P": "y", "R": "x", "O": "x", "N": "z"}
ORDER = (
    "+F0", "+F1", "-F0", "-F1", "+I", "+U", "Kback", "-I", "-U", "+R",
    "+O", "+E", "+P", "-R", "+U", "-O", "+N", "-P", "+I", "-N",
    "+R", "-E", "+N", "+P", "-U", "Kt4", "-I", "+O", "+I", "-R",
    "+sm", "-N", "+R", "-sm", "+U", "-P", "-I", "+I", "+N", "-U",
    "+P", "-R", "+U", "-O", "+R", "-I", "+O", "-N", "+I", "-P",
    "+N", "-R", "+P", "-U", "+R", "-I", "+sm", "-O", "-N", "+O",
    "-P", "+I", "+P", "-O", "+U", "-R", "-sm", "+R", "+sm", "-I",
    "+O", "-U", "-P", "+P", "-R", "+U", "+N", "-sm", "+sm", "-P",
    "+R", "-O", "-U", "+O", "+P", "-N", "-sm", "-R", "+sm", "+N",
    "-O", "+O", "-P", "-N", "+N", "-O", "-sm", "-N",
)


def silu(v):
    return v * jax.nn.sigmoid(v)


def silu_slope(v):
    s = jax.nn.sigmoid(v)
    return s * (1.0 + v * (1.0 - s))


def dot(a, b):
    return jnp.dot(a, b, preferred_element_type=F32)


def dot_rows(a, b):
    return lax.dot_general(a, b, (((0,), (0,)), ((), ())), preferred_element_type=F32)


def dot_cols(a, b):
    return lax.dot_general(a, b, (((1,), (1,)), ((), ())), preferred_element_type=F32)


def norm_parts(v):
    center = v - jnp.mean(v, -1, keepdims=True)
    scale = lax.rsqrt(jnp.mean(center * center, -1, keepdims=True) + 1e-05)
    return center * scale, scale


def norm_back(grad, hat, scale):
    return scale * (
        grad - jnp.mean(grad, -1, keepdims=True) - hat * jnp.mean(grad * hat, -1, keepdims=True)
    )


def call(kernel, outs, args, flops, scratch=(), smem=(), limit=12 << 20):
    specs = [
        pl.BlockSpec(memory_space=pltpu.SMEM if i in smem else pltpu.VMEM)
        for i in range(len(args))
    ]
    outs = [jax.ShapeDtypeStruct(s, d) for s, d in outs]
    size = sum(a.size * a.dtype.itemsize for a in args) + sum(
        o.size * o.dtype.itemsize for o in outs
    )
    return pl.pallas_call(
        kernel,
        out_shape=outs,
        in_specs=specs,
        out_specs=[pl.BlockSpec(memory_space=pltpu.VMEM) for _ in outs],
        scratch_shapes=list(scratch),
        compiler_params=pltpu.CompilerParams(vmem_limit_bytes=limit),
        cost_estimate=pl.CostEstimate(flops=int(flops), bytes_accessed=int(size), transcendentals=0),
    )(*args)


def bcast(ref, row, lanes):
    return jnp.broadcast_to(ref[pl.ds(row, 1), lanes], (CHUNKS, LANES))


def shifted(v, by, fill):
    place = lax.broadcasted_iota(jnp.int32, v.shape, 0)
    if by > 0:
        return jnp.where(place >= by, pltpu.roll(v, by, 0), fill)
    return jnp.where(place < CHUNKS + by, pltpu.roll(v, CHUNKS + by, 0), fill)


def power(v, n):
    out = None
    while n:
        if n & 1:
            out = v if out is None else out * v
        n >>= 1
        if n:
            v = v * v
    return out


def chunk_powers(base, order):
    place = lax.broadcasted_iota(jnp.int32, base.shape, 0)
    place = place if order > 0 else (CHUNKS - 1) - place
    out = jnp.where(place & 1 == 1, base, 1.0)
    base = base * base
    out = out * jnp.where(place & 2 == 2, base, 1.0)
    base = base * base
    return out * jnp.where(place & 4 == 4, base, 1.0)


def rate_tables(al_ref, de_ref, be_ref, dec_ref, drv_ref):
    alpha = jax.nn.sigmoid(al_ref[...])
    dec_ref[...] = 1.0 - alpha * jax.nn.sigmoid(de_ref[...])
    drv_ref[...] = alpha * be_ref[...]


def steps_of(ref, base, steps):
    return [ref[pl.ds(base + k, CHUNKS, stride=steps), :] for k in range(steps)]


def into_slabs(ref, v):
    tokens = v.shape[0]
    for j in range(v.shape[1] // LANES):
        ref[j * tokens : (j + 1) * tokens, :] = v[:, j * LANES : (j + 1) * LANES]


def from_slabs(v, tokens):
    return jnp.concatenate(
        [v[at : at + tokens] for at in range(0, v.shape[0], tokens)], 1
    )


def product(values):
    out = values[0]
    for v in values[1:]:
        out = out * v
    return out


def first_pass(rows, x_ref, g_ref, al_ref, de_ref, be_ref, keep_ref, normed_ref, low_ref, init_ref, last_ref, dec_ref, drv_ref):
    hat, _ = norm_parts(x_ref[...].astype(F32))
    normed = hat * g_ref[...]
    into_slabs(normed_ref, normed)
    low_ref[...] = normed.astype(LOW)
    rate_tables(al_ref, de_ref, be_ref, dec_ref, drv_ref)
    dims, width = al_ref.shape
    tokens = x_ref.shape[0]
    length = tokens // rows
    steps = length // CHUNKS

    def lane(j, carry):
        lanes = pl.ds(pl.multiple_of(j * LANES, LANES), LANES)
        for row in range(rows):
            token = steps_of(normed_ref, j * tokens + row * length, steps)
            kept = steps_of(keep_ref, row * length, steps)
            whole = product(kept)
            for n in range(dims):
                d, b = bcast(dec_ref, n, lanes), bcast(drv_ref, n, lanes)
                s = b * token[0]
                for k in range(1, steps):
                    s = (kept[k] * d) * s + b * token[k]
                a = power(d, steps) * whole
                for by in (1, 2, 4):
                    s = s + a * shifted(s, by, 0.0)
                    a = a * shifted(a, by, 1.0)
                init_ref[pl.ds((row * dims + n) * CHUNKS, CHUNKS), lanes] = shifted(s, 1, 0.0)
                last_ref[pl.ds(row * dims + n, 1), lanes] = s[CHUNKS - 1 :, :]
        return carry

    lax.fori_loop(0, width // LANES, lane, 0)


def second_pass(rows, normed_ref, init_ref, f1_ref, f2_ref, keep_ref, flag_ref, al_ref, de_ref, be_ref, eta_ref, om_ref, wz_ref, wu_ref, qg_ref, qb_ref, kg_ref, mask_ref, pre_ref, mixed_ref, zpre_ref, gate_ref, probs_ref, dec_ref, drv_ref):
    rate_tables(al_ref, de_ref, be_ref, dec_ref, drv_ref)
    dims, width = al_ref.shape
    tokens = keep_ref.shape[0]
    length = tokens // rows
    steps = length // CHUNKS

    def lane(j, carry):
        lanes = pl.ds(pl.multiple_of(j * LANES, LANES), LANES)
        omega = bcast(om_ref, 0, lanes)
        for row in range(rows):
            base = j * tokens + row * length
            token = steps_of(normed_ref, base, steps)
            kept = steps_of(keep_ref, row * length, steps)
            reach = shifted(product(kept), 1, 1.0)
            for by in (1, 2, 4):
                reach = reach * shifted(reach, by, 1.0)
            flag = bcast(flag_ref, row, pl.ds(0, LANES))
            total = [omega * t for t in token]
            for n in range(dims):
                d, b, e = bcast(dec_ref, n, lanes), bcast(drv_ref, n, lanes), bcast(eta_ref, n, lanes)
                chunk = power(d, steps)
                entering = bcast(f1_ref, row * dims + n, lanes) + (
                    power(chunk, CHUNKS) * flag
                ) * bcast(f2_ref, row * dims + n, lanes)
                s = (
                    init_ref[pl.ds((row * dims + n) * CHUNKS, CHUNKS), lanes]
                    + reach * chunk_powers(chunk, 1) * entering
                )
                for k in range(steps):
                    s = (kept[k] * d) * s + b * token[k]
                    total[k] = total[k] + e * s
            for k in range(steps):
                pre_ref[pl.ds(base + k, CHUNKS, stride=steps), :] = total[k]
        return carry

    lax.fori_loop(0, width // LANES, lane, 0)
    mixed_low = from_slabs(silu(pre_ref[...]).astype(LOW), tokens)
    mixed_ref[...] = mixed_low
    z_pre = dot(mixed_low, wz_ref[...])
    zpre_ref[...] = z_pre
    gate_ref[...] = jax.nn.sigmoid(dot(mixed_low, wu_ref[...]))
    z_low = silu(z_pre).astype(LOW).astype(F32)
    queries = (z_low * qg_ref[...] + qb_ref[...]).astype(LOW)
    keys = (z_low * kg_ref[...]).astype(LOW)
    for start in range(0, z_low.shape[0], STRETCH):
        block = slice(start, start + STRETCH)
        scores = dot_cols(queries[block], keys[block]) * z_low.shape[1] ** (-0.5)
        scores = jnp.where(mask_ref[block, :] > 0.5, scores, -1e30)
        shift = jnp.exp(scores - jnp.max(scores, -1, keepdims=True))
        probs_ref[block, :] = shift / jnp.sum(shift, -1, keepdims=True)


def value_part(normed_ref, mixed_ref, probs_ref, va_ref, ra_ref, vb_ref, rb_ref, vpre_ref, rpre_ref, att_ref, united_ref):
    tokens = normed_ref.shape[0]
    for i, (v_ref, r_ref) in enumerate(((va_ref, ra_ref), (vb_ref, rb_ref))):
        value_pre = dot(normed_ref[...], v_ref[...])
        reset_pre = dot(mixed_ref[...], r_ref[...])
        vpre_ref[i] = value_pre
        rpre_ref[i] = reset_pre
        values = silu(value_pre).astype(LOW)
        for start in range(0, tokens, STRETCH):
            block = slice(start, start + STRETCH)
            att_ref[i, block, :] = dot(probs_ref[block, :].astype(LOW), values[block])
        united_ref[i] = (silu(reset_pre) * att_ref[i]).astype(LOW)


def blend_part(offs_ref, x_ref, mixed_ref, gate_ref, u0_ref, u1_ref, ga_ref, gb_ref, gain_ref, hpre_ref, blended_ref, second_ref, whid_ref):
    cols = whid_ref.shape[0] // 4
    for r in range(4):
        whid_ref[pl.ds(pl.multiple_of(offs_ref[r], 64), cols), :] = (ga_ref, gb_ref)[r % 2][r // 2, :cols, :]
    hidden_pre = dot(mixed_ref[...], whid_ref[...])
    for r in range(4):
        united = (u0_ref, u1_ref)[r // 2][r % 2]
        hidden_pre = hidden_pre + dot(united, (ga_ref, gb_ref)[r % 2][r // 2, cols:, :])
    hpre_ref[...] = hidden_pre
    x = x_ref[...].astype(F32)
    blended = x + gate_ref[...] * (silu(hidden_pre) - x)
    blended_ref[...] = blended
    hat, _ = norm_parts(blended)
    second_ref[...] = (hat * gain_ref[...]).astype(LOW)


def ffn_part(second_ref, cot_ref, ia_ref, ib_ref, oa_ref, ob_ref, out_ref, sg_ref, keep_ref, send_ref):
    second, cot = second_ref[...], cot_ref[...]
    depth, units = ia_ref.shape
    half = depth // 2
    for i, (in_ref, fo_ref, pack_ref) in enumerate(
        ((ia_ref, oa_ref, keep_ref), (ib_ref, ob_ref, send_ref))
    ):
        up_pre = dot(second, in_ref[...])
        activated = silu(up_pre).astype(LOW)
        up_grad = (dot_cols(cot, fo_ref[...]) * silu_slope(up_pre)).astype(LOW)
        out = dot(activated, fo_ref[...])
        back = dot_cols(up_grad, in_ref[...])
        out_ref[...] = out if i == 0 else out_ref[...] + out
        sg_ref[...] = back if i == 0 else sg_ref[...] + back
        kind = pack_ref.dtype
        pack_ref[:depth, :] = dot_rows(second, up_grad).astype(kind)
        for h in range(2):
            pack_ref[depth + h * units : depth + (h + 1) * units, :] = dot_rows(
                activated, cot[:, h * half : (h + 1) * half]
            ).astype(kind)


def blend_back(offs_ref, x_ref, cot_ref, blended_ref, s0_ref, s1_ref, o0_ref, o1_ref, hpre_ref, gate_ref, mixed_ref, gain_ref, wu_ref, whid_ref, y_ref, direct_ref, hidden_ref, mg_ref, gg_ref, keep_ref, send_ref, full_ref):
    blended = blended_ref[...]
    y_ref[...] = (blended + (o0_ref[...] + o1_ref[...])).astype(LOW)
    second_grad = s0_ref[...] + s1_ref[...]
    hat, scale = norm_parts(blended)
    gg_ref[...] = jnp.sum(second_grad * hat, 0, keepdims=True)
    grad = cot_ref[...].astype(F32) + norm_back(second_grad * gain_ref[...], hat, scale)
    gate, hidden_pre, x = gate_ref[...], hpre_ref[...], x_ref[...].astype(F32)
    direct_ref[...] = grad * (1.0 - gate)
    hidden_low = (grad * gate * silu_slope(hidden_pre)).astype(LOW)
    gate_low = (grad * (silu(hidden_pre) - x) * gate * (1.0 - gate)).astype(LOW)
    hidden_ref[...] = hidden_low
    mg_ref[...] = dot_cols(gate_low, wu_ref[...]) + dot_cols(hidden_low, whid_ref[...])
    width = x.shape[1]
    cols, half = width // 4, width // 2
    for i, low in enumerate((gate_low, hidden_low)):
        full_ref[...] = dot_rows(mixed_ref[...], low)
        for r in range(4):
            pack_ref = (keep_ref, send_ref)[r % 2]
            rows = pl.ds(pl.multiple_of(offs_ref[r], 64), cols)
            for h in range(2):
                at = (2 * i + h) * cols
                pack_ref[r // 2, at : at + cols, :] = full_ref[
                    rows, h * half : (h + 1) * half
                ].astype(pack_ref.dtype)


def value_back(part, hidden_ref, normed_ref, mixed_ref, probs_ref, vpre_ref, rpre_ref, att_ref, united_ref, ga_ref, gb_ref, va_ref, ra_ref, vb_ref, rb_ref, ng_ref, mg_ref, pg_ref, *packs):
    hidden, normed, mixed = hidden_ref[...], normed_ref[...], mixed_ref[...]
    tokens, depth = hidden.shape
    units = va_ref.shape[1]
    cols = ga_ref.shape[1] - units
    half = depth // 2
    for i, (g_ref, v_ref, r_ref, pack) in enumerate(
        ((ga_ref, va_ref, ra_ref, packs[:3]), (gb_ref, vb_ref, rb_ref, packs[3:]))
    ):
        reset_pack, out_pack, value_pack = pack
        kind = reset_pack.dtype
        united_grad = dot_cols(hidden, g_ref[part, cols:, :])
        reset_pre, value_pre = rpre_ref[i], vpre_ref[i]
        reset_low = (united_grad * att_ref[i] * silu_slope(reset_pre)).astype(LOW)
        attended_low = (united_grad * silu(reset_pre)).astype(LOW)
        values = silu(value_pre).astype(LOW)
        parts = []
        for start in range(0, tokens, STRETCH):
            block = slice(start, start + STRETCH)
            parts.append(dot_rows(probs_ref[block, :].astype(LOW), attended_low[block]))
            back = dot_cols(attended_low[block], values[block])
            first = i == 0 and part == 1
            pg_ref[block, :] = back if first else pg_ref[block, :] + back
        value_low = (jnp.concatenate(parts, 0) * silu_slope(value_pre)).astype(LOW)
        into_normed = dot_cols(value_low, v_ref[...])
        into_mixed = dot_cols(reset_low, r_ref[...])
        first = i == 0 and part == 1
        ng_ref[...] = into_normed if first else ng_ref[...] + into_normed
        mg_ref[...] = into_mixed if first else mg_ref[...] + into_mixed
        reset_pack[part] = dot_rows(mixed, reset_low).astype(kind)
        for h in range(2):
            out_pack[part, h * units : (h + 1) * units, :] = dot_rows(
                united_ref[i], hidden[:, h * half : (h + 1) * half]
            ).astype(kind)
        value_pack[part] = dot_rows(normed, value_low).astype(kind)


def third_pass(rows, zpre_ref, probs_ref, p_ref, qg_ref, qb_ref, kg_ref, wz_ref, mixed_ref, m0_ref, m1_ref, pre_ref, keep_ref, al_ref, de_ref, pg_ref, dz_ref, small_ref, im_ref, iv_ref, lm_ref, lv_ref, qk_ref):
    z_pre = zpre_ref[...]
    z_low = silu(z_pre).astype(LOW).astype(F32)
    queries = (z_low * qg_ref[...] + qb_ref[...]).astype(LOW)
    keys = (z_low * kg_ref[...]).astype(LOW)
    for start in range(0, z_low.shape[0], STRETCH):
        block = slice(start, start + STRETCH)
        probs = probs_ref[block, :]
        grad = p_ref[block, :]
        grad = probs * (grad - jnp.sum(probs * grad, -1, keepdims=True)) * z_low.shape[1] ** (-0.5)
        high = grad.astype(LOW)
        rest = (grad - high.astype(F32)).astype(LOW)
        qk_ref[0, block, :] = dot(high, keys[block]) + dot(rest, keys[block])
        qk_ref[1, block, :] = dot_rows(high, queries[block]) + dot_rows(rest, queries[block])
    query_grad, key_grad = qk_ref[0], qk_ref[1]
    small_ref[...] = jnp.zeros_like(small_ref)
    small_ref[0:1, :] = jnp.sum(query_grad * z_low, 0, keepdims=True)
    small_ref[1:2, :] = jnp.sum(query_grad, 0, keepdims=True)
    small_ref[2:3, :] = jnp.sum(key_grad * z_low, 0, keepdims=True)
    z_grad = ((query_grad * qg_ref[...] + key_grad * kg_ref[...]) * silu_slope(z_pre)).astype(LOW)
    dz_ref[...] = dot_rows(mixed_ref[...], z_grad)
    mixed_grad = m0_ref[...] + m1_ref[...] + dot_cols(z_grad, wz_ref[...])
    into_slabs(pg_ref, mixed_grad)
    pg_ref[...] = pg_ref[...] * silu_slope(pre_ref[...])
    dims, width = al_ref.shape
    tokens = z_pre.shape[0]
    length = tokens // rows
    steps = length // CHUNKS

    def lane(j, carry):
        lanes = pl.ds(pl.multiple_of(j * LANES, LANES), LANES)
        for row in range(rows):
            token = steps_of(pg_ref, j * tokens + row * length, steps)
            kept = steps_of(keep_ref, row * length, steps)
            whole = product(kept)
            for n in range(dims):
                alpha = jax.nn.sigmoid(bcast(al_ref, n, lanes))
                d = 1.0 - alpha * jax.nn.sigmoid(bcast(de_ref, n, lanes))
                mu = token[steps - 1]
                m = (kept[steps - 1] * d) * mu
                v = kept[steps - 1] * mu
                for k in range(steps - 2, -1, -1):
                    mu = token[k] + m
                    rate = kept[k] * d
                    m = rate * mu
                    v = kept[k] * mu + rate * v
                a = power(d, steps) * whole
                b = steps * power(d, steps - 1) * whole
                for by in (-1, -2, -4):
                    mp, vp = shifted(m, by, 0.0), shifted(v, by, 0.0)
                    ap, bp = shifted(a, by, 1.0), shifted(b, by, 0.0)
                    v = v + a * vp + b * mp
                    m = m + a * mp
                    b = a * bp + b * ap
                    a = a * ap
                at = pl.ds((row * dims + n) * CHUNKS, CHUNKS)
                im_ref[at, lanes] = shifted(m, -1, 0.0)
                iv_ref[at, lanes] = shifted(v, -1, 0.0)
                lm_ref[pl.ds(row * dims + n, 1), lanes] = m[0:1, :]
                lv_ref[pl.ds(row * dims + n, 1), lanes] = v[0:1, :]
        return carry

    lax.fori_loop(0, width // LANES, lane, 0)


def back_pass(rows, *refs):
    offs_ref, x_ref, cot_ref, blended_ref, s0_ref, s1_ref, o0_ref, o1_ref, hpre_ref, gate_ref = refs[:10]
    mixed_ref, gain_ref, wu_ref, whid_ref, normed_ref, probs_ref = refs[10:16]
    own_part, far_part, (ga_ref, gb_ref), weights = refs[16:20], refs[20:24], refs[24:26], refs[26:34]
    zpre_ref, qg_ref, qb_ref, kg_ref, wz_ref, pre_ref, keep_ref, al_ref, de_ref = refs[34:43]
    y_ref, direct_ref, gg_ref, pair_keep_ref, pair_send_ref, ng_ref = refs[43:49]
    packs, outs = refs[49:55], refs[55:62]
    mg_ref, p_ref, qk_ref, m0_ref, full_ref, hidden_ref = refs[62:]
    blend_back(
        offs_ref, x_ref, cot_ref, blended_ref, s0_ref, s1_ref, o0_ref, o1_ref, hpre_ref, gate_ref,
        mixed_ref, gain_ref, wu_ref, whid_ref, y_ref, direct_ref, hidden_ref, m0_ref, gg_ref,
        pair_keep_ref, pair_send_ref, full_ref,
    )
    for part, parts in ((1, far_part), (0, own_part)):
        value_back(
            part, hidden_ref, normed_ref, mixed_ref, probs_ref, *parts, ga_ref, gb_ref,
            *weights[4 * part : 4 * part + 4], ng_ref, mg_ref, p_ref, *packs,
        )
    third_pass(
        rows, zpre_ref, probs_ref, p_ref, qg_ref, qb_ref, kg_ref, wz_ref, mixed_ref, m0_ref,
        mg_ref, pre_ref, keep_ref, al_ref, de_ref, *outs, qk_ref,
    )


def fourth_pass(rows, pg_ref, normed_ref, im_ref, iv_ref, near_ref, far_ref, keep_ref, flag_ref, al_ref, de_ref, be_ref, eta_ref, om_ref, n0_ref, x_ref, g_ref, direct_ref, gg_ref, qk_ref, xg_ref, sums_ref, dec_ref, drv_ref, ng_ref):
    rate_tables(al_ref, de_ref, be_ref, dec_ref, drv_ref)
    dims, width = al_ref.shape
    tokens = keep_ref.shape[0]
    length = tokens // rows
    steps = length // CHUNKS
    span = rows * dims
    sums_ref[...] = jnp.zeros_like(sums_ref)

    def lane(j, carry):
        lanes = pl.ds(pl.multiple_of(j * LANES, LANES), LANES)
        omega = bcast(om_ref, 0, lanes)
        for row in range(rows):
            base = j * tokens + row * length
            grad = steps_of(pg_ref, base, steps)
            token = steps_of(normed_ref, base, steps)
            kept = steps_of(keep_ref, row * length, steps)
            reach = shifted(product(kept), -1, 1.0)
            for by in (-1, -2, -4):
                reach = reach * shifted(reach, by, 1.0)
            place = lax.broadcasted_iota(jnp.int32, (CHUNKS, LANES), 0)
            later = (steps * (CHUNKS - 1 - place)).astype(F32)
            flag = bcast(flag_ref, row, pl.ds(0, LANES))
            total = [omega * t for t in grad]
            for n in range(dims):
                d, b, e = bcast(dec_ref, n, lanes), bcast(drv_ref, n, lanes), bcast(eta_ref, n, lanes)
                chunk = power(d, steps)
                inverse = 1.0 / d
                part = power(chunk, CHUNKS) * flag
                slope = (float(length) * part) * inverse
                at = row * dims + n
                m2 = bcast(far_ref, at, lanes)
                m_in = bcast(near_ref, at, lanes) + part * m2
                v_in = bcast(near_ref, span + at, lanes) + part * bcast(far_ref, span + at, lanes) + slope * m2
                through = reach * chunk_powers(chunk, -1)
                at = pl.ds(at * CHUNKS, CHUNKS)
                m = im_ref[at, lanes] + through * m_in
                v = iv_ref[at, lanes] + through * v_in + (later * through * inverse) * m_in
                coef = e * b
                sum_m = jnp.zeros((CHUNKS, LANES), F32)
                sum_v = jnp.zeros((CHUNKS, LANES), F32)
                for k in range(steps - 1, -1, -1):
                    mu = grad[k] + m
                    sum_m = sum_m + token[k] * mu
                    sum_v = sum_v + token[k] * v
                    total[k] = total[k] + coef * mu
                    rate = kept[k] * d
                    m = rate * mu
                    v = kept[k] * mu + rate * v
                sums_ref[pl.ds(n, 1), lanes] += jnp.sum(sum_m, 0, keepdims=True)
                sums_ref[pl.ds(dims + n, 1), lanes] += jnp.sum(sum_v, 0, keepdims=True)
            for k in range(steps):
                ng_ref[pl.ds(base + k, CHUNKS, stride=steps), :] = total[k]
        return carry

    lax.fori_loop(0, width // LANES, lane, 0)
    normed_grad = from_slabs(ng_ref[...], tokens) + n0_ref[...]
    hat, scale = norm_parts(x_ref[...].astype(F32))
    at = 2 * dims
    for j in range(width // LANES):
        slab = slice(j * tokens, (j + 1) * tokens)
        sums_ref[at : at + 1, j * LANES : (j + 1) * LANES] = jnp.sum(
            pg_ref[slab, :] * normed_ref[slab, :], 0, keepdims=True
        )
    sums_ref[at + 1 : at + 2, :] = jnp.sum(normed_grad * hat, 0, keepdims=True)
    sums_ref[at + 2 : at + 3, :] = gg_ref[...]
    zd = qk_ref.shape[1]
    for i in range(3):
        sums_ref[at + 3 : at + 4, i * zd : (i + 1) * zd] = qk_ref[i : i + 1, :]
    xg_ref[...] = (direct_ref[...] + norm_back(normed_grad * g_ref[...], hat, scale)).astype(LOW)


def swap(x, axis, bit):
    size = lax.axis_size(axis)
    return lax.ppermute(x, axis, [(i, i ^ bit) for i in range(size)])


def shift(x, by):
    size = lax.axis_size("tensor")
    return lax.ppermute(
        x, "tensor", [(i, i + by) for i in range(size) if 0 <= i + by < size]
    )


def pick(first, pair):
    return jnp.where(first, *pair)


def split_rows(v):
    half = v.shape[0] // 2
    return v[:half], v[half:]


def joined(mine, other, first):
    return pick(
        first, (jnp.concatenate([mine, other], 0), jnp.concatenate([other, mine], 0))
    )


tied = lax.optimization_barrier


def rounded(v):
    return lax.reduce_precision(v, 8, 7)


def halves(v, first):
    low, high = split_rows(v)
    return pick(first, (low, high)), pick(first, (high, low)).astype(LOW)


def reduction(kind, packs, firsts):
    bits = [1 << b for b in range(lax.axis_size("dp").bit_length() - 1)]
    lead, spread, rest = {
        "x": ([1], [2], []),
        "z": ([2], [1], []),
        "y": ([], [1, 2], []),
        "w": ([], [2, 1], []),
        "X": ([1], [], [2]),
        "Z": ([2], [], [1]),
        "Y": ([], [1], [2]),
        "W": ([], [2], [1]),
    }[kind]
    near, far = yield from packs
    for bit in lead:
        near, away = halves(near, firsts[bit])
        far, far_away = halves(far, firsts[bit])
        got = yield "dp", bit, jnp.concatenate([away, far_away], 0)
        got = got.astype(F32)
        near, far = near + got[: near.shape[0]], far + got[near.shape[0] :]
    got = yield "tensor", 2, far.astype(LOW)
    total = near + got.astype(F32)
    for bit in spread:
        total, away = halves(total, firsts[bit])
        got = yield "dp", bit, away
        total = total + got.astype(F32)
    for bit in rest + bits[2:]:
        total = rounded(total)
        got = yield "dp", bit, total.astype(LOW)
        total = total + got.astype(F32)
    low = total.astype(LOW)
    for bit in reversed(lead + spread):
        got = yield "dp", bit, low
        low = joined(low, got, firsts[bit])
    return low


def one_swap(axis, bit, v):
    got = yield axis, bit, v
    return got


def everywhere(coarse, fine):
    at, end = coarse.shape[0], coarse.shape[0] + fine.shape[0]
    for axis in ("tensor", "dp"):
        for b in range(lax.axis_size(axis).bit_length() - 1):
            coarse, high = rounded(coarse), rounded(fine)
            low = rounded(fine - high)
            packed = jnp.concatenate([coarse, high, low], 0).astype(LOW)
            got = yield axis, 1 << b, packed
            got = got.astype(F32)
            coarse = coarse + got[:at]
            fine = (high + low) + (got[at:end] + got[end:])
    return coarse, fine


class Pump:
    def __init__(self, token):
        self.token = token
        self.flows, self.ready, self.flying, self.done = {}, {}, {}, {}

    def gate(self, v):
        v, self.token = tied((v, self.token))
        return v

    def add(self, name, flow):
        self.flows[name] = flow
        self.ready[name] = next(flow)

    def issue(self, name):
        axis, bit, v = self.ready.pop(name)
        self.flying[name] = swap(self.gate(v), axis, bit)

    def finish(self, name):
        got = self.gate(self.flying.pop(name))
        try:
            self.ready[name] = self.flows[name].send(got)
        except StopIteration as end:
            self.done[name] = end.value

    def drain(self):
        while self.ready or self.flying:
            for name in list(self.ready):
                self.issue(name)
            for name in list(self.flying):
                self.finish(name)


def side_by_side(pack):
    half = pack.shape[0] // 2
    return jnp.concatenate([pack[:half], pack[half:]], 1)


def shards(
    layer_input,
    doc_lengths,
    norm1_gain,
    alpha_raw,
    delta_raw,
    ema_beta,
    ema_eta,
    ema_omega,
    w_z,
    q_gain,
    q_bias,
    k_gain,
    w_value,
    w_reset,
    w_update,
    w_hidden,
    w_out,
    norm2_gain,
    w_ffn_in,
    w_ffn_out,
    cotangent,
):
    member = lax.axis_index("tensor")
    place = lax.axis_index("dp")
    layer_input, begin, offs, *firsts = tied(
        (
            layer_input,
            member * layer_input.shape[1],
            (member ^ jnp.arange(4, dtype=jnp.int32)) * w_hidden.shape[0],
            (place & 1) == 0,
            (place & 2) == 0,
            (member & 1) == 0,
            (member & 2) == 0,
        )
    )
    first_core, first_chip = firsts[2:]
    firsts = dict(zip((1, 2), firsts[:2], strict=True))
    rows, length, width = layer_input.shape
    tokens = rows * length
    dims = alpha_raw.shape[0]
    zd = w_z.shape[1]
    units = w_value.shape[1]
    cols = w_hidden.shape[0]
    x = layer_input.reshape(tokens, width)
    cot = cotangent.reshape(tokens, width)
    g1, g2, om = norm1_gain[None], norm2_gain[None], ema_omega[None]
    qg, qb, kg = q_gain[None], q_bias[None], k_gain[None]

    docs = doc_lengths.shape[1]
    order = jnp.arange(docs)
    ends = jnp.sum(
        jnp.where(order[:, None] <= order[None, :], doc_lengths[:, :, None], 0), 1
    ).astype(jnp.int32)
    starts = ends - doc_lengths
    starts, ends = starts - begin, ends - begin
    places = jnp.arange(length, dtype=jnp.int32)
    docid = jnp.sum((places[None, :, None] >= ends[:, None, :]).astype(jnp.int32), 2)
    keep = 1.0 - jnp.any(places[None, :, None] == starts[:, None, :], 2).astype(F32)
    keep = jnp.broadcast_to(keep.reshape(tokens, 1), (tokens, LANES))
    blocks = docid.reshape(tokens // STRETCH, STRETCH)
    spot = jnp.arange(STRETCH)
    mask = (spot[None, :] <= spot[:, None])[None] & (blocks[:, :, None] == blocks[:, None, :])
    mask = mask.astype(F32).reshape(tokens, STRETCH)

    def unbroken(part):
        low, high = part * length, (part + 1) * length
        inside = jnp.any((starts >= low) & (starts < high), 1)
        return jnp.broadcast_to(1.0 - inside.astype(F32)[:, None], (rows, LANES))

    vm = lambda shape: pltpu.VMEM(shape, F32)
    tab = (dims, width)
    wide = (tokens, width)
    mat = 2.0 * tokens * width
    ema = 8.0 * tokens * width * dims
    chunked = (rows * dims * CHUNKS, width)
    finals = (rows * dims, width)
    slabs = (tokens * width // LANES, LANES)

    w_join = jnp.concatenate([w_hidden, w_out], 0)
    shares = (w_value, w_reset, w_join, w_ffn_in, w_ffn_out)
    bits = (1, 1, 2, 1, 1)
    pump = Pump(offs)
    beside = [swap(w, "tensor", 1) for w in (w_value, w_reset, w_ffn_in, w_ffn_out)]
    half_v, half_r, half_g, half_i, half_o = (
        pick(firsts[bit], split_rows(w)) for w, bit in zip(shares, bits, strict=True)
    )

    over_v = swap(half_v, "tensor", 2)
    beside = [pump.gate(w) for w in beside]
    over_r = swap(pump.gate(half_r), "tensor", 2)
    x = pump.gate(x)

    normed, normed_low, init, last = call(
        functools.partial(first_pass, rows),
        [(slabs, F32), (wide, LOW), (chunked, F32), (finals, F32)],
        (x, g1, alpha_raw, delta_raw, ema_beta, keep),
        ema,
        [vm(tab), vm(tab)],
    )
    last = pump.gate(last)
    over_v = pump.gate(over_v)
    other_v = swap(over_v, "dp", 1)
    f1, f2 = shift(last, 1), shift(last, 2)
    over_r = pump.gate(over_r)
    other_r = swap(over_r, "dp", 1)
    f1, f2 = pump.gate(f1), pump.gate(f2)
    over_g = swap(pump.gate(half_g), "tensor", 2)
    half_i = pump.gate(half_i)
    pre, mixed_low, z_pre, gate, probs = call(
        functools.partial(second_pass, rows),
        [(slabs, F32), (wide, LOW), ((tokens, zd), F32), (wide, F32), ((tokens, STRETCH), F32)],
        (normed, init, f1, f2, keep, unbroken(-1), alpha_raw, delta_raw, ema_beta,
         ema_eta, om, w_z, w_update, qg, qb, kg, mask),
        ema + mat * width,
        [vm(tab), vm(tab)],
    )
    split = (2, tokens, units)
    mixed_low = pump.gate(mixed_low)
    over_i = swap(half_i, "tensor", 2)
    other_v = pump.gate(other_v)
    mixed_low = pump.gate(mixed_low)

    def values(weights):
        return call(
            value_part,
            [(split, F32), (split, F32), (split, F32), (split, LOW)],
            (normed_low, mixed_low, probs, *weights),
            4 * mat * units,
        )

    own_part = values((w_value, w_reset, beside[0], beside[1]))
    united0 = pump.gate(own_part[3])
    other_r = pump.gate(other_r)
    over_g = pump.gate(over_g)
    other_g = swap(over_g, "dp", 2)
    over_o = swap(pump.gate(half_o), "tensor", 2)
    over_i = pump.gate(over_i)
    other_i = swap(over_i, "dp", 1)
    over_o = pump.gate(over_o)
    other_o = swap(over_o, "dp", 1)
    full_v = pump.gate(joined(over_v, other_v, firsts[1]))
    both_v = swap(full_v, "tensor", 1)
    full_r = pump.gate(joined(over_r, other_r, firsts[1]))
    both_r = swap(full_r, "tensor", 1)
    other_g = pump.gate(other_g)
    near_g = pump.gate(jnp.stack([w_join, joined(over_g, other_g, firsts[2])]))
    beside_g = swap(near_g, "tensor", 1)
    both_v, both_r = pump.gate(both_v), pump.gate(both_r)
    full_v = pump.gate(full_v)
    far_part = values((full_v, full_r, both_v, both_r))
    united1 = pump.gate(far_part[3])
    other_i = pump.gate(other_i)
    full_i = pump.gate(joined(over_i, other_i, firsts[1]))
    both_i = swap(full_i, "tensor", 1)
    beside_g = pump.gate(beside_g)
    wg = (near_g, beside_g)
    wv, wr = (w_value, beside[0], full_v, both_v), (w_reset, beside[1], full_r, both_r)
    kept_parts = ((*own_part[:3], united0), (*far_part[:3], united1))
    hidden_pre, blended, second, whid = call(
        blend_part,
        [(wide, F32), (wide, F32), (wide, LOW), ((width, width), LOW)],
        (offs, x, mixed_low, gate, united0, united1, *wg, g2),
        mat * (width + 4 * units),
        smem=(0,),
    )
    second = pump.gate(second)
    ffn_rows = width + 2 * units

    def ffn_of(weights):
        return call(
            ffn_part,
            [(wide, F32), (wide, F32), ((ffn_rows, units), F32), ((ffn_rows, units), LOW)],
            (second, cot, *weights),
            12 * mat * units,
        )

    ffn0 = ffn_of((w_ffn_in, beside[2], w_ffn_out, beside[3]))
    back0 = pump.gate(ffn0[1])
    other_o = pump.gate(other_o)
    full_o = pump.gate(joined(over_o, other_o, firsts[1]))
    both_o = swap(full_o, "tensor", 1)
    both_i, both_o = pump.gate(both_i), pump.gate(both_o)
    ffn1 = ffn_of((full_i, both_i, full_o, both_o))
    pump.add("F0", one_swap("tensor", 1, ffn0[3]))
    pump.add("F1", one_swap("tensor", 1, ffn1[3]))
    own = (2, 4 * cols, width // 2)
    held = {}

    def run_back():
        pack = (2, width, units)
        outs = call(
            functools.partial(back_pass, rows),
            [(wide, LOW), (wide, F32), ((1, width), F32), (own, F32), (own, LOW), (wide, F32),
             *[(pack, F32)] * 3, *[(pack, LOW)] * 3,
             (slabs, F32), ((width, zd), F32), ((8, zd), F32), (chunked, F32), (chunked, F32), (finals, F32), (finals, F32)],
            (offs, x, cot, pump.gate(blended), ffn1[1], back0, ffn0[0], ffn1[0], hidden_pre, gate,
             mixed_low, g2, w_update, whid, normed_low, probs, *kept_parts[0], *kept_parts[1], *wg,
             wv[0], wr[0], wv[1], wr[1], wv[2], wr[2], wv[3], wr[3],
             z_pre, qg, qb, kg, w_z, pre, keep, alpha_raw, delta_raw),
            (4 * width + 28 * units) * mat,
            [vm(wide), vm((tokens, STRETCH)), vm((2, tokens, zd)), vm(wide), vm((width, width)),
             pltpu.VMEM(wide, LOW)],
            smem=(0,),
        )
        held["bb"], held["v"] = outs[:5], outs[5:12]
        held["t3"] = list(outs[12:])
        pump.token, held["t3"][5] = tied((pump.token, held["t3"][5]))

    def send_back():
        back = pump.gate(jnp.concatenate([held["t3"][5], held["t3"][6]], 0))
        held["back"] = shift(back, -1), shift(back, -2)

    def take_back():
        held["back"] = [pump.gate(v) for v in held["back"]]

    def run_fourth():
        t3 = held["t3"]
        held["t4"] = call(
            functools.partial(fourth_pass, rows),
            [(wide, LOW), ((2 * dims + 8, width), F32)],
            (t3[0], normed, t3[3], t3[4], *held["back"], keep, unbroken(1), alpha_raw,
             delta_raw, ema_beta, ema_eta, om, held["v"][0], x, g1, held["bb"][1],
             held["bb"][2], t3[2]),
            2 * ema,
            [vm(tab), vm(tab), vm(slabs)],
        )
        sums = pump.gate(held["t4"][1])
        sums = jnp.concatenate([sums[:, at : at + LANES] for at in range(0, width, LANES)], 0)
        pump.add("sm", everywhere(held["t3"][1], sums))

    def packs_of(name):
        if name in "IU":
            rows_of = slice(0, width) if name == "I" else slice(width, 2 * width)
            return tuple(
                keep[rows_of] + pump.done[swapped][rows_of].astype(F32)
                for keep, swapped in ((ffn0[2], "F0"), (ffn1[2], "F1"))
            )
        kept, sent = held["bb"][3:] if name == "P" else held["v"]["RON".index(name) + 1 : 7 : 3]
        got = yield "tensor", 1, sent
        got = got.astype(F32)
        return kept[0] + got[0], kept[1] + got[1]

    def add_flow(name):
        pump.add(name, reduction(KINDS[name], packs_of(name), firsts))

    kernels = {
        "back": run_back,
        "t4": run_fourth,
    }
    for word in ORDER:
        sign, name = word[0], word[1:]
        if sign == "K":
            kernels[name]()
        elif name == "E":
            (send_back if sign == "+" else take_back)()
        elif sign == "+":
            if name in KINDS and name not in pump.flows:
                add_flow(name)
            pump.issue(name)
        else:
            pump.finish(name)
    pump.drain()
    output, input_grad = held["bb"][0], held["t4"][0]
    dz_sum, sums = pump.done["sm"]
    sums = from_slabs(sums, 2 * dims + 8)
    pair_sum, reset_sum, out_sum, value_sum, in_sum, fout_sum = (pump.done[n] for n in "PRONIU")

    alpha, sigma = jax.nn.sigmoid(alpha_raw), jax.nn.sigmoid(delta_raw)
    with_mu, with_nu = sums[:dims], sums[dims : 2 * dims]
    drive_grad = ema_eta * with_mu
    decay_grad = ema_eta * (alpha * ema_beta) * with_nu
    at = 2 * dims
    quarter = side_by_side(pair_sum[: 2 * cols])
    update_grad = joined(quarter, swap(quarter, "tensor", 1), first_core)
    update_grad = joined(update_grad, swap(update_grad, "tensor", 2), first_chip)
    return (
        output.reshape(layer_input.shape),
        input_grad.reshape(layer_input.shape),
        sums[at + 1],
        (ema_beta * drive_grad - sigma * decay_grad) * alpha * (1.0 - alpha),
        -alpha * decay_grad * sigma * (1.0 - sigma),
        alpha * drive_grad,
        (alpha * ema_beta) * with_mu,
        sums[at],
        dz_sum,
        sums[at + 3, :zd],
        sums[at + 3, zd : 2 * zd],
        sums[at + 3, 2 * zd : 3 * zd],
        value_sum.astype(F32),
        reset_sum.astype(F32),
        update_grad.astype(F32),
        side_by_side(pair_sum[2 * cols :]).astype(F32),
        side_by_side(out_sum).astype(F32),
        sums[at + 2],
        in_sum.astype(F32),
        side_by_side(fout_sum).astype(F32),
    )


def solution(mesh):
    whole, by_row = P(), P("dp", "tensor", None)
    by_col, by_unit = P(None, "tensor"), P("tensor", None)
    return jax.shard_map(
        shards,
        mesh=mesh,
        in_specs=(by_row, P("dp", None), *(whole,) * 10, by_col, by_col, whole, by_unit, by_unit, whole, by_col, by_unit, by_row),
        out_specs=(by_row, by_row, *(whole,) * 10, by_col, by_col, whole, by_unit, by_unit, whole, by_col, by_unit),
        check_vma=False,
    )
```

```python
import functools

import jax
import jax.numpy as jnp
from jax import lax
from jax.experimental import pallas as pl
from jax.experimental.pallas import tpu as pltpu
from jax.sharding import PartitionSpec as P

STRETCH = 128
LANES = 128
CHUNKS = 8
F32 = jnp.float32
LOW = jnp.bfloat16
KINDS = {"I": "y", "U": "x", "Q": "z", "P": "x", "N": "y"}
ORDER = (
    "+F0", "+F1", "-F0", "-F1", "+U", "+I", "Kback", "-U", "-I", "+Q",
    "+U", "+P", "+I", "+N", "-Q", "+Q", "-P", "+P", "-N", "-U",
    "+E", "-I", "+N", "-E", "Kt4", "-P", "-N", "-Q", "+P", "+sm",
    "+U", "-sm", "+Q", "+N", "+I", "-U", "-P", "+U", "+P", "-I",
    "+sm", "-N", "+I", "-Q", "-P", "-U", "+Q", "+U", "+P", "-sm",
    "-I", "+sm", "+I", "-U", "-Q", "+N", "+Q", "-P", "-I", "+U",
    "-sm", "-N", "+sm", "+I", "+P", "-U", "+N", "-Q", "-sm", "+Q",
    "-I", "-P", "+sm", "+P", "-N", "+N", "-Q", "+Q", "-P", "-N",
    "+N", "-sm", "-N", "-Q",
)


def silu(v):
    return v * jax.nn.sigmoid(v)


def silu_slope(v):
    s = jax.nn.sigmoid(v)
    return s * (1.0 + v * (1.0 - s))


def dot(a, b):
    return jnp.dot(a, b, preferred_element_type=F32)


def dot_rows(a, b):
    return lax.dot_general(a, b, (((0,), (0,)), ((), ())), preferred_element_type=F32)


def dot_cols(a, b):
    return lax.dot_general(a, b, (((1,), (1,)), ((), ())), preferred_element_type=F32)


def norm_parts(v):
    center = v - jnp.mean(v, -1, keepdims=True)
    scale = lax.rsqrt(jnp.mean(center * center, -1, keepdims=True) + 1e-05)
    return center * scale, scale


def norm_back(grad, hat, scale):
    return scale * (
        grad - jnp.mean(grad, -1, keepdims=True) - hat * jnp.mean(grad * hat, -1, keepdims=True)
    )


def call(kernel, outs, args, flops, scratch=(), smem=(), limit=12 << 20):
    specs = [
        pl.BlockSpec(memory_space=pltpu.SMEM if i in smem else pltpu.VMEM)
        for i in range(len(args))
    ]
    outs = [jax.ShapeDtypeStruct(s, d) for s, d in outs]
    size = sum(a.size * a.dtype.itemsize for a in args) + sum(
        o.size * o.dtype.itemsize for o in outs
    )
    return pl.pallas_call(
        kernel,
        out_shape=outs,
        in_specs=specs,
        out_specs=[pl.BlockSpec(memory_space=pltpu.VMEM) for _ in outs],
        scratch_shapes=list(scratch),
        compiler_params=pltpu.CompilerParams(vmem_limit_bytes=limit),
        cost_estimate=pl.CostEstimate(flops=int(flops), bytes_accessed=int(size), transcendentals=0),
    )(*args)


def bcast(ref, row, lanes):
    return jnp.broadcast_to(ref[pl.ds(row, 1), lanes], (CHUNKS, LANES))


def shifted(v, by, fill):
    place = lax.broadcasted_iota(jnp.int32, v.shape, 0)
    if by > 0:
        return jnp.where(place >= by, pltpu.roll(v, by, 0), fill)
    return jnp.where(place < CHUNKS + by, pltpu.roll(v, CHUNKS + by, 0), fill)


def power(v, n):
    out = None
    while n:
        if n & 1:
            out = v if out is None else out * v
        n >>= 1
        if n:
            v = v * v
    return out


def chunk_powers(base, order):
    place = lax.broadcasted_iota(jnp.int32, base.shape, 0)
    place = place if order > 0 else (CHUNKS - 1) - place
    out = jnp.where(place & 1 == 1, base, 1.0)
    base = base * base
    out = out * jnp.where(place & 2 == 2, base, 1.0)
    base = base * base
    return out * jnp.where(place & 4 == 4, base, 1.0)


def rate_tables(al_ref, de_ref, be_ref, dec_ref, drv_ref):
    alpha = jax.nn.sigmoid(al_ref[...])
    dec_ref[...] = 1.0 - alpha * jax.nn.sigmoid(de_ref[...])
    drv_ref[...] = alpha * be_ref[...]


def steps_of(ref, base, steps):
    return [ref[pl.ds(base + k, CHUNKS, stride=steps), :] for k in range(steps)]


def into_slabs(ref, v):
    tokens = v.shape[0]
    for j in range(v.shape[1] // LANES):
        ref[j * tokens : (j + 1) * tokens, :] = v[:, j * LANES : (j + 1) * LANES]


def from_slabs(v, tokens):
    return jnp.concatenate(
        [v[at : at + tokens] for at in range(0, v.shape[0], tokens)], 1
    )


def product(values):
    out = values[0]
    for v in values[1:]:
        out = out * v
    return out


def first_pass(rows, x_ref, g_ref, al_ref, de_ref, be_ref, keep_ref, normed_ref, low_ref, init_ref, last_ref, dec_ref, drv_ref):
    hat, _ = norm_parts(x_ref[...].astype(F32))
    normed = hat * g_ref[...]
    into_slabs(normed_ref, normed)
    low_ref[...] = normed.astype(LOW)
    rate_tables(al_ref, de_ref, be_ref, dec_ref, drv_ref)
    dims, width = al_ref.shape
    tokens = x_ref.shape[0]
    length = tokens // rows
    steps = length // CHUNKS

    def lane(j, carry):
        lanes = pl.ds(pl.multiple_of(j * LANES, LANES), LANES)
        for row in range(rows):
            token = steps_of(normed_ref, j * tokens + row * length, steps)
            kept = steps_of(keep_ref, row * length, steps)
            whole = product(kept)
            for n in range(dims):
                d, b = bcast(dec_ref, n, lanes), bcast(drv_ref, n, lanes)
                s = b * token[0]
                for k in range(1, steps):
                    s = (kept[k] * d) * s + b * token[k]
                a = power(d, steps) * whole
                for by in (1, 2, 4):
                    s = s + a * shifted(s, by, 0.0)
                    a = a * shifted(a, by, 1.0)
                init_ref[pl.ds((row * dims + n) * CHUNKS, CHUNKS), lanes] = shifted(s, 1, 0.0)
                last_ref[pl.ds(row * dims + n, 1), lanes] = s[CHUNKS - 1 :, :]
        return carry

    lax.fori_loop(0, width // LANES, lane, 0)


def second_pass(rows, normed_ref, init_ref, f1_ref, f2_ref, keep_ref, flag_ref, al_ref, de_ref, be_ref, eta_ref, om_ref, wz_ref, wu_ref, qg_ref, qb_ref, kg_ref, mask_ref, pre_ref, mixed_ref, zpre_ref, gate_ref, probs_ref, dec_ref, drv_ref):
    rate_tables(al_ref, de_ref, be_ref, dec_ref, drv_ref)
    dims, width = al_ref.shape
    tokens = keep_ref.shape[0]
    length = tokens // rows
    steps = length // CHUNKS

    def lane(j, carry):
        lanes = pl.ds(pl.multiple_of(j * LANES, LANES), LANES)
        omega = bcast(om_ref, 0, lanes)
        for row in range(rows):
            base = j * tokens + row * length
            token = steps_of(normed_ref, base, steps)
            kept = steps_of(keep_ref, row * length, steps)
            reach = shifted(product(kept), 1, 1.0)
            for by in (1, 2, 4):
                reach = reach * shifted(reach, by, 1.0)
            flag = bcast(flag_ref, row, pl.ds(0, LANES))
            total = [omega * t for t in token]
            for n in range(dims):
                d, b, e = bcast(dec_ref, n, lanes), bcast(drv_ref, n, lanes), bcast(eta_ref, n, lanes)
                chunk = power(d, steps)
                entering = bcast(f1_ref, row * dims + n, lanes) + (
                    power(chunk, CHUNKS) * flag
                ) * bcast(f2_ref, row * dims + n, lanes)
                s = (
                    init_ref[pl.ds((row * dims + n) * CHUNKS, CHUNKS), lanes]
                    + reach * chunk_powers(chunk, 1) * entering
                )
                for k in range(steps):
                    s = (kept[k] * d) * s + b * token[k]
                    total[k] = total[k] + e * s
            for k in range(steps):
                pre_ref[pl.ds(base + k, CHUNKS, stride=steps), :] = total[k]
        return carry

    lax.fori_loop(0, width // LANES, lane, 0)
    mixed_low = from_slabs(silu(pre_ref[...]).astype(LOW), tokens)
    mixed_ref[...] = mixed_low
    z_pre = dot(mixed_low, wz_ref[...])
    zpre_ref[...] = z_pre
    gate_ref[...] = jax.nn.sigmoid(dot(mixed_low, wu_ref[...]))
    z_low = silu(z_pre).astype(LOW).astype(F32)
    queries = (z_low * qg_ref[...] + qb_ref[...]).astype(LOW)
    keys = (z_low * kg_ref[...]).astype(LOW)
    for start in range(0, z_low.shape[0], STRETCH):
        block = slice(start, start + STRETCH)
        scores = dot_cols(queries[block], keys[block]) * z_low.shape[1] ** (-0.5)
        scores = jnp.where(mask_ref[block, :] > 0.5, scores, -1e30)
        shift = jnp.exp(scores - jnp.max(scores, -1, keepdims=True))
        probs_ref[block, :] = shift / jnp.sum(shift, -1, keepdims=True)


def value_part(normed_ref, mixed_ref, probs_ref, va_ref, ra_ref, vb_ref, rb_ref, vpre_ref, rpre_ref, att_ref, united_ref):
    tokens = normed_ref.shape[0]
    for i, (v_ref, r_ref) in enumerate(((va_ref, ra_ref), (vb_ref, rb_ref))):
        value_pre = dot(normed_ref[...], v_ref[...])
        reset_pre = dot(mixed_ref[...], r_ref[...])
        vpre_ref[i] = value_pre
        rpre_ref[i] = reset_pre
        values = silu(value_pre).astype(LOW)
        for start in range(0, tokens, STRETCH):
            block = slice(start, start + STRETCH)
            att_ref[i, block, :] = dot(probs_ref[block, :].astype(LOW), values[block])
        united_ref[i] = (silu(reset_pre) * att_ref[i]).astype(LOW)


def blend_part(offs_ref, x_ref, mixed_ref, gate_ref, u0_ref, u1_ref, ga_ref, gb_ref, gain_ref, hpre_ref, blended_ref, second_ref, whid_ref):
    cols = whid_ref.shape[0] // 4
    for r in range(4):
        whid_ref[pl.ds(pl.multiple_of(offs_ref[r], 64), cols), :] = (ga_ref, gb_ref)[r % 2][r // 2, :cols, :]
    hidden_pre = dot(mixed_ref[...], whid_ref[...])
    for r in range(4):
        united = (u0_ref, u1_ref)[r // 2][r % 2]
        hidden_pre = hidden_pre + dot(united, (ga_ref, gb_ref)[r % 2][r // 2, cols:, :])
    hpre_ref[...] = hidden_pre
    x = x_ref[...].astype(F32)
    blended = x + gate_ref[...] * (silu(hidden_pre) - x)
    blended_ref[...] = blended
    hat, _ = norm_parts(blended)
    second_ref[...] = (hat * gain_ref[...]).astype(LOW)


def ffn_part(second_ref, cot_ref, ia_ref, ib_ref, oa_ref, ob_ref, out_ref, sg_ref, keep_ref, send_ref):
    second, cot = second_ref[...], cot_ref[...]
    depth, units = ia_ref.shape
    half = depth // 2
    for i, (in_ref, fo_ref, pack_ref) in enumerate(
        ((ia_ref, oa_ref, keep_ref), (ib_ref, ob_ref, send_ref))
    ):
        up_pre = dot(second, in_ref[...])
        activated = silu(up_pre).astype(LOW)
        up_grad = (dot_cols(cot, fo_ref[...]) * silu_slope(up_pre)).astype(LOW)
        out = dot(activated, fo_ref[...])
        back = dot_cols(up_grad, in_ref[...])
        out_ref[...] = out if i == 0 else out_ref[...] + out
        sg_ref[...] = back if i == 0 else sg_ref[...] + back
        kind = pack_ref.dtype
        pack_ref[:depth, :] = dot_rows(second, up_grad).astype(kind)
        for h in range(2):
            pack_ref[depth + h * units : depth + (h + 1) * units, :] = dot_rows(
                activated, cot[:, h * half : (h + 1) * half]
            ).astype(kind)


def blend_back(offs_ref, x_ref, cot_ref, blended_ref, s0_ref, s1_ref, o0_ref, o1_ref, hpre_ref, gate_ref, mixed_ref, gain_ref, wu_ref, whid_ref, y_ref, direct_ref, hidden_ref, mg_ref, gg_ref, keep_ref, send_ref, full_ref):
    blended = blended_ref[...]
    y_ref[...] = (blended + (o0_ref[...] + o1_ref[...])).astype(LOW)
    second_grad = s0_ref[...] + s1_ref[...]
    hat, scale = norm_parts(blended)
    gg_ref[...] = jnp.sum(second_grad * hat, 0, keepdims=True)
    grad = cot_ref[...].astype(F32) + norm_back(second_grad * gain_ref[...], hat, scale)
    gate, hidden_pre, x = gate_ref[...], hpre_ref[...], x_ref[...].astype(F32)
    direct_ref[...] = grad * (1.0 - gate)
    hidden_low = (grad * gate * silu_slope(hidden_pre)).astype(LOW)
    gate_low = (grad * (silu(hidden_pre) - x) * gate * (1.0 - gate)).astype(LOW)
    hidden_ref[...] = hidden_low
    mg_ref[...] = dot_cols(gate_low, wu_ref[...]) + dot_cols(hidden_low, whid_ref[...])
    width = x.shape[1]
    cols, half = width // 4, width // 2
    for i, low in enumerate((gate_low, hidden_low)):
        full_ref[...] = dot_rows(mixed_ref[...], low)
        for r in range(4):
            pack_ref = (keep_ref, send_ref)[r % 2]
            rows = pl.ds(pl.multiple_of(offs_ref[r], 64), cols)
            for h in range(2):
                at = (2 * i + h) * cols
                pack_ref[r // 2, at : at + cols, :] = full_ref[
                    rows, h * half : (h + 1) * half
                ].astype(pack_ref.dtype)


def value_back(part, hidden_ref, normed_ref, mixed_ref, probs_ref, vpre_ref, rpre_ref, att_ref, united_ref, ga_ref, gb_ref, va_ref, ra_ref, vb_ref, rb_ref, ng_ref, mg_ref, pg_ref, *packs):
    hidden, normed, mixed = hidden_ref[...], normed_ref[...], mixed_ref[...]
    tokens, depth = hidden.shape
    units = va_ref.shape[1]
    cols = ga_ref.shape[1] - units
    half = depth // 2
    for i, (g_ref, v_ref, r_ref, pack) in enumerate(
        ((ga_ref, va_ref, ra_ref, packs[:2]), (gb_ref, vb_ref, rb_ref, packs[2:]))
    ):
        gate_pack, value_pack = pack
        kind = gate_pack.dtype
        united_grad = dot_cols(hidden, g_ref[part, cols:, :])
        reset_pre, value_pre = rpre_ref[i], vpre_ref[i]
        reset_low = (united_grad * att_ref[i] * silu_slope(reset_pre)).astype(LOW)
        attended_low = (united_grad * silu(reset_pre)).astype(LOW)
        values = silu(value_pre).astype(LOW)
        parts = []
        for start in range(0, tokens, STRETCH):
            block = slice(start, start + STRETCH)
            parts.append(dot_rows(probs_ref[block, :].astype(LOW), attended_low[block]))
            back = dot_cols(attended_low[block], values[block])
            first = i == 0 and part == 1
            pg_ref[block, :] = back if first else pg_ref[block, :] + back
        value_low = (jnp.concatenate(parts, 0) * silu_slope(value_pre)).astype(LOW)
        into_normed = dot_cols(value_low, v_ref[...])
        into_mixed = dot_cols(reset_low, r_ref[...])
        first = i == 0 and part == 1
        ng_ref[...] = into_normed if first else ng_ref[...] + into_normed
        mg_ref[...] = into_mixed if first else mg_ref[...] + into_mixed
        gate_pack[part, :depth, :] = dot_rows(mixed, reset_low).astype(kind)
        for h in range(2):
            gate_pack[part, depth + h * units : depth + (h + 1) * units, :] = dot_rows(
                united_ref[i], hidden[:, h * half : (h + 1) * half]
            ).astype(kind)
        value_pack[part] = dot_rows(normed, value_low).astype(kind)


def third_pass(rows, zpre_ref, probs_ref, p_ref, qg_ref, qb_ref, kg_ref, wz_ref, mixed_ref, m0_ref, m1_ref, pre_ref, keep_ref, al_ref, de_ref, pg_ref, dz_ref, small_ref, im_ref, iv_ref, lm_ref, lv_ref, qk_ref):
    z_pre = zpre_ref[...]
    z_low = silu(z_pre).astype(LOW).astype(F32)
    queries = (z_low * qg_ref[...] + qb_ref[...]).astype(LOW)
    keys = (z_low * kg_ref[...]).astype(LOW)
    for start in range(0, z_low.shape[0], STRETCH):
        block = slice(start, start + STRETCH)
        probs = probs_ref[block, :]
        grad = p_ref[block, :]
        grad = probs * (grad - jnp.sum(probs * grad, -1, keepdims=True)) * z_low.shape[1] ** (-0.5)
        high = grad.astype(LOW)
        rest = (grad - high.astype(F32)).astype(LOW)
        qk_ref[0, block, :] = dot(high, keys[block]) + dot(rest, keys[block])
        qk_ref[1, block, :] = dot_rows(high, queries[block]) + dot_rows(rest, queries[block])
    query_grad, key_grad = qk_ref[0], qk_ref[1]
    small_ref[...] = jnp.zeros_like(small_ref)
    small_ref[0:1, :] = jnp.sum(query_grad * z_low, 0, keepdims=True)
    small_ref[1:2, :] = jnp.sum(query_grad, 0, keepdims=True)
    small_ref[2:3, :] = jnp.sum(key_grad * z_low, 0, keepdims=True)
    z_grad = ((query_grad * qg_ref[...] + key_grad * kg_ref[...]) * silu_slope(z_pre)).astype(LOW)
    dz_ref[...] = dot_rows(mixed_ref[...], z_grad)
    mixed_grad = m0_ref[...] + m1_ref[...] + dot_cols(z_grad, wz_ref[...])
    into_slabs(pg_ref, mixed_grad)
    pg_ref[...] = pg_ref[...] * silu_slope(pre_ref[...])
    dims, width = al_ref.shape
    tokens = z_pre.shape[0]
    length = tokens // rows
    steps = length // CHUNKS

    def lane(j, carry):
        lanes = pl.ds(pl.multiple_of(j * LANES, LANES), LANES)
        for row in range(rows):
            token = steps_of(pg_ref, j * tokens + row * length, steps)
            kept = steps_of(keep_ref, row * length, steps)
            whole = product(kept)
            for n in range(dims):
                alpha = jax.nn.sigmoid(bcast(al_ref, n, lanes))
                d = 1.0 - alpha * jax.nn.sigmoid(bcast(de_ref, n, lanes))
                mu = token[steps - 1]
                m = (kept[steps - 1] * d) * mu
                v = kept[steps - 1] * mu
                for k in range(steps - 2, -1, -1):
                    mu = token[k] + m
                    rate = kept[k] * d
                    m = rate * mu
                    v = kept[k] * mu + rate * v
                a = power(d, steps) * whole
                b = steps * power(d, steps - 1) * whole
                for by in (-1, -2, -4):
                    mp, vp = shifted(m, by, 0.0), shifted(v, by, 0.0)
                    ap, bp = shifted(a, by, 1.0), shifted(b, by, 0.0)
                    v = v + a * vp + b * mp
                    m = m + a * mp
                    b = a * bp + b * ap
                    a = a * ap
                at = pl.ds((row * dims + n) * CHUNKS, CHUNKS)
                im_ref[at, lanes] = shifted(m, -1, 0.0)
                iv_ref[at, lanes] = shifted(v, -1, 0.0)
                lm_ref[pl.ds(row * dims + n, 1), lanes] = m[0:1, :]
                lv_ref[pl.ds(row * dims + n, 1), lanes] = v[0:1, :]
        return carry

    lax.fori_loop(0, width // LANES, lane, 0)


def back_pass(rows, *refs):
    offs_ref, x_ref, cot_ref, blended_ref, s0_ref, s1_ref, o0_ref, o1_ref, hpre_ref, gate_ref = refs[:10]
    mixed_ref, gain_ref, wu_ref, whid_ref, normed_ref, probs_ref = refs[10:16]
    own_part, far_part, (ga_ref, gb_ref), weights = refs[16:20], refs[20:24], refs[24:26], refs[26:34]
    zpre_ref, qg_ref, qb_ref, kg_ref, wz_ref, pre_ref, keep_ref, al_ref, de_ref = refs[34:43]
    y_ref, direct_ref, gg_ref, pair_keep_ref, pair_send_ref, ng_ref = refs[43:49]
    packs, outs = refs[49:53], refs[53:60]
    mg_ref, p_ref, qk_ref, m0_ref, full_ref, hidden_ref = refs[60:]
    blend_back(
        offs_ref, x_ref, cot_ref, blended_ref, s0_ref, s1_ref, o0_ref, o1_ref, hpre_ref, gate_ref,
        mixed_ref, gain_ref, wu_ref, whid_ref, y_ref, direct_ref, hidden_ref, m0_ref, gg_ref,
        pair_keep_ref, pair_send_ref, full_ref,
    )
    for part, parts in ((1, far_part), (0, own_part)):
        value_back(
            part, hidden_ref, normed_ref, mixed_ref, probs_ref, *parts, ga_ref, gb_ref,
            *weights[4 * part : 4 * part + 4], ng_ref, mg_ref, p_ref, *packs,
        )
    third_pass(
        rows, zpre_ref, probs_ref, p_ref, qg_ref, qb_ref, kg_ref, wz_ref, mixed_ref, m0_ref,
        mg_ref, pre_ref, keep_ref, al_ref, de_ref, *outs, qk_ref,
    )


def fourth_pass(rows, pg_ref, normed_ref, im_ref, iv_ref, near_ref, far_ref, keep_ref, flag_ref, al_ref, de_ref, be_ref, eta_ref, om_ref, n0_ref, x_ref, g_ref, direct_ref, gg_ref, qk_ref, xg_ref, sums_ref, dec_ref, drv_ref, ng_ref):
    rate_tables(al_ref, de_ref, be_ref, dec_ref, drv_ref)
    dims, width = al_ref.shape
    tokens = keep_ref.shape[0]
    length = tokens // rows
    steps = length // CHUNKS
    span = rows * dims
    sums_ref[...] = jnp.zeros_like(sums_ref)

    def lane(j, carry):
        lanes = pl.ds(pl.multiple_of(j * LANES, LANES), LANES)
        omega = bcast(om_ref, 0, lanes)
        for row in range(rows):
            base = j * tokens + row * length
            grad = steps_of(pg_ref, base, steps)
            token = steps_of(normed_ref, base, steps)
            kept = steps_of(keep_ref, row * length, steps)
            reach = shifted(product(kept), -1, 1.0)
            for by in (-1, -2, -4):
                reach = reach * shifted(reach, by, 1.0)
            place = lax.broadcasted_iota(jnp.int32, (CHUNKS, LANES), 0)
            later = (steps * (CHUNKS - 1 - place)).astype(F32)
            flag = bcast(flag_ref, row, pl.ds(0, LANES))
            total = [omega * t for t in grad]
            for n in range(dims):
                d, b, e = bcast(dec_ref, n, lanes), bcast(drv_ref, n, lanes), bcast(eta_ref, n, lanes)
                chunk = power(d, steps)
                inverse = 1.0 / d
                part = power(chunk, CHUNKS) * flag
                slope = (float(length) * part) * inverse
                at = row * dims + n
                m2 = bcast(far_ref, at, lanes)
                m_in = bcast(near_ref, at, lanes) + part * m2
                v_in = bcast(near_ref, span + at, lanes) + part * bcast(far_ref, span + at, lanes) + slope * m2
                through = reach * chunk_powers(chunk, -1)
                at = pl.ds(at * CHUNKS, CHUNKS)
                m = im_ref[at, lanes] + through * m_in
                v = iv_ref[at, lanes] + through * v_in + (later * through * inverse) * m_in
                coef = e * b
                sum_m = jnp.zeros((CHUNKS, LANES), F32)
                sum_v = jnp.zeros((CHUNKS, LANES), F32)
                for k in range(steps - 1, -1, -1):
                    mu = grad[k] + m
                    sum_m = sum_m + token[k] * mu
                    sum_v = sum_v + token[k] * v
                    total[k] = total[k] + coef * mu
                    rate = kept[k] * d
                    m = rate * mu
                    v = kept[k] * mu + rate * v
                sums_ref[pl.ds(n, 1), lanes] += jnp.sum(sum_m, 0, keepdims=True)
                sums_ref[pl.ds(dims + n, 1), lanes] += jnp.sum(sum_v, 0, keepdims=True)
            for k in range(steps):
                ng_ref[pl.ds(base + k, CHUNKS, stride=steps), :] = total[k]
        return carry

    lax.fori_loop(0, width // LANES, lane, 0)
    normed_grad = from_slabs(ng_ref[...], tokens) + n0_ref[...]
    hat, scale = norm_parts(x_ref[...].astype(F32))
    at = 2 * dims
    for j in range(width // LANES):
        slab = slice(j * tokens, (j + 1) * tokens)
        sums_ref[at : at + 1, j * LANES : (j + 1) * LANES] = jnp.sum(
            pg_ref[slab, :] * normed_ref[slab, :], 0, keepdims=True
        )
    sums_ref[at + 1 : at + 2, :] = jnp.sum(normed_grad * hat, 0, keepdims=True)
    sums_ref[at + 2 : at + 3, :] = gg_ref[...]
    zd = qk_ref.shape[1]
    for i in range(3):
        sums_ref[at + 3 : at + 4, i * zd : (i + 1) * zd] = qk_ref[i : i + 1, :]
    xg_ref[...] = (direct_ref[...] + norm_back(normed_grad * g_ref[...], hat, scale)).astype(LOW)


def swap(x, axis, bit):
    size = lax.axis_size(axis)
    return lax.ppermute(x, axis, [(i, i ^ bit) for i in range(size)])


def shift(x, by):
    size = lax.axis_size("tensor")
    return lax.ppermute(
        x, "tensor", [(i, i + by) for i in range(size) if 0 <= i + by < size]
    )


def pick(first, pair):
    return jnp.where(first, *pair)


def split_rows(v):
    half = v.shape[0] // 2
    return v[:half], v[half:]


def joined(mine, other, first):
    return pick(
        first, (jnp.concatenate([mine, other], 0), jnp.concatenate([other, mine], 0))
    )


tied = lax.optimization_barrier


def rounded(v):
    return lax.reduce_precision(v, 8, 7)


def halves(v, first):
    low, high = split_rows(v)
    return pick(first, (low, high)), pick(first, (high, low)).astype(LOW)


def reduction(kind, packs, firsts):
    bits = [1 << b for b in range(lax.axis_size("dp").bit_length() - 1)]
    lead, spread, rest = {
        "x": ([1], [2], []),
        "z": ([2], [1], []),
        "y": ([], [1, 2], []),
        "w": ([], [2, 1], []),
        "X": ([1], [], [2]),
        "Z": ([2], [], [1]),
        "Y": ([], [1], [2]),
        "W": ([], [2], [1]),
    }[kind]
    near, far = yield from packs
    for bit in lead:
        near, away = halves(near, firsts[bit])
        far, far_away = halves(far, firsts[bit])
        got = yield "dp", bit, jnp.concatenate([away, far_away], 0)
        got = got.astype(F32)
        near, far = near + got[: near.shape[0]], far + got[near.shape[0] :]
    got = yield "tensor", 2, far.astype(LOW)
    total = near + got.astype(F32)
    for bit in spread:
        total, away = halves(total, firsts[bit])
        got = yield "dp", bit, away
        total = total + got.astype(F32)
    for bit in rest + bits[2:]:
        total = rounded(total)
        got = yield "dp", bit, total.astype(LOW)
        total = total + got.astype(F32)
    low = total.astype(LOW)
    for bit in reversed(lead + spread):
        got = yield "dp", bit, low
        low = joined(low, got, firsts[bit])
    return low


def one_swap(axis, bit, v):
    got = yield axis, bit, v
    return got


def everywhere(coarse, fine):
    at, end = coarse.shape[0], coarse.shape[0] + fine.shape[0]
    for axis in ("tensor", "dp"):
        for b in range(lax.axis_size(axis).bit_length() - 1):
            coarse, high = rounded(coarse), rounded(fine)
            low = rounded(fine - high)
            packed = jnp.concatenate([coarse, high, low], 0).astype(LOW)
            got = yield axis, 1 << b, packed
            got = got.astype(F32)
            coarse = coarse + got[:at]
            fine = (high + low) + (got[at:end] + got[end:])
    return coarse, fine


class Pump:
    def __init__(self, token):
        self.token = token
        self.flows, self.ready, self.flying, self.done = {}, {}, {}, {}

    def gate(self, v):
        v, self.token = tied((v, self.token))
        return v

    def add(self, name, flow):
        self.flows[name] = flow
        self.ready[name] = next(flow)

    def issue(self, name):
        axis, bit, v = self.ready.pop(name)
        self.flying[name] = swap(self.gate(v), axis, bit)

    def finish(self, name):
        got = self.gate(self.flying.pop(name))
        try:
            self.ready[name] = self.flows[name].send(got)
        except StopIteration as end:
            self.done[name] = end.value

    def drain(self):
        while self.ready or self.flying:
            for name in list(self.ready):
                self.issue(name)
            for name in list(self.flying):
                self.finish(name)


def side_by_side(pack):
    half = pack.shape[0] // 2
    return jnp.concatenate([pack[:half], pack[half:]], 1)


def shards(
    layer_input,
    doc_lengths,
    norm1_gain,
    alpha_raw,
    delta_raw,
    ema_beta,
    ema_eta,
    ema_omega,
    w_z,
    q_gain,
    q_bias,
    k_gain,
    w_value,
    w_reset,
    w_update,
    w_hidden,
    w_out,
    norm2_gain,
    w_ffn_in,
    w_ffn_out,
    cotangent,
):
    member = lax.axis_index("tensor")
    place = lax.axis_index("dp")
    layer_input, begin, offs, *firsts = tied(
        (
            layer_input,
            member * layer_input.shape[1],
            (member ^ jnp.arange(4, dtype=jnp.int32)) * w_hidden.shape[0],
            (place & 1) == 0,
            (place & 2) == 0,
            (member & 1) == 0,
            (member & 2) == 0,
        )
    )
    first_core, first_chip = firsts[2:]
    firsts = dict(zip((1, 2), firsts[:2], strict=True))
    rows, length, width = layer_input.shape
    tokens = rows * length
    dims = alpha_raw.shape[0]
    zd = w_z.shape[1]
    units = w_value.shape[1]
    cols = w_hidden.shape[0]
    x = layer_input.reshape(tokens, width)
    cot = cotangent.reshape(tokens, width)
    g1, g2, om = norm1_gain[None], norm2_gain[None], ema_omega[None]
    qg, qb, kg = q_gain[None], q_bias[None], k_gain[None]

    docs = doc_lengths.shape[1]
    order = jnp.arange(docs)
    ends = jnp.sum(
        jnp.where(order[:, None] <= order[None, :], doc_lengths[:, :, None], 0), 1
    ).astype(jnp.int32)
    starts = ends - doc_lengths
    starts, ends = starts - begin, ends - begin
    places = jnp.arange(length, dtype=jnp.int32)
    docid = jnp.sum((places[None, :, None] >= ends[:, None, :]).astype(jnp.int32), 2)
    keep = 1.0 - jnp.any(places[None, :, None] == starts[:, None, :], 2).astype(F32)
    keep = jnp.broadcast_to(keep.reshape(tokens, 1), (tokens, LANES))
    blocks = docid.reshape(tokens // STRETCH, STRETCH)
    spot = jnp.arange(STRETCH)
    mask = (spot[None, :] <= spot[:, None])[None] & (blocks[:, :, None] == blocks[:, None, :])
    mask = mask.astype(F32).reshape(tokens, STRETCH)

    def unbroken(part):
        low, high = part * length, (part + 1) * length
        inside = jnp.any((starts >= low) & (starts < high), 1)
        return jnp.broadcast_to(1.0 - inside.astype(F32)[:, None], (rows, LANES))

    vm = lambda shape: pltpu.VMEM(shape, F32)
    tab = (dims, width)
    wide = (tokens, width)
    mat = 2.0 * tokens * width
    ema = 8.0 * tokens * width * dims
    chunked = (rows * dims * CHUNKS, width)
    finals = (rows * dims, width)
    slabs = (tokens * width // LANES, LANES)

    w_join = jnp.concatenate([w_hidden, w_out], 0)
    shares = (w_value, w_reset, w_join, w_ffn_in, w_ffn_out)
    bits = (1, 1, 2, 1, 1)
    pump = Pump(offs)
    beside = [swap(w, "tensor", 1) for w in (w_value, w_reset, w_ffn_in, w_ffn_out)]
    half_v, half_r, half_g, half_i, half_o = (
        pick(firsts[bit], split_rows(w)) for w, bit in zip(shares, bits, strict=True)
    )

    over_v = swap(half_v, "tensor", 2)
    beside = [pump.gate(w) for w in beside]
    over_r = swap(pump.gate(half_r), "tensor", 2)
    x = pump.gate(x)

    normed, normed_low, init, last = call(
        functools.partial(first_pass, rows),
        [(slabs, F32), (wide, LOW), (chunked, F32), (finals, F32)],
        (x, g1, alpha_raw, delta_raw, ema_beta, keep),
        ema,
        [vm(tab), vm(tab)],
    )
    last = pump.gate(last)
    over_v = pump.gate(over_v)
    other_v = swap(over_v, "dp", 1)
    f1, f2 = shift(last, 1), shift(last, 2)
    over_r = pump.gate(over_r)
    other_r = swap(over_r, "dp", 1)
    f1, f2 = pump.gate(f1), pump.gate(f2)
    over_g = swap(pump.gate(half_g), "tensor", 2)
    half_i = pump.gate(half_i)
    pre, mixed_low, z_pre, gate, probs = call(
        functools.partial(second_pass, rows),
        [(slabs, F32), (wide, LOW), ((tokens, zd), F32), (wide, F32), ((tokens, STRETCH), F32)],
        (normed, init, f1, f2, keep, unbroken(-1), alpha_raw, delta_raw, ema_beta,
         ema_eta, om, w_z, w_update, qg, qb, kg, mask),
        ema + mat * width,
        [vm(tab), vm(tab)],
    )
    split = (2, tokens, units)
    mixed_low = pump.gate(mixed_low)
    over_i = swap(half_i, "tensor", 2)
    other_v = pump.gate(other_v)
    mixed_low = pump.gate(mixed_low)

    def values(weights):
        return call(
            value_part,
            [(split, F32), (split, F32), (split, F32), (split, LOW)],
            (normed_low, mixed_low, probs, *weights),
            4 * mat * units,
        )

    own_part = values((w_value, w_reset, beside[0], beside[1]))
    united0 = pump.gate(own_part[3])
    other_r = pump.gate(other_r)
    over_g = pump.gate(over_g)
    other_g = swap(over_g, "dp", 2)
    over_o = swap(pump.gate(half_o), "tensor", 2)
    over_i = pump.gate(over_i)
    other_i = swap(over_i, "dp", 1)
    over_o = pump.gate(over_o)
    other_o = swap(over_o, "dp", 1)
    other_v, other_r = pump.gate(other_v), pump.gate(other_r)
    full_v = pump.gate(joined(over_v, other_v, firsts[1]))
    both_v = swap(full_v, "tensor", 1)
    full_r = pump.gate(joined(over_r, other_r, firsts[1]))
    both_r = swap(full_r, "tensor", 1)
    other_g = pump.gate(other_g)
    near_g = pump.gate(jnp.stack([w_join, joined(over_g, other_g, firsts[2])]))
    beside_g = swap(near_g, "tensor", 1)
    both_v, both_r = pump.gate(both_v), pump.gate(both_r)
    full_v = pump.gate(full_v)
    far_part = values((full_v, full_r, both_v, both_r))
    united1 = pump.gate(far_part[3])
    other_i = pump.gate(other_i)
    full_i = pump.gate(joined(over_i, other_i, firsts[1]))
    both_i = swap(full_i, "tensor", 1)
    beside_g = pump.gate(beside_g)
    wg = (near_g, beside_g)
    wv, wr = (w_value, beside[0], full_v, both_v), (w_reset, beside[1], full_r, both_r)
    kept_parts = ((*own_part[:3], united0), (*far_part[:3], united1))
    hidden_pre, blended, second, whid = call(
        blend_part,
        [(wide, F32), (wide, F32), (wide, LOW), ((width, width), LOW)],
        (offs, x, mixed_low, gate, united0, united1, *wg, g2),
        mat * (width + 4 * units),
        smem=(0,),
    )
    second = pump.gate(second)
    ffn_rows = width + 2 * units

    def ffn_of(weights):
        return call(
            ffn_part,
            [(wide, F32), (wide, F32), ((ffn_rows, units), LOW), ((ffn_rows, units), LOW)],
            (second, cot, *weights),
            12 * mat * units,
        )

    ffn0 = ffn_of((w_ffn_in, beside[2], w_ffn_out, beside[3]))
    back0 = pump.gate(ffn0[1])
    other_o = pump.gate(other_o)
    full_o = pump.gate(joined(over_o, other_o, firsts[1]))
    both_o = swap(full_o, "tensor", 1)
    both_i, both_o = pump.gate(both_i), pump.gate(both_o)
    ffn1 = ffn_of((full_i, both_i, full_o, both_o))
    pump.add("F0", one_swap("tensor", 1, ffn0[3]))
    pump.add("F1", one_swap("tensor", 1, ffn1[3]))
    own = (2, 4 * cols, width // 2)
    held = {}

    def run_back():
        outs = call(
            functools.partial(back_pass, rows),
            [(wide, LOW), (wide, F32), ((1, width), F32), (own, LOW), (own, LOW), (wide, F32),
             *[((2, 2 * width, units), LOW), ((2, width, units), LOW)] * 2,
             (slabs, F32), ((width, zd), F32), ((8, zd), F32), (chunked, F32), (chunked, F32), (finals, F32), (finals, F32)],
            (offs, x, cot, pump.gate(blended), ffn1[1], back0, ffn0[0], ffn1[0], hidden_pre, gate,
             mixed_low, g2, w_update, whid, normed_low, probs, *kept_parts[0], *kept_parts[1], *wg,
             wv[0], wr[0], wv[1], wr[1], wv[2], wr[2], wv[3], wr[3],
             z_pre, qg, qb, kg, w_z, pre, keep, alpha_raw, delta_raw),
            (4 * width + 28 * units) * mat,
            [vm(wide), vm((tokens, STRETCH)), vm((2, tokens, zd)), vm(wide), vm((width, width)),
             pltpu.VMEM(wide, LOW)],
            smem=(0,),
        )
        held["bb"], held["v"] = outs[:5], outs[5:10]
        held["t3"] = list(outs[10:])
        pump.token, held["t3"][5] = tied((pump.token, held["t3"][5]))

    def send_back():
        back = pump.gate(jnp.concatenate([held["t3"][5], held["t3"][6]], 0))
        held["back"] = shift(back, -1), shift(back, -2)

    def take_back():
        held["back"] = [pump.gate(v) for v in held["back"]]

    def run_fourth():
        t3 = held["t3"]
        held["t4"] = call(
            functools.partial(fourth_pass, rows),
            [(wide, LOW), ((2 * dims + 8, width), F32)],
            (t3[0], normed, t3[3], t3[4], *held["back"], keep, unbroken(1), alpha_raw,
             delta_raw, ema_beta, ema_eta, om, held["v"][0], x, g1, held["bb"][1],
             held["bb"][2], t3[2]),
            2 * ema,
            [vm(tab), vm(tab), vm(slabs)],
        )
        sums = pump.gate(held["t4"][1])
        sums = jnp.concatenate([sums[:, at : at + LANES] for at in range(0, width, LANES)], 0)
        pump.add("sm", everywhere(held["t3"][1], sums))

    def packs_of(name):
        if name in "IU":
            rows_of = slice(0, width) if name == "I" else slice(width, 2 * width)
            return tuple(
                keep[rows_of].astype(F32) + pump.done[swapped][rows_of].astype(F32)
                for keep, swapped in ((ffn0[2], "F0"), (ffn1[2], "F1"))
            )
        kept, sent = held["bb"][3:] if name == "P" else held["v"]["QN".index(name) + 1 : 5 : 2]
        got = yield "tensor", 1, sent
        both = kept.astype(F32) + got.astype(F32)
        return both[0], both[1]

    def add_flow(name):
        pump.add(name, reduction(KINDS[name], packs_of(name), firsts))

    kernels = {
        "back": run_back,
        "t4": run_fourth,
    }
    for word in ORDER:
        sign, name = word[0], word[1:]
        if sign == "K":
            kernels[name]()
        elif name == "E":
            (send_back if sign == "+" else take_back)()
        elif sign == "+":
            if name in KINDS and name not in pump.flows:
                add_flow(name)
            pump.issue(name)
        else:
            pump.finish(name)
    pump.drain()
    output, input_grad = held["bb"][0], held["t4"][0]
    dz_sum, sums = pump.done["sm"]
    sums = from_slabs(sums, 2 * dims + 8)
    pair_sum, gate_sum, value_sum, in_sum, fout_sum = (pump.done[n] for n in "PQNIU")

    alpha, sigma = jax.nn.sigmoid(alpha_raw), jax.nn.sigmoid(delta_raw)
    with_mu, with_nu = sums[:dims], sums[dims : 2 * dims]
    drive_grad = ema_eta * with_mu
    decay_grad = ema_eta * (alpha * ema_beta) * with_nu
    at = 2 * dims
    quarter = side_by_side(pair_sum[: 2 * cols])
    update_grad = joined(quarter, swap(quarter, "tensor", 1), first_core)
    update_grad = joined(update_grad, swap(update_grad, "tensor", 2), first_chip)
    return (
        output.reshape(layer_input.shape),
        input_grad.reshape(layer_input.shape),
        sums[at + 1],
        (ema_beta * drive_grad - sigma * decay_grad) * alpha * (1.0 - alpha),
        -alpha * decay_grad * sigma * (1.0 - sigma),
        alpha * drive_grad,
        (alpha * ema_beta) * with_mu,
        sums[at],
        dz_sum,
        sums[at + 3, :zd],
        sums[at + 3, zd : 2 * zd],
        sums[at + 3, 2 * zd : 3 * zd],
        value_sum.astype(F32),
        gate_sum[:width].astype(F32),
        update_grad.astype(F32),
        side_by_side(pair_sum[2 * cols :]).astype(F32),
        side_by_side(gate_sum[width:]).astype(F32),
        sums[at + 2],
        in_sum.astype(F32),
        side_by_side(fout_sum).astype(F32),
    )


def solution(mesh):
    whole, by_row = P(), P("dp", "tensor", None)
    by_col, by_unit = P(None, "tensor"), P("tensor", None)
    return jax.shard_map(
        shards,
        mesh=mesh,
        in_specs=(by_row, P("dp", None), *(whole,) * 10, by_col, by_col, whole, by_unit, by_unit, whole, by_col, by_unit, by_row),
        out_specs=(by_row, by_row, *(whole,) * 10, by_col, by_col, whole, by_unit, by_unit, whole, by_col, by_unit),
        check_vma=False,
    )
```

```python
import functools

import jax
import jax.numpy as jnp
from jax import lax
from jax.experimental import pallas as pl
from jax.experimental.pallas import tpu as pltpu
from jax.sharding import PartitionSpec as P

STRETCH = 128
LANES = 128
CHUNKS = 8
F32 = jnp.float32
LOW = jnp.bfloat16
KINDS = {"I": "z", "U": "W", "Q": "z", "P": "x", "N": "x"}
ORDER = (
    "+F0", "+F1", "-F0", "-F1", "+I", "+U", "Kback", "-I", "-U", "+P",
    "+Q", "+U", "+I", "-P", "+N", "+P", "-Q", "+Q", "-N", "-U",
    "+E", "-I", "+N", "-E", "-P", "+P", "+I", "Kt4", "-P", "-N",
    "-Q", "-I", "+Q", "+P", "+U", "+I", "+sm", "-P", "-sm", "+P",
    "+N", "-U", "+sm", "-Q", "-I", "+Q", "+U", "-N", "+I", "-P",
    "-sm", "+P", "-Q", "+sm", "+N", "-I", "+Q", "-P", "-sm", "+P",
    "-U", "-N", "+sm", "+I", "+N", "-sm", "-P", "+U", "+P", "-Q",
    "+Q", "-I", "-P", "+sm", "+P", "-N", "+N", "-U", "-Q", "+Q",
    "-sm", "-N", "+N", "-P", "-N", "-Q",
)


def silu(v):
    return v * jax.nn.sigmoid(v)


def silu_slope(v):
    s = jax.nn.sigmoid(v)
    return s * (1.0 + v * (1.0 - s))


def dot(a, b):
    return jnp.dot(a, b, preferred_element_type=F32)


def dot_rows(a, b):
    return lax.dot_general(a, b, (((0,), (0,)), ((), ())), preferred_element_type=F32)


def dot_cols(a, b):
    return lax.dot_general(a, b, (((1,), (1,)), ((), ())), preferred_element_type=F32)


def norm_parts(v):
    center = v - jnp.mean(v, -1, keepdims=True)
    scale = lax.rsqrt(jnp.mean(center * center, -1, keepdims=True) + 1e-05)
    return center * scale, scale


def norm_back(grad, hat, scale):
    return scale * (
        grad - jnp.mean(grad, -1, keepdims=True) - hat * jnp.mean(grad * hat, -1, keepdims=True)
    )


def call(kernel, outs, args, flops, scratch=(), smem=(), limit=12 << 20):
    specs = [
        pl.BlockSpec(memory_space=pltpu.SMEM if i in smem else pltpu.VMEM)
        for i in range(len(args))
    ]
    outs = [jax.ShapeDtypeStruct(s, d) for s, d in outs]
    size = sum(a.size * a.dtype.itemsize for a in args) + sum(
        o.size * o.dtype.itemsize for o in outs
    )
    return pl.pallas_call(
        kernel,
        out_shape=outs,
        in_specs=specs,
        out_specs=[pl.BlockSpec(memory_space=pltpu.VMEM) for _ in outs],
        scratch_shapes=list(scratch),
        compiler_params=pltpu.CompilerParams(vmem_limit_bytes=limit),
        cost_estimate=pl.CostEstimate(flops=int(flops), bytes_accessed=int(size), transcendentals=0),
    )(*args)


def bcast(ref, row, lanes):
    return jnp.broadcast_to(ref[pl.ds(row, 1), lanes], (CHUNKS, LANES))


def shifted(v, by, fill):
    place = lax.broadcasted_iota(jnp.int32, v.shape, 0)
    if by > 0:
        return jnp.where(place >= by, pltpu.roll(v, by, 0), fill)
    return jnp.where(place < CHUNKS + by, pltpu.roll(v, CHUNKS + by, 0), fill)


def power(v, n):
    out = None
    while n:
        if n & 1:
            out = v if out is None else out * v
        n >>= 1
        if n:
            v = v * v
    return out


def chunk_powers(base, order):
    place = lax.broadcasted_iota(jnp.int32, base.shape, 0)
    place = place if order > 0 else (CHUNKS - 1) - place
    out = jnp.where(place & 1 == 1, base, 1.0)
    base = base * base
    out = out * jnp.where(place & 2 == 2, base, 1.0)
    base = base * base
    return out * jnp.where(place & 4 == 4, base, 1.0)


def rate_tables(al_ref, de_ref, be_ref, dec_ref, drv_ref):
    alpha = jax.nn.sigmoid(al_ref[...])
    dec_ref[...] = 1.0 - alpha * jax.nn.sigmoid(de_ref[...])
    drv_ref[...] = alpha * be_ref[...]


def steps_of(ref, base, steps):
    return [ref[pl.ds(base + k, CHUNKS, stride=steps), :] for k in range(steps)]


def into_slabs(ref, v):
    tokens = v.shape[0]
    for j in range(v.shape[1] // LANES):
        ref[j * tokens : (j + 1) * tokens, :] = v[:, j * LANES : (j + 1) * LANES]


def from_slabs(v, tokens):
    return jnp.concatenate(
        [v[at : at + tokens] for at in range(0, v.shape[0], tokens)], 1
    )


def product(values):
    out = values[0]
    for v in values[1:]:
        out = out * v
    return out


def first_pass(rows, x_ref, g_ref, al_ref, de_ref, be_ref, keep_ref, normed_ref, low_ref, init_ref, last_ref, dec_ref, drv_ref):
    hat, _ = norm_parts(x_ref[...].astype(F32))
    normed = hat * g_ref[...]
    into_slabs(normed_ref, normed)
    low_ref[...] = normed.astype(LOW)
    rate_tables(al_ref, de_ref, be_ref, dec_ref, drv_ref)
    dims, width = al_ref.shape
    tokens = x_ref.shape[0]
    length = tokens // rows
    steps = length // CHUNKS

    def lane(j, carry):
        lanes = pl.ds(pl.multiple_of(j * LANES, LANES), LANES)
        for row in range(rows):
            token = steps_of(normed_ref, j * tokens + row * length, steps)
            kept = steps_of(keep_ref, row * length, steps)
            whole = product(kept)
            for n in range(dims):
                d, b = bcast(dec_ref, n, lanes), bcast(drv_ref, n, lanes)
                s = b * token[0]
                for k in range(1, steps):
                    s = (kept[k] * d) * s + b * token[k]
                a = power(d, steps) * whole
                for by in (1, 2, 4):
                    s = s + a * shifted(s, by, 0.0)
                    a = a * shifted(a, by, 1.0)
                init_ref[pl.ds((row * dims + n) * CHUNKS, CHUNKS), lanes] = shifted(s, 1, 0.0)
                last_ref[pl.ds(row * dims + n, 1), lanes] = s[CHUNKS - 1 :, :]
        return carry

    lax.fori_loop(0, width // LANES, lane, 0)


def second_pass(rows, normed_ref, init_ref, f1_ref, f2_ref, keep_ref, flag_ref, al_ref, de_ref, be_ref, eta_ref, om_ref, wz_ref, wu_ref, qg_ref, qb_ref, kg_ref, mask_ref, pre_ref, mixed_ref, zpre_ref, gate_ref, probs_ref, dec_ref, drv_ref):
    rate_tables(al_ref, de_ref, be_ref, dec_ref, drv_ref)
    dims, width = al_ref.shape
    tokens = keep_ref.shape[0]
    length = tokens // rows
    steps = length // CHUNKS

    def lane(j, carry):
        lanes = pl.ds(pl.multiple_of(j * LANES, LANES), LANES)
        omega = bcast(om_ref, 0, lanes)
        for row in range(rows):
            base = j * tokens + row * length
            token = steps_of(normed_ref, base, steps)
            kept = steps_of(keep_ref, row * length, steps)
            reach = shifted(product(kept), 1, 1.0)
            for by in (1, 2, 4):
                reach = reach * shifted(reach, by, 1.0)
            flag = bcast(flag_ref, row, pl.ds(0, LANES))
            total = [omega * t for t in token]
            for n in range(dims):
                d, b, e = bcast(dec_ref, n, lanes), bcast(drv_ref, n, lanes), bcast(eta_ref, n, lanes)
                chunk = power(d, steps)
                entering = bcast(f1_ref, row * dims + n, lanes) + (
                    power(chunk, CHUNKS) * flag
                ) * bcast(f2_ref, row * dims + n, lanes)
                s = (
                    init_ref[pl.ds((row * dims + n) * CHUNKS, CHUNKS), lanes]
                    + reach * chunk_powers(chunk, 1) * entering
                )
                for k in range(steps):
                    s = (kept[k] * d) * s + b * token[k]
                    total[k] = total[k] + e * s
            for k in range(steps):
                pre_ref[pl.ds(base + k, CHUNKS, stride=steps), :] = total[k]
        return carry

    lax.fori_loop(0, width // LANES, lane, 0)
    mixed_low = from_slabs(silu(pre_ref[...]).astype(LOW), tokens)
    mixed_ref[...] = mixed_low
    z_pre = dot(mixed_low, wz_ref[...])
    zpre_ref[...] = z_pre
    gate_ref[...] = jax.nn.sigmoid(dot(mixed_low, wu_ref[...]))
    z_low = silu(z_pre).astype(LOW).astype(F32)
    queries = (z_low * qg_ref[...] + qb_ref[...]).astype(LOW)
    keys = (z_low * kg_ref[...]).astype(LOW)
    for start in range(0, z_low.shape[0], STRETCH):
        block = slice(start, start + STRETCH)
        scores = dot_cols(queries[block], keys[block]) * z_low.shape[1] ** (-0.5)
        scores = jnp.where(mask_ref[block, :] > 0.5, scores, -1e30)
        shift = jnp.exp(scores - jnp.max(scores, -1, keepdims=True))
        probs_ref[block, :] = shift / jnp.sum(shift, -1, keepdims=True)


def value_part(normed_ref, mixed_ref, probs_ref, va_ref, ra_ref, vb_ref, rb_ref, vpre_ref, rpre_ref, att_ref, united_ref):
    tokens = normed_ref.shape[0]
    for i, (v_ref, r_ref) in enumerate(((va_ref, ra_ref), (vb_ref, rb_ref))):
        value_pre = dot(normed_ref[...], v_ref[...])
        reset_pre = dot(mixed_ref[...], r_ref[...])
        vpre_ref[i] = value_pre
        rpre_ref[i] = reset_pre
        values = silu(value_pre).astype(LOW)
        for start in range(0, tokens, STRETCH):
            block = slice(start, start + STRETCH)
            att_ref[i, block, :] = dot(probs_ref[block, :].astype(LOW), values[block])
        united_ref[i] = (silu(reset_pre) * att_ref[i]).astype(LOW)


def blend_part(offs_ref, x_ref, mixed_ref, gate_ref, u0_ref, u1_ref, ga_ref, gb_ref, gain_ref, hpre_ref, blended_ref, second_ref, whid_ref):
    cols = whid_ref.shape[0] // 4
    for r in range(4):
        whid_ref[pl.ds(pl.multiple_of(offs_ref[r], 64), cols), :] = (ga_ref, gb_ref)[r % 2][r // 2, :cols, :]
    hidden_pre = dot(mixed_ref[...], whid_ref[...])
    for r in range(4):
        united = (u0_ref, u1_ref)[r // 2][r % 2]
        hidden_pre = hidden_pre + dot(united, (ga_ref, gb_ref)[r % 2][r // 2, cols:, :])
    hpre_ref[...] = hidden_pre
    x = x_ref[...].astype(F32)
    blended = x + gate_ref[...] * (silu(hidden_pre) - x)
    blended_ref[...] = blended
    hat, _ = norm_parts(blended)
    second_ref[...] = (hat * gain_ref[...]).astype(LOW)


def ffn_part(second_ref, cot_ref, ia_ref, ib_ref, oa_ref, ob_ref, out_ref, sg_ref, keep_ref, send_ref):
    second, cot = second_ref[...], cot_ref[...]
    depth, units = ia_ref.shape
    half = depth // 2
    for i, (in_ref, fo_ref, pack_ref) in enumerate(
        ((ia_ref, oa_ref, keep_ref), (ib_ref, ob_ref, send_ref))
    ):
        up_pre = dot(second, in_ref[...])
        activated = silu(up_pre).astype(LOW)
        up_grad = (dot_cols(cot, fo_ref[...]) * silu_slope(up_pre)).astype(LOW)
        out = dot(activated, fo_ref[...])
        back = dot_cols(up_grad, in_ref[...])
        out_ref[...] = out if i == 0 else out_ref[...] + out
        sg_ref[...] = back if i == 0 else sg_ref[...] + back
        kind = pack_ref.dtype
        pack_ref[:depth, :] = dot_rows(second, up_grad).astype(kind)
        for h in range(2):
            pack_ref[depth + h * units : depth + (h + 1) * units, :] = dot_rows(
                activated, cot[:, h * half : (h + 1) * half]
            ).astype(kind)


def blend_back(offs_ref, x_ref, cot_ref, blended_ref, s0_ref, s1_ref, o0_ref, o1_ref, hpre_ref, gate_ref, mixed_ref, gain_ref, wu_ref, whid_ref, y_ref, direct_ref, hidden_ref, mg_ref, gg_ref, keep_ref, send_ref, full_ref):
    blended = blended_ref[...]
    y_ref[...] = (blended + (o0_ref[...] + o1_ref[...])).astype(LOW)
    second_grad = s0_ref[...] + s1_ref[...]
    hat, scale = norm_parts(blended)
    gg_ref[...] = jnp.sum(second_grad * hat, 0, keepdims=True)
    grad = cot_ref[...].astype(F32) + norm_back(second_grad * gain_ref[...], hat, scale)
    gate, hidden_pre, x = gate_ref[...], hpre_ref[...], x_ref[...].astype(F32)
    direct_ref[...] = grad * (1.0 - gate)
    hidden_low = (grad * gate * silu_slope(hidden_pre)).astype(LOW)
    gate_low = (grad * (silu(hidden_pre) - x) * gate * (1.0 - gate)).astype(LOW)
    hidden_ref[...] = hidden_low
    mg_ref[...] = dot_cols(gate_low, wu_ref[...]) + dot_cols(hidden_low, whid_ref[...])
    width = x.shape[1]
    cols, half = width // 4, width // 2
    for i, low in enumerate((gate_low, hidden_low)):
        full_ref[...] = dot_rows(mixed_ref[...], low)
        for r in range(4):
            pack_ref = (keep_ref, send_ref)[r % 2]
            rows = pl.ds(pl.multiple_of(offs_ref[r], 64), cols)
            for h in range(2):
                at = (2 * i + h) * cols
                pack_ref[r // 2, at : at + cols, :] = full_ref[
                    rows, h * half : (h + 1) * half
                ].astype(pack_ref.dtype)


def value_back(part, hidden_ref, normed_ref, mixed_ref, probs_ref, vpre_ref, rpre_ref, att_ref, united_ref, ga_ref, gb_ref, va_ref, ra_ref, vb_ref, rb_ref, ng_ref, mg_ref, pg_ref, *packs):
    hidden, normed, mixed = hidden_ref[...], normed_ref[...], mixed_ref[...]
    tokens, depth = hidden.shape
    units = va_ref.shape[1]
    cols = ga_ref.shape[1] - units
    half = depth // 2
    for i, (g_ref, v_ref, r_ref, pack) in enumerate(
        ((ga_ref, va_ref, ra_ref, packs[:2]), (gb_ref, vb_ref, rb_ref, packs[2:]))
    ):
        gate_pack, value_pack = pack
        kind = gate_pack.dtype
        united_grad = dot_cols(hidden, g_ref[part, cols:, :])
        reset_pre, value_pre = rpre_ref[i], vpre_ref[i]
        reset_low = (united_grad * att_ref[i] * silu_slope(reset_pre)).astype(LOW)
        attended_low = (united_grad * silu(reset_pre)).astype(LOW)
        values = silu(value_pre).astype(LOW)
        parts = []
        for start in range(0, tokens, STRETCH):
            block = slice(start, start + STRETCH)
            parts.append(dot_rows(probs_ref[block, :].astype(LOW), attended_low[block]))
            back = dot_cols(attended_low[block], values[block])
            first = i == 0 and part == 1
            pg_ref[block, :] = back if first else pg_ref[block, :] + back
        value_low = (jnp.concatenate(parts, 0) * silu_slope(value_pre)).astype(LOW)
        into_normed = dot_cols(value_low, v_ref[...])
        into_mixed = dot_cols(reset_low, r_ref[...])
        first = i == 0 and part == 1
        ng_ref[...] = into_normed if first else ng_ref[...] + into_normed
        mg_ref[...] = into_mixed if first else mg_ref[...] + into_mixed
        gate_pack[part, :depth, :] = dot_rows(mixed, reset_low).astype(kind)
        for h in range(2):
            gate_pack[part, depth + h * units : depth + (h + 1) * units, :] = dot_rows(
                united_ref[i], hidden[:, h * half : (h + 1) * half]
            ).astype(kind)
        value_pack[part] = dot_rows(normed, value_low).astype(kind)


def third_pass(rows, zpre_ref, probs_ref, p_ref, qg_ref, qb_ref, kg_ref, wz_ref, mixed_ref, m0_ref, m1_ref, pre_ref, keep_ref, al_ref, de_ref, pg_ref, dz_ref, small_ref, im_ref, iv_ref, lm_ref, lv_ref, qk_ref):
    z_pre = zpre_ref[...]
    z_low = silu(z_pre).astype(LOW).astype(F32)
    queries = (z_low * qg_ref[...] + qb_ref[...]).astype(LOW)
    keys = (z_low * kg_ref[...]).astype(LOW)
    for start in range(0, z_low.shape[0], STRETCH):
        block = slice(start, start + STRETCH)
        probs = probs_ref[block, :]
        grad = p_ref[block, :]
        grad = probs * (grad - jnp.sum(probs * grad, -1, keepdims=True)) * z_low.shape[1] ** (-0.5)
        high = grad.astype(LOW)
        rest = (grad - high.astype(F32)).astype(LOW)
        qk_ref[0, block, :] = dot(high, keys[block]) + dot(rest, keys[block])
        qk_ref[1, block, :] = dot_rows(high, queries[block]) + dot_rows(rest, queries[block])
    query_grad, key_grad = qk_ref[0], qk_ref[1]
    small_ref[...] = jnp.zeros_like(small_ref)
    small_ref[0:1, :] = jnp.sum(query_grad * z_low, 0, keepdims=True)
    small_ref[1:2, :] = jnp.sum(query_grad, 0, keepdims=True)
    small_ref[2:3, :] = jnp.sum(key_grad * z_low, 0, keepdims=True)
    z_grad = ((query_grad * qg_ref[...] + key_grad * kg_ref[...]) * silu_slope(z_pre)).astype(LOW)
    dz_ref[...] = dot_rows(mixed_ref[...], z_grad)
    mixed_grad = m0_ref[...] + m1_ref[...] + dot_cols(z_grad, wz_ref[...])
    into_slabs(pg_ref, mixed_grad)
    pg_ref[...] = pg_ref[...] * silu_slope(pre_ref[...])
    dims, width = al_ref.shape
    tokens = z_pre.shape[0]
    length = tokens // rows
    steps = length // CHUNKS

    def lane(j, carry):
        lanes = pl.ds(pl.multiple_of(j * LANES, LANES), LANES)
        for row in range(rows):
            token = steps_of(pg_ref, j * tokens + row * length, steps)
            kept = steps_of(keep_ref, row * length, steps)
            whole = product(kept)
            for n in range(dims):
                alpha = jax.nn.sigmoid(bcast(al_ref, n, lanes))
                d = 1.0 - alpha * jax.nn.sigmoid(bcast(de_ref, n, lanes))
                mu = token[steps - 1]
                m = (kept[steps - 1] * d) * mu
                v = kept[steps - 1] * mu
                for k in range(steps - 2, -1, -1):
                    mu = token[k] + m
                    rate = kept[k] * d
                    m = rate * mu
                    v = kept[k] * mu + rate * v
                a = power(d, steps) * whole
                b = steps * power(d, steps - 1) * whole
                for by in (-1, -2, -4):
                    mp, vp = shifted(m, by, 0.0), shifted(v, by, 0.0)
                    ap, bp = shifted(a, by, 1.0), shifted(b, by, 0.0)
                    v = v + a * vp + b * mp
                    m = m + a * mp
                    b = a * bp + b * ap
                    a = a * ap
                at = pl.ds((row * dims + n) * CHUNKS, CHUNKS)
                im_ref[at, lanes] = shifted(m, -1, 0.0)
                iv_ref[at, lanes] = shifted(v, -1, 0.0)
                lm_ref[pl.ds(row * dims + n, 1), lanes] = m[0:1, :]
                lv_ref[pl.ds(row * dims + n, 1), lanes] = v[0:1, :]
        return carry

    lax.fori_loop(0, width // LANES, lane, 0)


def back_pass(rows, *refs):
    offs_ref, x_ref, cot_ref, blended_ref, s0_ref, s1_ref, o0_ref, o1_ref, hpre_ref, gate_ref = refs[:10]
    mixed_ref, gain_ref, wu_ref, whid_ref, normed_ref, probs_ref = refs[10:16]
    own_part, far_part, (ga_ref, gb_ref), weights = refs[16:20], refs[20:24], refs[24:26], refs[26:34]
    zpre_ref, qg_ref, qb_ref, kg_ref, wz_ref, pre_ref, keep_ref, al_ref, de_ref = refs[34:43]
    y_ref, direct_ref, gg_ref, pair_keep_ref, pair_send_ref, ng_ref = refs[43:49]
    packs, outs = refs[49:53], refs[53:59]
    mg_ref, p_ref, qk_ref, m0_ref, full_ref, hidden_ref, dz_ref = refs[59:]
    blend_back(
        offs_ref, x_ref, cot_ref, blended_ref, s0_ref, s1_ref, o0_ref, o1_ref, hpre_ref, gate_ref,
        mixed_ref, gain_ref, wu_ref, whid_ref, y_ref, direct_ref, hidden_ref, m0_ref, gg_ref,
        pair_keep_ref, pair_send_ref, full_ref,
    )
    for part, parts in ((1, far_part), (0, own_part)):
        value_back(
            part, hidden_ref, normed_ref, mixed_ref, probs_ref, *parts, ga_ref, gb_ref,
            *weights[4 * part : 4 * part + 4], ng_ref, mg_ref, p_ref, *packs,
        )
    third_pass(
        rows, zpre_ref, probs_ref, p_ref, qg_ref, qb_ref, kg_ref, wz_ref, mixed_ref, m0_ref,
        mg_ref, pre_ref, keep_ref, al_ref, de_ref, outs[0], dz_ref, *outs[1:], qk_ref,
    )
    width, zd = dz_ref.shape
    blocks, cols = width // (2 * zd), width // 4
    share = cols // blocks
    for r in range(4):
        pack_ref = (pair_keep_ref, pair_send_ref)[r % 2]
        for c in range(blocks):
            rows_at = pl.ds(pl.multiple_of(offs_ref[r] + c * share, 64), share)
            pack_ref[r // 2, 4 * cols : 4 * cols + share, c * zd : (c + 1) * zd] = dz_ref[
                rows_at, :
            ].astype(pack_ref.dtype)
        pack_ref[r // 2, 4 * cols + share :, :] = jnp.zeros((share, width // 2), pack_ref.dtype)


def fourth_pass(rows, pg_ref, normed_ref, im_ref, iv_ref, near_ref, far_ref, keep_ref, flag_ref, al_ref, de_ref, be_ref, eta_ref, om_ref, n0_ref, x_ref, g_ref, direct_ref, gg_ref, qk_ref, xg_ref, sums_ref, dec_ref, drv_ref, ng_ref):
    rate_tables(al_ref, de_ref, be_ref, dec_ref, drv_ref)
    dims, width = al_ref.shape
    tokens = keep_ref.shape[0]
    length = tokens // rows
    steps = length // CHUNKS
    span = rows * dims
    sums_ref[...] = jnp.zeros_like(sums_ref)

    def lane(j, carry):
        lanes = pl.ds(pl.multiple_of(j * LANES, LANES), LANES)
        omega = bcast(om_ref, 0, lanes)
        for row in range(rows):
            base = j * tokens + row * length
            grad = steps_of(pg_ref, base, steps)
            token = steps_of(normed_ref, base, steps)
            kept = steps_of(keep_ref, row * length, steps)
            reach = shifted(product(kept), -1, 1.0)
            for by in (-1, -2, -4):
                reach = reach * shifted(reach, by, 1.0)
            place = lax.broadcasted_iota(jnp.int32, (CHUNKS, LANES), 0)
            later = (steps * (CHUNKS - 1 - place)).astype(F32)
            flag = bcast(flag_ref, row, pl.ds(0, LANES))
            total = [omega * t for t in grad]
            for n in range(dims):
                d, b, e = bcast(dec_ref, n, lanes), bcast(drv_ref, n, lanes), bcast(eta_ref, n, lanes)
                chunk = power(d, steps)
                inverse = 1.0 / d
                part = power(chunk, CHUNKS) * flag
                slope = (float(length) * part) * inverse
                at = row * dims + n
                m2 = bcast(far_ref, at, lanes)
                m_in = bcast(near_ref, at, lanes) + part * m2
                v_in = bcast(near_ref, span + at, lanes) + part * bcast(far_ref, span + at, lanes) + slope * m2
                through = reach * chunk_powers(chunk, -1)
                at = pl.ds(at * CHUNKS, CHUNKS)
                m = im_ref[at, lanes] + through * m_in
                v = iv_ref[at, lanes] + through * v_in + (later * through * inverse) * m_in
                coef = e * b
                sum_m = jnp.zeros((CHUNKS, LANES), F32)
                sum_v = jnp.zeros((CHUNKS, LANES), F32)
                for k in range(steps - 1, -1, -1):
                    mu = grad[k] + m
                    sum_m = sum_m + token[k] * mu
                    sum_v = sum_v + token[k] * v
                    total[k] = total[k] + coef * mu
                    rate = kept[k] * d
                    m = rate * mu
                    v = kept[k] * mu + rate * v
                sums_ref[pl.ds(n, 1), lanes] += jnp.sum(sum_m, 0, keepdims=True)
                sums_ref[pl.ds(dims + n, 1), lanes] += jnp.sum(sum_v, 0, keepdims=True)
            for k in range(steps):
                ng_ref[pl.ds(base + k, CHUNKS, stride=steps), :] = total[k]
        return carry

    lax.fori_loop(0, width // LANES, lane, 0)
    normed_grad = from_slabs(ng_ref[...], tokens) + n0_ref[...]
    hat, scale = norm_parts(x_ref[...].astype(F32))
    at = 2 * dims
    for j in range(width // LANES):
        slab = slice(j * tokens, (j + 1) * tokens)
        sums_ref[at : at + 1, j * LANES : (j + 1) * LANES] = jnp.sum(
            pg_ref[slab, :] * normed_ref[slab, :], 0, keepdims=True
        )
    sums_ref[at + 1 : at + 2, :] = jnp.sum(normed_grad * hat, 0, keepdims=True)
    sums_ref[at + 2 : at + 3, :] = gg_ref[...]
    zd = qk_ref.shape[1]
    for i in range(3):
        sums_ref[at + 3 : at + 4, i * zd : (i + 1) * zd] = qk_ref[i : i + 1, :]
    xg_ref[...] = (direct_ref[...] + norm_back(normed_grad * g_ref[...], hat, scale)).astype(LOW)


def swap(x, axis, bit):
    size = lax.axis_size(axis)
    return lax.ppermute(x, axis, [(i, i ^ bit) for i in range(size)])


def shift(x, by):
    size = lax.axis_size("tensor")
    return lax.ppermute(
        x, "tensor", [(i, i + by) for i in range(size) if 0 <= i + by < size]
    )


def pick(first, pair):
    return jnp.where(first, *pair)


def split_rows(v):
    half = v.shape[0] // 2
    return v[:half], v[half:]


def joined(mine, other, first):
    return pick(
        first, (jnp.concatenate([mine, other], 0), jnp.concatenate([other, mine], 0))
    )


tied = lax.optimization_barrier


def rounded(v):
    return lax.reduce_precision(v, 8, 7)


def halves(v, first):
    low, high = split_rows(v)
    return pick(first, (low, high)), pick(first, (high, low)).astype(LOW)


def reduction(kind, packs, firsts):
    bits = [1 << b for b in range(lax.axis_size("dp").bit_length() - 1)]
    lead, spread, rest = {
        "x": ([1], [2], []),
        "z": ([2], [1], []),
        "y": ([], [1, 2], []),
        "w": ([], [2, 1], []),
        "X": ([1], [], [2]),
        "Z": ([2], [], [1]),
        "Y": ([], [1], [2]),
        "W": ([], [2], [1]),
    }[kind]
    near, far = yield from packs
    for bit in lead:
        near, away = halves(near, firsts[bit])
        far, far_away = halves(far, firsts[bit])
        got = yield "dp", bit, jnp.concatenate([away, far_away], 0)
        got = got.astype(F32)
        near, far = near + got[: near.shape[0]], far + got[near.shape[0] :]
    got = yield "tensor", 2, far.astype(LOW)
    total = near + got.astype(F32)
    for bit in spread:
        total, away = halves(total, firsts[bit])
        got = yield "dp", bit, away
        total = total + got.astype(F32)
    for bit in rest + bits[2:]:
        total = rounded(total)
        got = yield "dp", bit, total.astype(LOW)
        total = total + got.astype(F32)
    low = total.astype(LOW)
    for bit in reversed(lead + spread):
        got = yield "dp", bit, low
        low = joined(low, got, firsts[bit])
    return low


def one_swap(axis, bit, v):
    got = yield axis, bit, v
    return got


def everywhere(v):
    size = v.shape[0]
    for axis in ("tensor", "dp"):
        for b in range(lax.axis_size(axis).bit_length() - 1):
            high = rounded(v)
            low = rounded(v - high)
            got = yield axis, 1 << b, jnp.concatenate([high, low], 0).astype(LOW)
            got = got.astype(F32)
            v = (high + low) + (got[:size] + got[size:])
    return v


class Pump:
    def __init__(self, token):
        self.token = token
        self.flows, self.ready, self.flying, self.done = {}, {}, {}, {}

    def gate(self, v):
        v, self.token = tied((v, self.token))
        return v

    def add(self, name, flow):
        self.flows[name] = flow
        self.ready[name] = next(flow)

    def issue(self, name):
        axis, bit, v = self.ready.pop(name)
        self.flying[name] = swap(self.gate(v), axis, bit)

    def finish(self, name):
        got = self.gate(self.flying.pop(name))
        try:
            self.ready[name] = self.flows[name].send(got)
        except StopIteration as end:
            self.done[name] = end.value

    def drain(self):
        while self.ready or self.flying:
            for name in list(self.ready):
                self.issue(name)
            for name in list(self.flying):
                self.finish(name)


def side_by_side(pack):
    half = pack.shape[0] // 2
    return jnp.concatenate([pack[:half], pack[half:]], 1)


def shards(
    layer_input,
    doc_lengths,
    norm1_gain,
    alpha_raw,
    delta_raw,
    ema_beta,
    ema_eta,
    ema_omega,
    w_z,
    q_gain,
    q_bias,
    k_gain,
    w_value,
    w_reset,
    w_update,
    w_hidden,
    w_out,
    norm2_gain,
    w_ffn_in,
    w_ffn_out,
    cotangent,
):
    member = lax.axis_index("tensor")
    place = lax.axis_index("dp")
    layer_input, begin, offs, *firsts = tied(
        (
            layer_input,
            member * layer_input.shape[1],
            (member ^ jnp.arange(4, dtype=jnp.int32)) * w_hidden.shape[0],
            (place & 1) == 0,
            (place & 2) == 0,
            (member & 1) == 0,
            (member & 2) == 0,
        )
    )
    first_core, first_chip = firsts[2:]
    firsts = dict(zip((1, 2), firsts[:2], strict=True))
    rows, length, width = layer_input.shape
    tokens = rows * length
    dims = alpha_raw.shape[0]
    zd = w_z.shape[1]
    units = w_value.shape[1]
    cols = w_hidden.shape[0]
    x = layer_input.reshape(tokens, width)
    cot = cotangent.reshape(tokens, width)
    g1, g2, om = norm1_gain[None], norm2_gain[None], ema_omega[None]
    qg, qb, kg = q_gain[None], q_bias[None], k_gain[None]

    docs = doc_lengths.shape[1]
    order = jnp.arange(docs)
    ends = jnp.sum(
        jnp.where(order[:, None] <= order[None, :], doc_lengths[:, :, None], 0), 1
    ).astype(jnp.int32)
    starts = ends - doc_lengths
    starts, ends = starts - begin, ends - begin
    places = jnp.arange(length, dtype=jnp.int32)
    docid = jnp.sum((places[None, :, None] >= ends[:, None, :]).astype(jnp.int32), 2)
    keep = 1.0 - jnp.any(places[None, :, None] == starts[:, None, :], 2).astype(F32)
    keep = jnp.broadcast_to(keep.reshape(tokens, 1), (tokens, LANES))
    blocks = docid.reshape(tokens // STRETCH, STRETCH)
    spot = jnp.arange(STRETCH)
    mask = (spot[None, :] <= spot[:, None])[None] & (blocks[:, :, None] == blocks[:, None, :])
    mask = mask.astype(F32).reshape(tokens, STRETCH)

    def unbroken(part):
        low, high = part * length, (part + 1) * length
        inside = jnp.any((starts >= low) & (starts < high), 1)
        return jnp.broadcast_to(1.0 - inside.astype(F32)[:, None], (rows, LANES))

    vm = lambda shape: pltpu.VMEM(shape, F32)
    tab = (dims, width)
    wide = (tokens, width)
    mat = 2.0 * tokens * width
    ema = 8.0 * tokens * width * dims
    chunked = (rows * dims * CHUNKS, width)
    finals = (rows * dims, width)
    slabs = (tokens * width // LANES, LANES)

    w_join = jnp.concatenate([w_hidden, w_out], 0)
    shares = (w_value, w_reset, w_join, w_ffn_in, w_ffn_out)
    bits = (1, 1, 2, 1, 1)
    pump = Pump(offs)
    beside = [swap(w, "tensor", 1) for w in (w_value, w_reset, w_ffn_in, w_ffn_out)]
    half_v, half_r, half_g, half_i, half_o = (
        pick(firsts[bit], split_rows(w)) for w, bit in zip(shares, bits, strict=True)
    )

    over_v = swap(half_v, "tensor", 2)
    beside = [pump.gate(w) for w in beside]
    over_r = swap(pump.gate(half_r), "tensor", 2)
    x = pump.gate(x)

    normed, normed_low, init, last = call(
        functools.partial(first_pass, rows),
        [(slabs, F32), (wide, LOW), (chunked, F32), (finals, F32)],
        (x, g1, alpha_raw, delta_raw, ema_beta, keep),
        ema,
        [vm(tab), vm(tab)],
    )
    last = pump.gate(last)
    over_v = pump.gate(over_v)
    other_v = swap(over_v, "dp", 1)
    f1, f2 = shift(last, 1), shift(last, 2)
    over_r = pump.gate(over_r)
    other_r = swap(over_r, "dp", 1)
    f1, f2 = pump.gate(f1), pump.gate(f2)
    over_g = swap(pump.gate(half_g), "tensor", 2)
    half_i = pump.gate(half_i)
    pre, mixed_low, z_pre, gate, probs = call(
        functools.partial(second_pass, rows),
        [(slabs, F32), (wide, LOW), ((tokens, zd), F32), (wide, F32), ((tokens, STRETCH), F32)],
        (normed, init, f1, f2, keep, unbroken(-1), alpha_raw, delta_raw, ema_beta,
         ema_eta, om, w_z, w_update, qg, qb, kg, mask),
        ema + mat * width,
        [vm(tab), vm(tab)],
    )
    split = (2, tokens, units)
    mixed_low = pump.gate(mixed_low)
    over_i = swap(half_i, "tensor", 2)
    other_v = pump.gate(other_v)
    mixed_low = pump.gate(mixed_low)

    def values(weights):
        return call(
            value_part,
            [(split, F32), (split, F32), (split, F32), (split, LOW)],
            (normed_low, mixed_low, probs, *weights),
            4 * mat * units,
        )

    own_part = values((w_value, w_reset, beside[0], beside[1]))
    united0 = pump.gate(own_part[3])
    other_r = pump.gate(other_r)
    over_g, over_i = pump.gate(over_g), pump.gate(over_i)
    over_g, over_i, half_o = pump.gate(over_g), pump.gate(over_i), pump.gate(half_o)
    over_o = swap(half_o, "tensor", 2)
    other_g = swap(over_g, "dp", 2)
    other_i = swap(over_i, "dp", 1)
    other_v, other_r = pump.gate(other_v), pump.gate(other_r)
    full_v = pump.gate(joined(over_v, other_v, firsts[1]))
    both_v = swap(full_v, "tensor", 1)
    full_r = pump.gate(joined(over_r, other_r, firsts[1]))
    both_r = swap(full_r, "tensor", 1)
    both_v, both_r = pump.gate(both_v), pump.gate(both_r)
    full_v = pump.gate(full_v)
    far_part = values((full_v, full_r, both_v, both_r))
    united1 = pump.gate(far_part[3])
    over_o = pump.gate(over_o)
    other_i = pump.gate(other_i)
    other_o = swap(over_o, "dp", 1)
    other_g = pump.gate(other_g)
    near_g = pump.gate(jnp.stack([w_join, joined(over_g, other_g, firsts[2])]))
    beside_g = swap(near_g, "tensor", 1)
    full_i = pump.gate(joined(over_i, other_i, firsts[1]))
    both_i = swap(full_i, "tensor", 1)
    beside_g = pump.gate(beside_g)
    wg = (near_g, beside_g)
    wv, wr = (w_value, beside[0], full_v, both_v), (w_reset, beside[1], full_r, both_r)
    kept_parts = ((*own_part[:3], united0), (*far_part[:3], united1))
    hidden_pre, blended, second, whid = call(
        blend_part,
        [(wide, F32), (wide, F32), (wide, LOW), ((width, width), LOW)],
        (offs, x, mixed_low, gate, united0, united1, *wg, g2),
        mat * (width + 4 * units),
        smem=(0,),
    )
    second = pump.gate(second)
    ffn_rows = width + 2 * units

    def ffn_of(weights):
        return call(
            ffn_part,
            [(wide, F32), (wide, F32), ((ffn_rows, units), LOW), ((ffn_rows, units), LOW)],
            (second, cot, *weights),
            12 * mat * units,
        )

    ffn0 = ffn_of((w_ffn_in, beside[2], w_ffn_out, beside[3]))
    back0 = pump.gate(ffn0[1])
    other_o = pump.gate(other_o)
    full_o = pump.gate(joined(over_o, other_o, firsts[1]))
    both_o = swap(full_o, "tensor", 1)
    both_i, both_o = pump.gate(both_i), pump.gate(both_o)
    ffn1 = ffn_of((full_i, both_i, full_o, both_o))
    pump.add("F0", one_swap("tensor", 1, ffn0[3]))
    pump.add("F1", one_swap("tensor", 1, ffn1[3]))
    share = cols * zd // (width // 2)
    own = (2, 4 * cols + 2 * share, width // 2)
    held = {}

    def run_back():
        outs = call(
            functools.partial(back_pass, rows),
            [(wide, LOW), (wide, F32), ((1, width), F32), (own, LOW), (own, LOW), (wide, F32),
             *[((2, 2 * width, units), LOW), ((2, width, units), LOW)] * 2,
             (slabs, F32), ((8, zd), F32), (chunked, F32), (chunked, F32), (finals, F32), (finals, F32)],
            (offs, x, cot, pump.gate(blended), ffn1[1], back0, ffn0[0], ffn1[0], hidden_pre, gate,
             mixed_low, g2, w_update, whid, normed_low, probs, *kept_parts[0], *kept_parts[1], *wg,
             wv[0], wr[0], wv[1], wr[1], wv[2], wr[2], wv[3], wr[3],
             z_pre, qg, qb, kg, w_z, pre, keep, alpha_raw, delta_raw),
            (4 * width + 28 * units) * mat,
            [vm(wide), vm((tokens, STRETCH)), vm((2, tokens, zd)), vm(wide), vm((width, width)),
             pltpu.VMEM(wide, LOW), vm((width, zd))],
            smem=(0,),
        )
        held["bb"], held["v"] = outs[:5], outs[5:10]
        held["t3"] = list(outs[10:])
        pump.token, held["t3"][4] = tied((pump.token, held["t3"][4]))

    def send_back():
        back = pump.gate(jnp.concatenate([held["t3"][4], held["t3"][5]], 0))
        held["back"] = shift(back, -1), shift(back, -2)

    def take_back():
        held["back"] = [pump.gate(v) for v in held["back"]]

    def run_fourth():
        t3 = held["t3"]
        held["t4"] = call(
            functools.partial(fourth_pass, rows),
            [(wide, LOW), ((2 * dims + 8, width), F32)],
            (t3[0], normed, t3[2], t3[3], *held["back"], keep, unbroken(1), alpha_raw,
             delta_raw, ema_beta, ema_eta, om, held["v"][0], x, g1, held["bb"][1],
             held["bb"][2], t3[1]),
            2 * ema,
            [vm(tab), vm(tab), vm(slabs)],
        )
        sums = pump.gate(held["t4"][1])
        sums = jnp.concatenate([sums[:, at : at + LANES] for at in range(0, width, LANES)], 0)
        pump.add("sm", everywhere(sums))

    def packs_of(name):
        if name in "IU":
            rows_of = slice(0, width) if name == "I" else slice(width, 2 * width)
            return tuple(
                keep[rows_of].astype(F32) + pump.done[swapped][rows_of].astype(F32)
                for keep, swapped in ((ffn0[2], "F0"), (ffn1[2], "F1"))
            )
        kept, sent = held["bb"][3:] if name == "P" else held["v"]["QN".index(name) + 1 : 5 : 2]
        got = yield "tensor", 1, sent
        both = kept.astype(F32) + got.astype(F32)
        return both[0], both[1]

    def with_shared():
        low = yield from reduction(KINDS["P"], packs_of("P"), firsts)
        v = jnp.concatenate([low[: 2 * cols], low[4 * cols : 4 * cols + share]], 0)
        for bit, first in ((1, first_core), (2, first_chip)):
            got = yield "tensor", bit, v
            v = joined(v, got, first)
        return low[2 * cols : 4 * cols], v.reshape(4, 2 * cols + share, width // 2)

    def add_flow(name):
        pump.add(
            name, with_shared() if name == "P" else reduction(KINDS[name], packs_of(name), firsts)
        )

    kernels = {
        "back": run_back,
        "t4": run_fourth,
    }
    for word in ORDER:
        sign, name = word[0], word[1:]
        if sign == "K":
            kernels[name]()
        elif name == "E":
            (send_back if sign == "+" else take_back)()
        elif sign == "+":
            if name in KINDS and name not in pump.flows:
                add_flow(name)
            pump.issue(name)
        else:
            pump.finish(name)
    pump.drain()
    output, input_grad = held["bb"][0], held["t4"][0]
    sums = from_slabs(pump.done["sm"], 2 * dims + 8)
    pair_sum, gate_sum, value_sum, in_sum, fout_sum = (pump.done[n] for n in "PQNIU")

    alpha, sigma = jax.nn.sigmoid(alpha_raw), jax.nn.sigmoid(delta_raw)
    with_mu, with_nu = sums[:dims], sums[dims : 2 * dims]
    drive_grad = ema_eta * with_mu
    decay_grad = ema_eta * (alpha * ema_beta) * with_nu
    at = 2 * dims
    hidden_sum, shared = pair_sum
    update_grad = jnp.concatenate([side_by_side(v[: 2 * cols]) for v in shared], 0)
    dz_sum = jnp.concatenate(
        [v[2 * cols :, at : at + zd] for v in shared for at in range(0, width // 2, zd)], 0
    )
    return (
        output.reshape(layer_input.shape),
        input_grad.reshape(layer_input.shape),
        sums[at + 1],
        (ema_beta * drive_grad - sigma * decay_grad) * alpha * (1.0 - alpha),
        -alpha * decay_grad * sigma * (1.0 - sigma),
        alpha * drive_grad,
        (alpha * ema_beta) * with_mu,
        sums[at],
        dz_sum.astype(F32),
        sums[at + 3, :zd],
        sums[at + 3, zd : 2 * zd],
        sums[at + 3, 2 * zd : 3 * zd],
        value_sum.astype(F32),
        gate_sum[:width].astype(F32),
        update_grad.astype(F32),
        side_by_side(hidden_sum).astype(F32),
        side_by_side(gate_sum[width:]).astype(F32),
        sums[at + 2],
        in_sum.astype(F32),
        side_by_side(fout_sum).astype(F32),
    )


def solution(mesh):
    whole, by_row = P(), P("dp", "tensor", None)
    by_col, by_unit = P(None, "tensor"), P("tensor", None)
    return jax.shard_map(
        shards,
        mesh=mesh,
        in_specs=(by_row, P("dp", None), *(whole,) * 10, by_col, by_col, whole, by_unit, by_unit, whole, by_col, by_unit, by_row),
        out_specs=(by_row, by_row, *(whole,) * 10, by_col, by_col, whole, by_unit, by_unit, whole, by_col, by_unit),
        check_vma=False,
    )
```

```python
import functools

import jax
import jax.numpy as jnp
from jax import lax
from jax.experimental import pallas as pl
from jax.experimental.pallas import tpu as pltpu
from jax.sharding import PartitionSpec as P

STRETCH = 128
LANES = 128
CHUNKS = 8
F32 = jnp.float32
LOW = jnp.bfloat16
KINDS = {"I": "y", "U": "z", "Q": "x", "P": "z", "N": "Z"}
ORDER = (
    "+F0", "+F1", "-F0", "-F1", "+I", "+U", "Kback", "-I", "-U", "+P",
    "+Q", "+I", "+U", "-P", "+N", "+P", "-Q", "+Q", "-N", "-I",
    "+E", "-U", "+N", "-E", "-P", "+P", "Kt4", "-P", "-N", "-Q",
    "+P", "+Q", "+I", "+U", "-P", "+sm", "+P", "-sm", "-I", "+N",
    "-U", "+I", "-Q", "+Q", "+sm", "-P", "+P", "-N", "+U", "-I",
    "-sm", "+I", "-Q", "-P", "+Q", "+N", "-I", "-U", "+P", "+U",
    "+I", "-N", "+N", "-U", "+sm", "-Q", "-P", "+Q", "+P", "-I",
    "-sm", "+sm", "+U", "-Q", "-N", "+Q", "-sm", "-P", "+sm", "+N",
    "+P", "-U", "-P", "-sm", "-N", "-Q",
)


def silu(v):
    return v * jax.nn.sigmoid(v)


def silu_slope(v):
    s = jax.nn.sigmoid(v)
    return s * (1.0 + v * (1.0 - s))


def dot(a, b):
    return jnp.dot(a, b, preferred_element_type=F32)


def dot_rows(a, b):
    return lax.dot_general(a, b, (((0,), (0,)), ((), ())), preferred_element_type=F32)


def dot_cols(a, b):
    return lax.dot_general(a, b, (((1,), (1,)), ((), ())), preferred_element_type=F32)


def norm_parts(v):
    center = v - jnp.mean(v, -1, keepdims=True)
    scale = lax.rsqrt(jnp.mean(center * center, -1, keepdims=True) + 1e-05)
    return center * scale, scale


def norm_back(grad, hat, scale):
    return scale * (
        grad - jnp.mean(grad, -1, keepdims=True) - hat * jnp.mean(grad * hat, -1, keepdims=True)
    )


def call(kernel, outs, args, flops, scratch=(), smem=(), limit=12 << 20):
    specs = [
        pl.BlockSpec(memory_space=pltpu.SMEM if i in smem else pltpu.VMEM)
        for i in range(len(args))
    ]
    outs = [jax.ShapeDtypeStruct(s, d) for s, d in outs]
    size = sum(a.size * a.dtype.itemsize for a in args) + sum(
        o.size * o.dtype.itemsize for o in outs
    )
    return pl.pallas_call(
        kernel,
        out_shape=outs,
        in_specs=specs,
        out_specs=[pl.BlockSpec(memory_space=pltpu.VMEM) for _ in outs],
        scratch_shapes=list(scratch),
        compiler_params=pltpu.CompilerParams(vmem_limit_bytes=limit),
        cost_estimate=pl.CostEstimate(flops=int(flops), bytes_accessed=int(size), transcendentals=0),
    )(*args)


def bcast(ref, row, lanes):
    return jnp.broadcast_to(ref[pl.ds(row, 1), lanes], (CHUNKS, LANES))


def shifted(v, by, fill):
    place = lax.broadcasted_iota(jnp.int32, v.shape, 0)
    if by > 0:
        return jnp.where(place >= by, pltpu.roll(v, by, 0), fill)
    return jnp.where(place < CHUNKS + by, pltpu.roll(v, CHUNKS + by, 0), fill)


def power(v, n):
    out = None
    while n:
        if n & 1:
            out = v if out is None else out * v
        n >>= 1
        if n:
            v = v * v
    return out


def chunk_powers(base, order):
    place = lax.broadcasted_iota(jnp.int32, base.shape, 0)
    place = place if order > 0 else (CHUNKS - 1) - place
    out = jnp.where(place & 1 == 1, base, 1.0)
    base = base * base
    out = out * jnp.where(place & 2 == 2, base, 1.0)
    base = base * base
    return out * jnp.where(place & 4 == 4, base, 1.0)


def rate_tables(al_ref, de_ref, be_ref, dec_ref, drv_ref):
    alpha = jax.nn.sigmoid(al_ref[...])
    dec_ref[...] = 1.0 - alpha * jax.nn.sigmoid(de_ref[...])
    drv_ref[...] = alpha * be_ref[...]


def steps_of(ref, base, steps):
    return [ref[pl.ds(base + k, CHUNKS, stride=steps), :] for k in range(steps)]


def into_slabs(ref, v):
    tokens = v.shape[0]
    for j in range(v.shape[1] // LANES):
        ref[j * tokens : (j + 1) * tokens, :] = v[:, j * LANES : (j + 1) * LANES]


def from_slabs(v, tokens):
    return jnp.concatenate(
        [v[at : at + tokens] for at in range(0, v.shape[0], tokens)], 1
    )


def product(values):
    out = values[0]
    for v in values[1:]:
        out = out * v
    return out


def first_pass(rows, x_ref, g_ref, al_ref, de_ref, be_ref, keep_ref, normed_ref, low_ref, init_ref, last_ref, dec_ref, drv_ref):
    hat, _ = norm_parts(x_ref[...].astype(F32))
    normed = hat * g_ref[...]
    into_slabs(normed_ref, normed)
    low_ref[...] = normed.astype(LOW)
    rate_tables(al_ref, de_ref, be_ref, dec_ref, drv_ref)
    dims, width = al_ref.shape
    tokens = x_ref.shape[0]
    length = tokens // rows
    steps = length // CHUNKS

    def lane(j, carry):
        lanes = pl.ds(pl.multiple_of(j * LANES, LANES), LANES)
        for row in range(rows):
            token = steps_of(normed_ref, j * tokens + row * length, steps)
            kept = steps_of(keep_ref, row * length, steps)
            whole = product(kept)
            for n in range(dims):
                d, b = bcast(dec_ref, n, lanes), bcast(drv_ref, n, lanes)
                s = b * token[0]
                for k in range(1, steps):
                    s = (kept[k] * d) * s + b * token[k]
                a = power(d, steps) * whole
                for by in (1, 2, 4):
                    s = s + a * shifted(s, by, 0.0)
                    a = a * shifted(a, by, 1.0)
                init_ref[pl.ds((row * dims + n) * CHUNKS, CHUNKS), lanes] = shifted(s, 1, 0.0)
                last_ref[pl.ds(row * dims + n, 1), lanes] = s[CHUNKS - 1 :, :]
        return carry

    lax.fori_loop(0, width // LANES, lane, 0)


def second_pass(rows, normed_ref, init_ref, f1_ref, f2_ref, keep_ref, flag_ref, al_ref, de_ref, be_ref, eta_ref, om_ref, wz_ref, wu_ref, qg_ref, qb_ref, kg_ref, mask_ref, pre_ref, mixed_ref, zpre_ref, gate_ref, probs_ref, dec_ref, drv_ref):
    rate_tables(al_ref, de_ref, be_ref, dec_ref, drv_ref)
    dims, width = al_ref.shape
    tokens = keep_ref.shape[0]
    length = tokens // rows
    steps = length // CHUNKS

    def lane(j, carry):
        lanes = pl.ds(pl.multiple_of(j * LANES, LANES), LANES)
        omega = bcast(om_ref, 0, lanes)
        for row in range(rows):
            base = j * tokens + row * length
            token = steps_of(normed_ref, base, steps)
            kept = steps_of(keep_ref, row * length, steps)
            reach = shifted(product(kept), 1, 1.0)
            for by in (1, 2, 4):
                reach = reach * shifted(reach, by, 1.0)
            flag = bcast(flag_ref, row, pl.ds(0, LANES))
            total = [omega * t for t in token]
            for n in range(dims):
                d, b, e = bcast(dec_ref, n, lanes), bcast(drv_ref, n, lanes), bcast(eta_ref, n, lanes)
                chunk = power(d, steps)
                entering = bcast(f1_ref, row * dims + n, lanes) + (
                    power(chunk, CHUNKS) * flag
                ) * bcast(f2_ref, row * dims + n, lanes)
                s = (
                    init_ref[pl.ds((row * dims + n) * CHUNKS, CHUNKS), lanes]
                    + reach * chunk_powers(chunk, 1) * entering
                )
                for k in range(steps):
                    s = (kept[k] * d) * s + b * token[k]
                    total[k] = total[k] + e * s
            for k in range(steps):
                pre_ref[pl.ds(base + k, CHUNKS, stride=steps), :] = total[k]
        return carry

    lax.fori_loop(0, width // LANES, lane, 0)
    mixed_low = from_slabs(silu(pre_ref[...]).astype(LOW), tokens)
    mixed_ref[...] = mixed_low
    z_pre = dot(mixed_low, wz_ref[...])
    zpre_ref[...] = z_pre
    gate_ref[...] = jax.nn.sigmoid(dot(mixed_low, wu_ref[...]))
    z_low = silu(z_pre).astype(LOW).astype(F32)
    queries = (z_low * qg_ref[...] + qb_ref[...]).astype(LOW)
    keys = (z_low * kg_ref[...]).astype(LOW)
    for start in range(0, z_low.shape[0], STRETCH):
        block = slice(start, start + STRETCH)
        scores = dot_cols(queries[block], keys[block]) * z_low.shape[1] ** (-0.5)
        scores = jnp.where(mask_ref[block, :] > 0.5, scores, -1e30)
        shift = jnp.exp(scores - jnp.max(scores, -1, keepdims=True))
        probs_ref[block, :] = shift / jnp.sum(shift, -1, keepdims=True)


def value_part(normed_ref, mixed_ref, probs_ref, va_ref, ra_ref, vb_ref, rb_ref, vpre_ref, rpre_ref, att_ref, united_ref):
    tokens = normed_ref.shape[0]
    for i, (v_ref, r_ref) in enumerate(((va_ref, ra_ref), (vb_ref, rb_ref))):
        value_pre = dot(normed_ref[...], v_ref[...])
        reset_pre = dot(mixed_ref[...], r_ref[...])
        vpre_ref[i] = value_pre
        rpre_ref[i] = reset_pre
        values = silu(value_pre).astype(LOW)
        for start in range(0, tokens, STRETCH):
            block = slice(start, start + STRETCH)
            att_ref[i, block, :] = dot(probs_ref[block, :].astype(LOW), values[block])
        united_ref[i] = (silu(reset_pre) * att_ref[i]).astype(LOW)


def blend_part(offs_ref, x_ref, mixed_ref, gate_ref, u0_ref, u1_ref, ga_ref, gb_ref, gain_ref, hpre_ref, blended_ref, second_ref, whid_ref):
    cols = whid_ref.shape[0] // 4
    for r in range(4):
        whid_ref[pl.ds(pl.multiple_of(offs_ref[r], 64), cols), :] = (ga_ref, gb_ref)[r % 2][r // 2, :cols, :]
    hidden_pre = dot(mixed_ref[...], whid_ref[...])
    for r in range(4):
        united = (u0_ref, u1_ref)[r // 2][r % 2]
        hidden_pre = hidden_pre + dot(united, (ga_ref, gb_ref)[r % 2][r // 2, cols:, :])
    hpre_ref[...] = hidden_pre
    x = x_ref[...].astype(F32)
    blended = x + gate_ref[...] * (silu(hidden_pre) - x)
    blended_ref[...] = blended
    hat, _ = norm_parts(blended)
    second_ref[...] = (hat * gain_ref[...]).astype(LOW)


def ffn_part(second_ref, cot_ref, ia_ref, ib_ref, oa_ref, ob_ref, out_ref, sg_ref, keep_ref, send_ref):
    second, cot = second_ref[...], cot_ref[...]
    depth, units = ia_ref.shape
    half = depth // 2
    for i, (in_ref, fo_ref, pack_ref) in enumerate(
        ((ia_ref, oa_ref, keep_ref), (ib_ref, ob_ref, send_ref))
    ):
        up_pre = dot(second, in_ref[...])
        activated = silu(up_pre).astype(LOW)
        up_grad = (dot_cols(cot, fo_ref[...]) * silu_slope(up_pre)).astype(LOW)
        out = dot(activated, fo_ref[...])
        back = dot_cols(up_grad, in_ref[...])
        out_ref[...] = out if i == 0 else out_ref[...] + out
        sg_ref[...] = back if i == 0 else sg_ref[...] + back
        kind = pack_ref.dtype
        pack_ref[:depth, :] = dot_rows(second, up_grad).astype(kind)
        for h in range(2):
            pack_ref[depth + h * units : depth + (h + 1) * units, :] = dot_rows(
                activated, cot[:, h * half : (h + 1) * half]
            ).astype(kind)


def blend_back(offs_ref, x_ref, cot_ref, blended_ref, s0_ref, s1_ref, o0_ref, o1_ref, hpre_ref, gate_ref, mixed_ref, gain_ref, wu_ref, whid_ref, y_ref, direct_ref, hidden_ref, mg_ref, gg_ref, keep_ref, send_ref, full_ref):
    blended = blended_ref[...]
    y_ref[...] = (blended + (o0_ref[...] + o1_ref[...])).astype(LOW)
    second_grad = s0_ref[...] + s1_ref[...]
    hat, scale = norm_parts(blended)
    gg_ref[...] = jnp.sum(second_grad * hat, 0, keepdims=True)
    grad = cot_ref[...].astype(F32) + norm_back(second_grad * gain_ref[...], hat, scale)
    gate, hidden_pre, x = gate_ref[...], hpre_ref[...], x_ref[...].astype(F32)
    direct_ref[...] = grad * (1.0 - gate)
    hidden_low = (grad * gate * silu_slope(hidden_pre)).astype(LOW)
    gate_low = (grad * (silu(hidden_pre) - x) * gate * (1.0 - gate)).astype(LOW)
    hidden_ref[...] = hidden_low
    mg_ref[...] = dot_cols(gate_low, wu_ref[...]) + dot_cols(hidden_low, whid_ref[...])
    width = x.shape[1]
    cols, half = width // 4, width // 2
    for i, low in enumerate((gate_low, hidden_low)):
        full_ref[...] = dot_rows(mixed_ref[...], low)
        for r in range(4):
            pack_ref = (keep_ref, send_ref)[r % 2]
            rows = pl.ds(pl.multiple_of(offs_ref[r], 64), cols)
            for h in range(2):
                at = (2 * i + h) * cols
                pack_ref[r // 2, at : at + cols, :] = full_ref[
                    rows, h * half : (h + 1) * half
                ].astype(pack_ref.dtype)


def value_back(part, hidden_ref, normed_ref, mixed_ref, probs_ref, vpre_ref, rpre_ref, att_ref, united_ref, ga_ref, gb_ref, va_ref, ra_ref, vb_ref, rb_ref, ng_ref, mg_ref, pg_ref, *packs):
    hidden, normed, mixed = hidden_ref[...], normed_ref[...], mixed_ref[...]
    tokens, depth = hidden.shape
    units = va_ref.shape[1]
    cols = ga_ref.shape[1] - units
    half = depth // 2
    for i, (g_ref, v_ref, r_ref, pack) in enumerate(
        ((ga_ref, va_ref, ra_ref, packs[:2]), (gb_ref, vb_ref, rb_ref, packs[2:]))
    ):
        gate_pack, value_pack = pack
        kind = gate_pack.dtype
        united_grad = dot_cols(hidden, g_ref[part, cols:, :])
        reset_pre, value_pre = rpre_ref[i], vpre_ref[i]
        reset_low = (united_grad * att_ref[i] * silu_slope(reset_pre)).astype(LOW)
        attended_low = (united_grad * silu(reset_pre)).astype(LOW)
        values = silu(value_pre).astype(LOW)
        parts = []
        for start in range(0, tokens, STRETCH):
            block = slice(start, start + STRETCH)
            parts.append(dot_rows(probs_ref[block, :].astype(LOW), attended_low[block]))
            back = dot_cols(attended_low[block], values[block])
            first = i == 0 and part == 1
            pg_ref[block, :] = back if first else pg_ref[block, :] + back
        value_low = (jnp.concatenate(parts, 0) * silu_slope(value_pre)).astype(LOW)
        into_normed = dot_cols(value_low, v_ref[...])
        into_mixed = dot_cols(reset_low, r_ref[...])
        first = i == 0 and part == 1
        ng_ref[...] = into_normed if first else ng_ref[...] + into_normed
        mg_ref[...] = into_mixed if first else mg_ref[...] + into_mixed
        gate_pack[part, :depth, :] = dot_rows(mixed, reset_low).astype(kind)
        for h in range(2):
            gate_pack[part, depth + h * units : depth + (h + 1) * units, :] = dot_rows(
                united_ref[i], hidden[:, h * half : (h + 1) * half]
            ).astype(kind)
        value_pack[part] = dot_rows(normed, value_low).astype(kind)


def third_pass(rows, zpre_ref, probs_ref, p_ref, qg_ref, qb_ref, kg_ref, wz_ref, mixed_ref, m0_ref, m1_ref, pre_ref, keep_ref, al_ref, de_ref, pg_ref, dz_ref, small_ref, im_ref, iv_ref, lm_ref, lv_ref, qk_ref):
    z_pre = zpre_ref[...]
    z_low = silu(z_pre).astype(LOW).astype(F32)
    queries = (z_low * qg_ref[...] + qb_ref[...]).astype(LOW)
    keys = (z_low * kg_ref[...]).astype(LOW)
    for start in range(0, z_low.shape[0], STRETCH):
        block = slice(start, start + STRETCH)
        probs = probs_ref[block, :]
        grad = p_ref[block, :]
        grad = probs * (grad - jnp.sum(probs * grad, -1, keepdims=True)) * z_low.shape[1] ** (-0.5)
        high = grad.astype(LOW)
        rest = (grad - high.astype(F32)).astype(LOW)
        qk_ref[0, block, :] = dot(high, keys[block]) + dot(rest, keys[block])
        qk_ref[1, block, :] = dot_rows(high, queries[block]) + dot_rows(rest, queries[block])
    query_grad, key_grad = qk_ref[0], qk_ref[1]
    small_ref[...] = jnp.zeros_like(small_ref)
    small_ref[0:1, :] = jnp.sum(query_grad * z_low, 0, keepdims=True)
    small_ref[1:2, :] = jnp.sum(query_grad, 0, keepdims=True)
    small_ref[2:3, :] = jnp.sum(key_grad * z_low, 0, keepdims=True)
    z_grad = ((query_grad * qg_ref[...] + key_grad * kg_ref[...]) * silu_slope(z_pre)).astype(LOW)
    dz_ref[...] = dot_rows(mixed_ref[...], z_grad)
    mixed_grad = m0_ref[...] + m1_ref[...] + dot_cols(z_grad, wz_ref[...])
    into_slabs(pg_ref, mixed_grad)
    pg_ref[...] = pg_ref[...] * silu_slope(pre_ref[...])
    dims, width = al_ref.shape
    tokens = z_pre.shape[0]
    length = tokens // rows
    steps = length // CHUNKS

    def lane(j, carry):
        lanes = pl.ds(pl.multiple_of(j * LANES, LANES), LANES)
        for row in range(rows):
            token = steps_of(pg_ref, j * tokens + row * length, steps)
            kept = steps_of(keep_ref, row * length, steps)
            whole = product(kept)
            for n in range(dims):
                alpha = jax.nn.sigmoid(bcast(al_ref, n, lanes))
                d = 1.0 - alpha * jax.nn.sigmoid(bcast(de_ref, n, lanes))
                mu = token[steps - 1]
                m = (kept[steps - 1] * d) * mu
                v = kept[steps - 1] * mu
                for k in range(steps - 2, -1, -1):
                    mu = token[k] + m
                    rate = kept[k] * d
                    m = rate * mu
                    v = kept[k] * mu + rate * v
                a = power(d, steps) * whole
                b = steps * power(d, steps - 1) * whole
                for by in (-1, -2, -4):
                    mp, vp = shifted(m, by, 0.0), shifted(v, by, 0.0)
                    ap, bp = shifted(a, by, 1.0), shifted(b, by, 0.0)
                    v = v + a * vp + b * mp
                    m = m + a * mp
                    b = a * bp + b * ap
                    a = a * ap
                at = pl.ds((row * dims + n) * CHUNKS, CHUNKS)
                im_ref[at, lanes] = shifted(m, -1, 0.0)
                iv_ref[at, lanes] = shifted(v, -1, 0.0)
                lm_ref[pl.ds(row * dims + n, 1), lanes] = m[0:1, :]
                lv_ref[pl.ds(row * dims + n, 1), lanes] = v[0:1, :]
        return carry

    lax.fori_loop(0, width // LANES, lane, 0)


def back_pass(rows, *refs):
    offs_ref, x_ref, cot_ref, blended_ref, s0_ref, s1_ref, o0_ref, o1_ref, hpre_ref, gate_ref = refs[:10]
    mixed_ref, gain_ref, wu_ref, whid_ref, normed_ref, probs_ref = refs[10:16]
    own_part, far_part, (ga_ref, gb_ref), weights = refs[16:20], refs[20:24], refs[24:26], refs[26:34]
    zpre_ref, qg_ref, qb_ref, kg_ref, wz_ref, pre_ref, keep_ref, al_ref, de_ref = refs[34:43]
    y_ref, direct_ref, gg_ref, pair_keep_ref, pair_send_ref, ng_ref = refs[43:49]
    packs, outs = refs[49:53], refs[53:59]
    mg_ref, p_ref, qk_ref, m0_ref, full_ref, hidden_ref, dz_ref = refs[59:]
    blend_back(
        offs_ref, x_ref, cot_ref, blended_ref, s0_ref, s1_ref, o0_ref, o1_ref, hpre_ref, gate_ref,
        mixed_ref, gain_ref, wu_ref, whid_ref, y_ref, direct_ref, hidden_ref, m0_ref, gg_ref,
        pair_keep_ref, pair_send_ref, full_ref,
    )
    for part, parts in ((1, far_part), (0, own_part)):
        value_back(
            part, hidden_ref, normed_ref, mixed_ref, probs_ref, *parts, ga_ref, gb_ref,
            *weights[4 * part : 4 * part + 4], ng_ref, mg_ref, p_ref, *packs,
        )
    third_pass(
        rows, zpre_ref, probs_ref, p_ref, qg_ref, qb_ref, kg_ref, wz_ref, mixed_ref, m0_ref,
        mg_ref, pre_ref, keep_ref, al_ref, de_ref, outs[0], dz_ref, *outs[1:], qk_ref,
    )
    width, zd = dz_ref.shape
    blocks, cols = width // (2 * zd), width // 4
    share = cols // blocks
    for r in range(4):
        pack_ref = (pair_keep_ref, pair_send_ref)[r % 2]
        for c in range(blocks):
            rows_at = pl.ds(pl.multiple_of(offs_ref[r] + c * share, 64), share)
            pack_ref[r // 2, 4 * cols : 4 * cols + share, c * zd : (c + 1) * zd] = dz_ref[
                rows_at, :
            ].astype(pack_ref.dtype)
        pack_ref[r // 2, 4 * cols + share :, :] = jnp.zeros((share, width // 2), pack_ref.dtype)


def fourth_pass(rows, pg_ref, normed_ref, im_ref, iv_ref, near_ref, far_ref, keep_ref, flag_ref, al_ref, de_ref, be_ref, eta_ref, om_ref, n0_ref, x_ref, g_ref, direct_ref, gg_ref, qk_ref, xg_ref, sums_ref, dec_ref, drv_ref, ng_ref):
    rate_tables(al_ref, de_ref, be_ref, dec_ref, drv_ref)
    dims, width = al_ref.shape
    tokens = keep_ref.shape[0]
    length = tokens // rows
    steps = length // CHUNKS
    span = rows * dims
    sums_ref[...] = jnp.zeros_like(sums_ref)

    def lane(j, carry):
        lanes = pl.ds(pl.multiple_of(j * LANES, LANES), LANES)
        omega = bcast(om_ref, 0, lanes)
        for row in range(rows):
            base = j * tokens + row * length
            grad = steps_of(pg_ref, base, steps)
            token = steps_of(normed_ref, base, steps)
            kept = steps_of(keep_ref, row * length, steps)
            reach = shifted(product(kept), -1, 1.0)
            for by in (-1, -2, -4):
                reach = reach * shifted(reach, by, 1.0)
            place = lax.broadcasted_iota(jnp.int32, (CHUNKS, LANES), 0)
            later = (steps * (CHUNKS - 1 - place)).astype(F32)
            flag = bcast(flag_ref, row, pl.ds(0, LANES))
            total = [omega * t for t in grad]
            for n in range(dims):
                d, b, e = bcast(dec_ref, n, lanes), bcast(drv_ref, n, lanes), bcast(eta_ref, n, lanes)
                chunk = power(d, steps)
                inverse = 1.0 / d
                part = power(chunk, CHUNKS) * flag
                slope = (float(length) * part) * inverse
                at = row * dims + n
                m2 = bcast(far_ref, at, lanes)
                m_in = bcast(near_ref, at, lanes) + part * m2
                v_in = bcast(near_ref, span + at, lanes) + part * bcast(far_ref, span + at, lanes) + slope * m2
                through = reach * chunk_powers(chunk, -1)
                at = pl.ds(at * CHUNKS, CHUNKS)
                m = im_ref[at, lanes] + through * m_in
                v = iv_ref[at, lanes] + through * v_in + (later * through * inverse) * m_in
                coef = e * b
                sum_m = jnp.zeros((CHUNKS, LANES), F32)
                sum_v = jnp.zeros((CHUNKS, LANES), F32)
                for k in range(steps - 1, -1, -1):
                    mu = grad[k] + m
                    sum_m = sum_m + token[k] * mu
                    sum_v = sum_v + token[k] * v
                    total[k] = total[k] + coef * mu
                    rate = kept[k] * d
                    m = rate * mu
                    v = kept[k] * mu + rate * v
                sums_ref[pl.ds(n, 1), lanes] += jnp.sum(sum_m, 0, keepdims=True)
                sums_ref[pl.ds(dims + n, 1), lanes] += jnp.sum(sum_v, 0, keepdims=True)
            for k in range(steps):
                ng_ref[pl.ds(base + k, CHUNKS, stride=steps), :] = total[k]
        return carry

    lax.fori_loop(0, width // LANES, lane, 0)
    normed_grad = from_slabs(ng_ref[...], tokens) + n0_ref[...]
    hat, scale = norm_parts(x_ref[...].astype(F32))
    at = 2 * dims
    for j in range(width // LANES):
        slab = slice(j * tokens, (j + 1) * tokens)
        sums_ref[at : at + 1, j * LANES : (j + 1) * LANES] = jnp.sum(
            pg_ref[slab, :] * normed_ref[slab, :], 0, keepdims=True
        )
    sums_ref[at + 1 : at + 2, :] = jnp.sum(normed_grad * hat, 0, keepdims=True)
    sums_ref[at + 2 : at + 3, :] = gg_ref[...]
    zd = qk_ref.shape[1]
    for i in range(3):
        sums_ref[at + 3 : at + 4, i * zd : (i + 1) * zd] = qk_ref[i : i + 1, :]
    xg_ref[...] = (direct_ref[...] + norm_back(normed_grad * g_ref[...], hat, scale)).astype(LOW)


def swap(x, axis, bit):
    size = lax.axis_size(axis)
    return lax.ppermute(x, axis, [(i, i ^ bit) for i in range(size)])


def shift(x, by):
    size = lax.axis_size("tensor")
    return lax.ppermute(
        x, "tensor", [(i, i + by) for i in range(size) if 0 <= i + by < size]
    )


def pick(first, pair):
    return jnp.where(first, *pair)


def split_rows(v):
    half = v.shape[0] // 2
    return v[:half], v[half:]


def joined(mine, other, first):
    return pick(
        first, (jnp.concatenate([mine, other], 0), jnp.concatenate([other, mine], 0))
    )


tied = lax.optimization_barrier


def rounded(v):
    return lax.reduce_precision(v, 8, 7)


def halves(v, first):
    low, high = split_rows(v)
    return pick(first, (low, high)), pick(first, (high, low)).astype(LOW)


def reduction(kind, packs, firsts):
    bits = [1 << b for b in range(lax.axis_size("dp").bit_length() - 1)]
    lead, spread, rest = {
        "x": ([1], [2], []),
        "z": ([2], [1], []),
        "y": ([], [1, 2], []),
        "w": ([], [2, 1], []),
        "X": ([1], [], [2]),
        "Z": ([2], [], [1]),
        "Y": ([], [1], [2]),
        "W": ([], [2], [1]),
    }[kind]
    near, far = yield from packs
    for bit in lead:
        near, away = halves(near, firsts[bit])
        far, far_away = halves(far, firsts[bit])
        got = yield "dp", bit, jnp.concatenate([away, far_away], 0)
        got = got.astype(F32)
        near, far = near + got[: near.shape[0]], far + got[near.shape[0] :]
    got = yield "tensor", 2, far.astype(LOW)
    total = near + got.astype(F32)
    for bit in spread:
        total, away = halves(total, firsts[bit])
        got = yield "dp", bit, away
        total = total + got.astype(F32)
    for bit in rest + bits[2:]:
        total = rounded(total)
        got = yield "dp", bit, total.astype(LOW)
        total = total + got.astype(F32)
    low = total.astype(LOW)
    for bit in reversed(lead + spread):
        got = yield "dp", bit, low
        low = joined(low, got, firsts[bit])
    return low


def one_swap(axis, bit, v):
    got = yield axis, bit, v
    return got


def everywhere(v):
    size = v.shape[0]
    for axis in ("tensor", "dp"):
        for b in range(lax.axis_size(axis).bit_length() - 1):
            high = rounded(v)
            low = rounded(v - high)
            got = yield axis, 1 << b, jnp.concatenate([high, low], 0).astype(LOW)
            got = got.astype(F32)
            v = (high + low) + (got[:size] + got[size:])
    return v


class Pump:
    def __init__(self, token):
        self.token = token
        self.flows, self.ready, self.flying, self.done = {}, {}, {}, {}

    def gate(self, v):
        v, self.token = tied((v, self.token))
        return v

    def add(self, name, flow):
        self.flows[name] = flow
        self.ready[name] = next(flow)

    def issue(self, name):
        axis, bit, v = self.ready.pop(name)
        self.flying[name] = swap(self.gate(v), axis, bit)

    def finish(self, name):
        got = self.gate(self.flying.pop(name))
        try:
            self.ready[name] = self.flows[name].send(got)
        except StopIteration as end:
            self.done[name] = end.value

    def drain(self):
        while self.ready or self.flying:
            for name in list(self.ready):
                self.issue(name)
            for name in list(self.flying):
                self.finish(name)


def side_by_side(pack):
    half = pack.shape[0] // 2
    return jnp.concatenate([pack[:half], pack[half:]], 1)


def shards(
    layer_input,
    doc_lengths,
    norm1_gain,
    alpha_raw,
    delta_raw,
    ema_beta,
    ema_eta,
    ema_omega,
    w_z,
    q_gain,
    q_bias,
    k_gain,
    w_value,
    w_reset,
    w_update,
    w_hidden,
    w_out,
    norm2_gain,
    w_ffn_in,
    w_ffn_out,
    cotangent,
):
    member = lax.axis_index("tensor")
    place = lax.axis_index("dp")
    layer_input, begin, offs, *firsts = tied(
        (
            layer_input,
            member * layer_input.shape[1],
            (member ^ jnp.arange(4, dtype=jnp.int32)) * w_hidden.shape[0],
            (place & 1) == 0,
            (place & 2) == 0,
            (member & 1) == 0,
            (member & 2) == 0,
        )
    )
    first_core, first_chip = firsts[2:]
    firsts = dict(zip((1, 2), firsts[:2], strict=True))
    rows, length, width = layer_input.shape
    tokens = rows * length
    dims = alpha_raw.shape[0]
    zd = w_z.shape[1]
    units = w_value.shape[1]
    cols = w_hidden.shape[0]
    x = layer_input.reshape(tokens, width)
    cot = cotangent.reshape(tokens, width)
    g1, g2, om = norm1_gain[None], norm2_gain[None], ema_omega[None]
    qg, qb, kg = q_gain[None], q_bias[None], k_gain[None]

    docs = doc_lengths.shape[1]
    order = jnp.arange(docs)
    ends = jnp.sum(
        jnp.where(order[:, None] <= order[None, :], doc_lengths[:, :, None], 0), 1
    ).astype(jnp.int32)
    starts = ends - doc_lengths
    starts, ends = starts - begin, ends - begin
    places = jnp.arange(length, dtype=jnp.int32)
    docid = jnp.sum((places[None, :, None] >= ends[:, None, :]).astype(jnp.int32), 2)
    keep = 1.0 - jnp.any(places[None, :, None] == starts[:, None, :], 2).astype(F32)
    keep = jnp.broadcast_to(keep.reshape(tokens, 1), (tokens, LANES))
    blocks = docid.reshape(tokens // STRETCH, STRETCH)
    spot = jnp.arange(STRETCH)
    mask = (spot[None, :] <= spot[:, None])[None] & (blocks[:, :, None] == blocks[:, None, :])
    mask = mask.astype(F32).reshape(tokens, STRETCH)

    def unbroken(part):
        low, high = part * length, (part + 1) * length
        inside = jnp.any((starts >= low) & (starts < high), 1)
        return jnp.broadcast_to(1.0 - inside.astype(F32)[:, None], (rows, LANES))

    vm = lambda shape: pltpu.VMEM(shape, F32)
    tab = (dims, width)
    wide = (tokens, width)
    mat = 2.0 * tokens * width
    ema = 8.0 * tokens * width * dims
    chunked = (rows * dims * CHUNKS, width)
    finals = (rows * dims, width)
    slabs = (tokens * width // LANES, LANES)

    w_join = jnp.concatenate([w_hidden, w_out], 0)
    shares = (w_value, w_reset, w_join, w_ffn_in, w_ffn_out)
    bits = (1, 1, 2, 1, 1)
    pump = Pump(offs)
    beside = [swap(w, "tensor", 1) for w in (w_value, w_reset, w_ffn_in, w_ffn_out)]
    half_v, half_r, half_g, half_i, half_o = (
        pick(firsts[bit], split_rows(w)) for w, bit in zip(shares, bits, strict=True)
    )

    over_v = swap(half_v, "tensor", 2)
    beside = [pump.gate(w) for w in beside]
    over_r = swap(pump.gate(half_r), "tensor", 2)
    x = pump.gate(x)

    normed, normed_low, init, last = call(
        functools.partial(first_pass, rows),
        [(slabs, F32), (wide, LOW), (chunked, F32), (finals, F32)],
        (x, g1, alpha_raw, delta_raw, ema_beta, keep),
        ema,
        [vm(tab), vm(tab)],
    )
    last = pump.gate(last)
    over_v = pump.gate(over_v)
    other_v = swap(over_v, "dp", 1)
    f1, f2 = shift(last, 1), shift(last, 2)
    over_r = pump.gate(over_r)
    other_r = swap(over_r, "dp", 1)
    f1, f2 = pump.gate(f1), pump.gate(f2)
    over_g = swap(pump.gate(half_g), "tensor", 2)
    half_i = pump.gate(half_i)
    pre, mixed_low, z_pre, gate, probs = call(
        functools.partial(second_pass, rows),
        [(slabs, F32), (wide, LOW), ((tokens, zd), F32), (wide, F32), ((tokens, STRETCH), F32)],
        (normed, init, f1, f2, keep, unbroken(-1), alpha_raw, delta_raw, ema_beta,
         ema_eta, om, w_z, w_update, qg, qb, kg, mask),
        ema + mat * width,
        [vm(tab), vm(tab)],
    )
    split = (2, tokens, units)
    mixed_low = pump.gate(mixed_low)
    over_i = swap(half_i, "tensor", 2)
    other_v = pump.gate(other_v)
    mixed_low = pump.gate(mixed_low)

    def values(weights):
        return call(
            value_part,
            [(split, F32), (split, F32), (split, F32), (split, LOW)],
            (normed_low, mixed_low, probs, *weights),
            4 * mat * units,
        )

    own_part = values((w_value, w_reset, beside[0], beside[1]))
    united0 = pump.gate(own_part[3])
    other_r = pump.gate(other_r)
    over_g, over_i = pump.gate(over_g), pump.gate(over_i)
    over_g, over_i, half_o = pump.gate(over_g), pump.gate(over_i), pump.gate(half_o)
    over_o = swap(half_o, "tensor", 2)
    other_g = swap(over_g, "dp", 2)
    other_i = swap(over_i, "dp", 1)
    other_v, other_r = pump.gate(other_v), pump.gate(other_r)
    full_v = pump.gate(joined(over_v, other_v, firsts[1]))
    both_v = swap(full_v, "tensor", 1)
    full_r = pump.gate(joined(over_r, other_r, firsts[1]))
    both_r = swap(full_r, "tensor", 1)
    both_v, both_r = pump.gate(both_v), pump.gate(both_r)
    full_v = pump.gate(full_v)
    far_part = values((full_v, full_r, both_v, both_r))
    united1 = pump.gate(far_part[3])
    over_o = pump.gate(over_o)
    other_i = pump.gate(other_i)
    other_o = swap(over_o, "dp", 1)
    other_g = pump.gate(other_g)
    near_g = pump.gate(jnp.stack([w_join, joined(over_g, other_g, firsts[2])]))
    beside_g = swap(near_g, "tensor", 1)
    full_i = pump.gate(joined(over_i, other_i, firsts[1]))
    both_i = swap(full_i, "tensor", 1)
    beside_g = pump.gate(beside_g)
    wg = (near_g, beside_g)
    wv, wr = (w_value, beside[0], full_v, both_v), (w_reset, beside[1], full_r, both_r)
    kept_parts = ((*own_part[:3], united0), (*far_part[:3], united1))
    hidden_pre, blended, second, whid = call(
        blend_part,
        [(wide, F32), (wide, F32), (wide, LOW), ((width, width), LOW)],
        (offs, x, mixed_low, gate, united0, united1, *wg, g2),
        mat * (width + 4 * units),
        smem=(0,),
    )
    second = pump.gate(second)
    ffn_rows = width + 2 * units

    def ffn_of(weights):
        return call(
            ffn_part,
            [(wide, F32), (wide, F32), ((ffn_rows, units), LOW), ((ffn_rows, units), LOW)],
            (second, cot, *weights),
            12 * mat * units,
        )

    ffn0 = ffn_of((w_ffn_in, beside[2], w_ffn_out, beside[3]))
    back0 = pump.gate(ffn0[1])
    other_o = pump.gate(other_o)
    full_o = pump.gate(joined(over_o, other_o, firsts[1]))
    both_o = swap(full_o, "tensor", 1)
    both_i, both_o = pump.gate(both_i), pump.gate(both_o)
    ffn1 = ffn_of((full_i, both_i, full_o, both_o))
    pump.add("F0", one_swap("tensor", 1, ffn0[3]))
    pump.add("F1", one_swap("tensor", 1, ffn1[3]))
    share = cols * zd // (width // 2)
    own = (2, 4 * cols + 2 * share, width // 2)
    held = {}

    def run_back():
        outs = call(
            functools.partial(back_pass, rows),
            [(wide, LOW), (wide, F32), ((1, width), F32), (own, LOW), (own, LOW), (wide, F32),
             *[((2, 2 * width, units), LOW), ((2, width, units), LOW)] * 2,
             (slabs, F32), ((8, zd), F32), (chunked, F32), (chunked, F32), (finals, F32), (finals, F32)],
            (offs, x, cot, pump.gate(blended), ffn1[1], back0, ffn0[0], ffn1[0], hidden_pre, gate,
             mixed_low, g2, w_update, whid, normed_low, probs, *kept_parts[0], *kept_parts[1], *wg,
             wv[0], wr[0], wv[1], wr[1], wv[2], wr[2], wv[3], wr[3],
             z_pre, qg, qb, kg, w_z, pre, keep, alpha_raw, delta_raw),
            (4 * width + 28 * units) * mat,
            [vm(wide), vm((tokens, STRETCH)), vm((2, tokens, zd)), vm(wide), vm((width, width)),
             pltpu.VMEM(wide, LOW), vm((width, zd))],
            smem=(0,),
        )
        held["bb"], held["v"] = outs[:5], outs[5:10]
        held["t3"] = list(outs[10:])
        pump.token, held["t3"][4] = tied((pump.token, held["t3"][4]))

    def send_back():
        back = pump.gate(jnp.concatenate([held["t3"][4], held["t3"][5]], 0))
        held["back"] = shift(back, -1), shift(back, -2)

    def take_back():
        held["back"] = [pump.gate(v) for v in held["back"]]

    def run_fourth():
        t3 = held["t3"]
        held["t4"] = call(
            functools.partial(fourth_pass, rows),
            [(wide, LOW), ((2 * dims + 8, width), F32)],
            (t3[0], normed, t3[2], t3[3], *held["back"], keep, unbroken(1), alpha_raw,
             delta_raw, ema_beta, ema_eta, om, held["v"][0], x, g1, held["bb"][1],
             held["bb"][2], t3[1]),
            2 * ema,
            [vm(tab), vm(tab), vm(slabs)],
        )
        sums = pump.gate(held["t4"][1])
        sums = jnp.concatenate([sums[:, at : at + LANES] for at in range(0, width, LANES)], 0)
        pump.add("sm", everywhere(sums))

    def packs_of(name):
        if name in "IU":
            rows_of = slice(0, width) if name == "I" else slice(width, 2 * width)
            return tuple(
                keep[rows_of].astype(F32) + pump.done[swapped][rows_of].astype(F32)
                for keep, swapped in ((ffn0[2], "F0"), (ffn1[2], "F1"))
            )
        kept, sent = held["bb"][3:] if name == "P" else held["v"]["QN".index(name) + 1 : 5 : 2]
        got = yield "tensor", 1, sent
        both = kept.astype(F32) + got.astype(F32)
        return both[0], both[1]

    def with_shared():
        low = yield from reduction(KINDS["P"], packs_of("P"), firsts)
        v = jnp.concatenate([low[: 2 * cols], low[4 * cols : 4 * cols + share]], 0)
        for bit, first in ((2, first_chip), (1, first_core)):
            got = yield "tensor", bit, v
            v = joined(v, got, first)
        v = v.reshape(2, 2, 2 * cols + share, width // 2)
        return low[2 * cols : 4 * cols], [v[core, chip] for chip in range(2) for core in range(2)]

    def add_flow(name):
        pump.add(
            name, with_shared() if name == "P" else reduction(KINDS[name], packs_of(name), firsts)
        )

    kernels = {
        "back": run_back,
        "t4": run_fourth,
    }
    for word in ORDER:
        sign, name = word[0], word[1:]
        if sign == "K":
            kernels[name]()
        elif name == "E":
            (send_back if sign == "+" else take_back)()
        elif sign == "+":
            if name in KINDS and name not in pump.flows:
                add_flow(name)
            pump.issue(name)
        else:
            pump.finish(name)
    pump.drain()
    output, input_grad = held["bb"][0], held["t4"][0]
    sums = from_slabs(pump.done["sm"], 2 * dims + 8)
    pair_sum, gate_sum, value_sum, in_sum, fout_sum = (pump.done[n] for n in "PQNIU")

    alpha, sigma = jax.nn.sigmoid(alpha_raw), jax.nn.sigmoid(delta_raw)
    with_mu, with_nu = sums[:dims], sums[dims : 2 * dims]
    drive_grad = ema_eta * with_mu
    decay_grad = ema_eta * (alpha * ema_beta) * with_nu
    at = 2 * dims
    hidden_sum, shared = pair_sum
    update_grad = jnp.concatenate([side_by_side(v[: 2 * cols]) for v in shared], 0)
    dz_sum = jnp.concatenate(
        [v[2 * cols :, at : at + zd] for v in shared for at in range(0, width // 2, zd)], 0
    )
    return (
        output.reshape(layer_input.shape),
        input_grad.reshape(layer_input.shape),
        sums[at + 1],
        (ema_beta * drive_grad - sigma * decay_grad) * alpha * (1.0 - alpha),
        -alpha * decay_grad * sigma * (1.0 - sigma),
        alpha * drive_grad,
        (alpha * ema_beta) * with_mu,
        sums[at],
        dz_sum.astype(F32),
        sums[at + 3, :zd],
        sums[at + 3, zd : 2 * zd],
        sums[at + 3, 2 * zd : 3 * zd],
        value_sum.astype(F32),
        gate_sum[:width].astype(F32),
        update_grad.astype(F32),
        side_by_side(hidden_sum).astype(F32),
        side_by_side(gate_sum[width:]).astype(F32),
        sums[at + 2],
        in_sum.astype(F32),
        side_by_side(fout_sum).astype(F32),
    )


def solution(mesh):
    whole, by_row = P(), P("dp", "tensor", None)
    by_col, by_unit = P(None, "tensor"), P("tensor", None)
    return jax.shard_map(
        shards,
        mesh=mesh,
        in_specs=(by_row, P("dp", None), *(whole,) * 10, by_col, by_col, whole, by_unit, by_unit, whole, by_col, by_unit, by_row),
        out_specs=(by_row, by_row, *(whole,) * 10, by_col, by_col, whole, by_unit, by_unit, whole, by_col, by_unit),
        check_vma=False,
    )
```

```python
import functools

import jax
import jax.numpy as jnp
from jax import lax
from jax.experimental import pallas as pl
from jax.experimental.pallas import tpu as pltpu
from jax.sharding import PartitionSpec as P

STRETCH = 128
LANES = 128
CHUNKS = 8
F32 = jnp.float32
LOW = jnp.bfloat16
KINDS = {"I": "y", "U": "z", "Q": "x", "P": "z", "N": "Z"}
ORDER = (
    "+F0", "+F1", "-F0", "-F1", "+I", "+U", "Kback", "-I", "-U", "+P",
    "+Q", "+I", "+U", "-P", "+N", "+P", "-Q", "+Q", "-N", "-I",
    "+E", "-U", "+N", "-E", "-P", "+P", "Kt4", "-P", "-N", "-Q",
    "+P", "+Q", "+I", "+U", "-P", "+sm", "+P", "-sm", "-I", "+N",
    "-U", "+I", "-Q", "+Q", "+sm", "-P", "+P", "-N", "+U", "-I",
    "-sm", "+I", "-Q", "-P", "+Q", "+N", "-I", "-U", "+P", "+U",
    "+I", "-N", "+N", "-U", "+sm", "-Q", "-P", "+Q", "+P", "-I",
    "-sm", "+sm", "+U", "-Q", "-N", "+Q", "-sm", "-P", "+sm", "+N",
    "+P", "-U", "-P", "-sm", "-N", "-Q",
)


def silu(v):
    return v * jax.nn.sigmoid(v)


def silu_slope(v):
    s = jax.nn.sigmoid(v)
    return s * (1.0 + v * (1.0 - s))


def dot(a, b):
    return jnp.dot(a, b, preferred_element_type=F32)


def dot_rows(a, b):
    return lax.dot_general(a, b, (((0,), (0,)), ((), ())), preferred_element_type=F32)


def dot_cols(a, b):
    return lax.dot_general(a, b, (((1,), (1,)), ((), ())), preferred_element_type=F32)


def norm_parts(v):
    center = v - jnp.mean(v, -1, keepdims=True)
    scale = lax.rsqrt(jnp.mean(center * center, -1, keepdims=True) + 1e-05)
    return center * scale, scale


def norm_back(grad, hat, scale):
    return scale * (
        grad - jnp.mean(grad, -1, keepdims=True) - hat * jnp.mean(grad * hat, -1, keepdims=True)
    )


def call(kernel, outs, args, flops, scratch=(), smem=(), limit=12 << 20):
    specs = [
        pl.BlockSpec(memory_space=pltpu.SMEM if i in smem else pltpu.VMEM)
        for i in range(len(args))
    ]
    outs = [jax.ShapeDtypeStruct(s, d) for s, d in outs]
    size = sum(a.size * a.dtype.itemsize for a in args) + sum(
        o.size * o.dtype.itemsize for o in outs
    )
    return pl.pallas_call(
        kernel,
        out_shape=outs,
        in_specs=specs,
        out_specs=[pl.BlockSpec(memory_space=pltpu.VMEM) for _ in outs],
        scratch_shapes=list(scratch),
        compiler_params=pltpu.CompilerParams(vmem_limit_bytes=limit),
        cost_estimate=pl.CostEstimate(flops=int(flops), bytes_accessed=int(size), transcendentals=0),
    )(*args)


def bcast(ref, row, lanes):
    return jnp.broadcast_to(ref[pl.ds(row, 1), lanes], (CHUNKS, LANES))


def shifted(v, by, fill):
    place = lax.broadcasted_iota(jnp.int32, v.shape, 0)
    if by > 0:
        return jnp.where(place >= by, pltpu.roll(v, by, 0), fill)
    return jnp.where(place < CHUNKS + by, pltpu.roll(v, CHUNKS + by, 0), fill)


def power(v, n):
    out = None
    while n:
        if n & 1:
            out = v if out is None else out * v
        n >>= 1
        if n:
            v = v * v
    return out


def chunk_powers(base, order):
    place = lax.broadcasted_iota(jnp.int32, base.shape, 0)
    place = place if order > 0 else (CHUNKS - 1) - place
    out = jnp.where(place & 1 == 1, base, 1.0)
    base = base * base
    out = out * jnp.where(place & 2 == 2, base, 1.0)
    base = base * base
    return out * jnp.where(place & 4 == 4, base, 1.0)


def rate_tables(al_ref, de_ref, be_ref, dec_ref, drv_ref):
    alpha = jax.nn.sigmoid(al_ref[...])
    dec_ref[...] = 1.0 - alpha * jax.nn.sigmoid(de_ref[...])
    drv_ref[...] = alpha * be_ref[...]


def steps_of(ref, base, steps):
    return [ref[pl.ds(base + k, CHUNKS, stride=steps), :] for k in range(steps)]


def into_slabs(ref, v):
    tokens = v.shape[0]
    for j in range(v.shape[1] // LANES):
        ref[j * tokens : (j + 1) * tokens, :] = v[:, j * LANES : (j + 1) * LANES]


def from_slabs(v, tokens):
    return jnp.concatenate(
        [v[at : at + tokens] for at in range(0, v.shape[0], tokens)], 1
    )


def product(values):
    out = values[0]
    for v in values[1:]:
        out = out * v
    return out


def first_pass(rows, x_ref, g_ref, al_ref, de_ref, be_ref, keep_ref, normed_ref, low_ref, init_ref, last_ref, dec_ref, drv_ref):
    hat, _ = norm_parts(x_ref[...].astype(F32))
    normed = hat * g_ref[...]
    into_slabs(normed_ref, normed)
    low_ref[...] = normed.astype(LOW)
    rate_tables(al_ref, de_ref, be_ref, dec_ref, drv_ref)
    dims, width = al_ref.shape
    tokens = x_ref.shape[0]
    length = tokens // rows
    steps = length // CHUNKS

    def lane(j, carry):
        lanes = pl.ds(pl.multiple_of(j * LANES, LANES), LANES)
        for row in range(rows):
            token = steps_of(normed_ref, j * tokens + row * length, steps)
            kept = steps_of(keep_ref, row * length, steps)
            whole = product(kept)
            for n in range(dims):
                d, b = bcast(dec_ref, n, lanes), bcast(drv_ref, n, lanes)
                s = b * token[0]
                for k in range(1, steps):
                    s = (kept[k] * d) * s + b * token[k]
                a = power(d, steps) * whole
                for by in (1, 2, 4):
                    s = s + a * shifted(s, by, 0.0)
                    a = a * shifted(a, by, 1.0)
                init_ref[pl.ds((row * dims + n) * CHUNKS, CHUNKS), lanes] = shifted(s, 1, 0.0)
                last_ref[pl.ds(row * dims + n, 1), lanes] = s[CHUNKS - 1 :, :]
        return carry

    lax.fori_loop(0, width // LANES, lane, 0)


def second_pass(rows, normed_ref, init_ref, f1_ref, f2_ref, keep_ref, flag_ref, al_ref, de_ref, be_ref, eta_ref, om_ref, wz_ref, wu_ref, qg_ref, qb_ref, kg_ref, mask_ref, pre_ref, mixed_ref, zpre_ref, gate_ref, probs_ref, dec_ref, drv_ref):
    rate_tables(al_ref, de_ref, be_ref, dec_ref, drv_ref)
    dims, width = al_ref.shape
    tokens = keep_ref.shape[0]
    length = tokens // rows
    steps = length // CHUNKS

    def lane(j, carry):
        lanes = pl.ds(pl.multiple_of(j * LANES, LANES), LANES)
        omega = bcast(om_ref, 0, lanes)
        for row in range(rows):
            base = j * tokens + row * length
            token = steps_of(normed_ref, base, steps)
            kept = steps_of(keep_ref, row * length, steps)
            reach = shifted(product(kept), 1, 1.0)
            for by in (1, 2, 4):
                reach = reach * shifted(reach, by, 1.0)
            flag = bcast(flag_ref, row, pl.ds(0, LANES))
            total = [omega * t for t in token]
            for n in range(dims):
                d, b, e = bcast(dec_ref, n, lanes), bcast(drv_ref, n, lanes), bcast(eta_ref, n, lanes)
                chunk = power(d, steps)
                entering = bcast(f1_ref, row * dims + n, lanes) + (
                    power(chunk, CHUNKS) * flag
                ) * bcast(f2_ref, row * dims + n, lanes)
                s = (
                    init_ref[pl.ds((row * dims + n) * CHUNKS, CHUNKS), lanes]
                    + reach * chunk_powers(chunk, 1) * entering
                )
                for k in range(steps):
                    s = (kept[k] * d) * s + b * token[k]
                    total[k] = total[k] + e * s
            for k in range(steps):
                pre_ref[pl.ds(base + k, CHUNKS, stride=steps), :] = total[k]
        return carry

    lax.fori_loop(0, width // LANES, lane, 0)
    mixed_low = from_slabs(silu(pre_ref[...]).astype(LOW), tokens)
    mixed_ref[...] = mixed_low
    z_pre = dot(mixed_low, wz_ref[...])
    zpre_ref[...] = z_pre
    gate_ref[...] = jax.nn.sigmoid(dot(mixed_low, wu_ref[...]))
    z_low = silu(z_pre).astype(LOW).astype(F32)
    queries = (z_low * qg_ref[...] + qb_ref[...]).astype(LOW)
    keys = (z_low * kg_ref[...]).astype(LOW)
    for start in range(0, z_low.shape[0], STRETCH):
        block = slice(start, start + STRETCH)
        scores = dot_cols(queries[block], keys[block]) * z_low.shape[1] ** (-0.5)
        scores = jnp.where(mask_ref[block, :] > 0.5, scores, -1e30)
        shift = jnp.exp(scores - jnp.max(scores, -1, keepdims=True))
        probs_ref[block, :] = shift / jnp.sum(shift, -1, keepdims=True)


def value_part(normed_ref, mixed_ref, probs_ref, va_ref, ra_ref, vb_ref, rb_ref, vpre_ref, rpre_ref, att_ref, united_ref):
    tokens = normed_ref.shape[0]
    for i, (v_ref, r_ref) in enumerate(((va_ref, ra_ref), (vb_ref, rb_ref))):
        value_pre = dot(normed_ref[...], v_ref[...])
        reset_pre = dot(mixed_ref[...], r_ref[...])
        vpre_ref[i] = value_pre
        rpre_ref[i] = reset_pre
        values = silu(value_pre).astype(LOW)
        for start in range(0, tokens, STRETCH):
            block = slice(start, start + STRETCH)
            att_ref[i, block, :] = dot(probs_ref[block, :].astype(LOW), values[block])
        united_ref[i] = (silu(reset_pre) * att_ref[i]).astype(LOW)


def blend_part(offs_ref, x_ref, mixed_ref, gate_ref, u0_ref, u1_ref, ga_ref, gb_ref, gain_ref, hpre_ref, blended_ref, second_ref, whid_ref):
    cols = whid_ref.shape[0] // 4
    for r in range(4):
        whid_ref[pl.ds(pl.multiple_of(offs_ref[r], 64), cols), :] = (ga_ref, gb_ref)[r % 2][r // 2, :cols, :]
    hidden_pre = dot(mixed_ref[...], whid_ref[...])
    for r in range(4):
        united = (u0_ref, u1_ref)[r // 2][r % 2]
        hidden_pre = hidden_pre + dot(united, (ga_ref, gb_ref)[r % 2][r // 2, cols:, :])
    hpre_ref[...] = hidden_pre
    x = x_ref[...].astype(F32)
    blended = x + gate_ref[...] * (silu(hidden_pre) - x)
    blended_ref[...] = blended
    hat, _ = norm_parts(blended)
    second_ref[...] = (hat * gain_ref[...]).astype(LOW)


def ffn_part(second_ref, cot_ref, ia_ref, ib_ref, oa_ref, ob_ref, out_ref, sg_ref, keep_ref, send_ref):
    second, cot = second_ref[...], cot_ref[...]
    depth, units = ia_ref.shape
    half = depth // 2
    for i, (in_ref, fo_ref, pack_ref) in enumerate(
        ((ia_ref, oa_ref, keep_ref), (ib_ref, ob_ref, send_ref))
    ):
        up_pre = dot(second, in_ref[...])
        activated = silu(up_pre).astype(LOW)
        up_grad = (dot_cols(cot, fo_ref[...]) * silu_slope(up_pre)).astype(LOW)
        out = dot(activated, fo_ref[...])
        back = dot_cols(up_grad, in_ref[...])
        out_ref[...] = out if i == 0 else out_ref[...] + out
        sg_ref[...] = back if i == 0 else sg_ref[...] + back
        kind = pack_ref.dtype
        pack_ref[:depth, :] = dot_rows(second, up_grad).astype(kind)
        for h in range(2):
            pack_ref[depth + h * units : depth + (h + 1) * units, :] = dot_rows(
                activated, cot[:, h * half : (h + 1) * half]
            ).astype(kind)


def blend_back(offs_ref, x_ref, cot_ref, blended_ref, s0_ref, s1_ref, o0_ref, o1_ref, hpre_ref, gate_ref, mixed_ref, gain_ref, wu_ref, whid_ref, y_ref, direct_ref, hidden_ref, mg_ref, gg_ref, keep_ref, send_ref, full_ref):
    blended = blended_ref[...]
    y_ref[...] = (blended + (o0_ref[...] + o1_ref[...])).astype(LOW)
    second_grad = s0_ref[...] + s1_ref[...]
    hat, scale = norm_parts(blended)
    gg_ref[...] = jnp.sum(second_grad * hat, 0, keepdims=True)
    grad = cot_ref[...].astype(F32) + norm_back(second_grad * gain_ref[...], hat, scale)
    gate, hidden_pre, x = gate_ref[...], hpre_ref[...], x_ref[...].astype(F32)
    direct_ref[...] = grad * (1.0 - gate)
    hidden_low = (grad * gate * silu_slope(hidden_pre)).astype(LOW)
    gate_low = (grad * (silu(hidden_pre) - x) * gate * (1.0 - gate)).astype(LOW)
    hidden_ref[...] = hidden_low
    mg_ref[...] = dot_cols(gate_low, wu_ref[...]) + dot_cols(hidden_low, whid_ref[...])
    width = x.shape[1]
    cols, half = width // 4, width // 2
    for i, low in enumerate((gate_low, hidden_low)):
        full_ref[...] = dot_rows(mixed_ref[...], low)
        for r in range(4):
            pack_ref = (keep_ref, send_ref)[r % 2]
            rows = pl.ds(pl.multiple_of(offs_ref[r], 64), cols)
            for h in range(2):
                at = (2 * i + h) * cols
                pack_ref[r // 2, at : at + cols, :] = full_ref[
                    rows, h * half : (h + 1) * half
                ].astype(pack_ref.dtype)


def value_back(part, hidden_ref, normed_ref, mixed_ref, probs_ref, vpre_ref, rpre_ref, att_ref, united_ref, ga_ref, gb_ref, va_ref, ra_ref, vb_ref, rb_ref, ng_ref, mg_ref, pg_ref, *packs):
    hidden, normed, mixed = hidden_ref[...], normed_ref[...], mixed_ref[...]
    tokens, depth = hidden.shape
    units = va_ref.shape[1]
    cols = ga_ref.shape[1] - units
    half = depth // 2
    for i, (g_ref, v_ref, r_ref, pack) in enumerate(
        ((ga_ref, va_ref, ra_ref, packs[:2]), (gb_ref, vb_ref, rb_ref, packs[2:]))
    ):
        gate_pack, value_pack = pack
        kind = gate_pack.dtype
        united_grad = dot_cols(hidden, g_ref[part, cols:, :])
        reset_pre, value_pre = rpre_ref[i], vpre_ref[i]
        reset_low = (united_grad * att_ref[i] * silu_slope(reset_pre)).astype(LOW)
        attended_low = (united_grad * silu(reset_pre)).astype(LOW)
        values = silu(value_pre).astype(LOW)
        parts = []
        for start in range(0, tokens, STRETCH):
            block = slice(start, start + STRETCH)
            parts.append(dot_rows(probs_ref[block, :].astype(LOW), attended_low[block]))
            back = dot_cols(attended_low[block], values[block])
            first = i == 0 and part == 1
            pg_ref[block, :] = back if first else pg_ref[block, :] + back
        value_low = (jnp.concatenate(parts, 0) * silu_slope(value_pre)).astype(LOW)
        into_normed = dot_cols(value_low, v_ref[...])
        into_mixed = dot_cols(reset_low, r_ref[...])
        first = i == 0 and part == 1
        ng_ref[...] = into_normed if first else ng_ref[...] + into_normed
        mg_ref[...] = into_mixed if first else mg_ref[...] + into_mixed
        gate_pack[part, :depth, :] = dot_rows(mixed, reset_low).astype(kind)
        for h in range(2):
            gate_pack[part, depth + h * units : depth + (h + 1) * units, :] = dot_rows(
                united_ref[i], hidden[:, h * half : (h + 1) * half]
            ).astype(kind)
        value_pack[part] = dot_rows(normed, value_low).astype(kind)


def third_pass(rows, zpre_ref, probs_ref, p_ref, qg_ref, qb_ref, kg_ref, wz_ref, mixed_ref, m0_ref, m1_ref, pre_ref, keep_ref, al_ref, de_ref, pg_ref, dz_ref, small_ref, im_ref, iv_ref, lm_ref, lv_ref, qk_ref):
    z_pre = zpre_ref[...]
    z_low = silu(z_pre).astype(LOW).astype(F32)
    queries = (z_low * qg_ref[...] + qb_ref[...]).astype(LOW)
    keys = (z_low * kg_ref[...]).astype(LOW)
    for start in range(0, z_low.shape[0], STRETCH):
        block = slice(start, start + STRETCH)
        probs = probs_ref[block, :]
        grad = p_ref[block, :]
        grad = probs * (grad - jnp.sum(probs * grad, -1, keepdims=True)) * z_low.shape[1] ** (-0.5)
        high = grad.astype(LOW)
        rest = (grad - high.astype(F32)).astype(LOW)
        qk_ref[0, block, :] = dot(high, keys[block]) + dot(rest, keys[block])
        qk_ref[1, block, :] = dot_rows(high, queries[block]) + dot_rows(rest, queries[block])
    query_grad, key_grad = qk_ref[0], qk_ref[1]
    small_ref[...] = jnp.zeros_like(small_ref)
    small_ref[0:1, :] = jnp.sum(query_grad * z_low, 0, keepdims=True)
    small_ref[1:2, :] = jnp.sum(query_grad, 0, keepdims=True)
    small_ref[2:3, :] = jnp.sum(key_grad * z_low, 0, keepdims=True)
    z_grad = ((query_grad * qg_ref[...] + key_grad * kg_ref[...]) * silu_slope(z_pre)).astype(LOW)
    dz_ref[...] = dot_rows(mixed_ref[...], z_grad)
    mixed_grad = m0_ref[...] + m1_ref[...] + dot_cols(z_grad, wz_ref[...])
    into_slabs(pg_ref, mixed_grad)
    pg_ref[...] = pg_ref[...] * silu_slope(pre_ref[...])
    dims, width = al_ref.shape
    tokens = z_pre.shape[0]
    length = tokens // rows
    steps = length // CHUNKS

    def lane(j, carry):
        lanes = pl.ds(pl.multiple_of(j * LANES, LANES), LANES)
        for row in range(rows):
            token = steps_of(pg_ref, j * tokens + row * length, steps)
            kept = steps_of(keep_ref, row * length, steps)
            whole = product(kept)
            for n in range(dims):
                alpha = jax.nn.sigmoid(bcast(al_ref, n, lanes))
                d = 1.0 - alpha * jax.nn.sigmoid(bcast(de_ref, n, lanes))
                mu = token[steps - 1]
                m = (kept[steps - 1] * d) * mu
                v = kept[steps - 1] * mu
                for k in range(steps - 2, -1, -1):
                    mu = token[k] + m
                    rate = kept[k] * d
                    m = rate * mu
                    v = kept[k] * mu + rate * v
                a = power(d, steps) * whole
                b = steps * power(d, steps - 1) * whole
                for by in (-1, -2, -4):
                    mp, vp = shifted(m, by, 0.0), shifted(v, by, 0.0)
                    ap, bp = shifted(a, by, 1.0), shifted(b, by, 0.0)
                    v = v + a * vp + b * mp
                    m = m + a * mp
                    b = a * bp + b * ap
                    a = a * ap
                at = pl.ds((row * dims + n) * CHUNKS, CHUNKS)
                im_ref[at, lanes] = shifted(m, -1, 0.0)
                iv_ref[at, lanes] = shifted(v, -1, 0.0)
                lm_ref[pl.ds(row * dims + n, 1), lanes] = m[0:1, :]
                lv_ref[pl.ds(row * dims + n, 1), lanes] = v[0:1, :]
        return carry

    lax.fori_loop(0, width // LANES, lane, 0)


def back_pass(rows, *refs):
    offs_ref, x_ref, cot_ref, blended_ref, s0_ref, s1_ref, o0_ref, o1_ref, hpre_ref, gate_ref = refs[:10]
    mixed_ref, gain_ref, wu_ref, whid_ref, normed_ref, probs_ref = refs[10:16]
    own_part, far_part, (ga_ref, gb_ref), weights = refs[16:20], refs[20:24], refs[24:26], refs[26:34]
    zpre_ref, qg_ref, qb_ref, kg_ref, wz_ref, pre_ref, keep_ref, al_ref, de_ref = refs[34:43]
    y_ref, direct_ref, gg_ref, pair_keep_ref, pair_send_ref, ng_ref = refs[43:49]
    packs, outs = refs[49:53], refs[53:59]
    mg_ref, p_ref, qk_ref, m0_ref, full_ref, hidden_ref, dz_ref = refs[59:]
    blend_back(
        offs_ref, x_ref, cot_ref, blended_ref, s0_ref, s1_ref, o0_ref, o1_ref, hpre_ref, gate_ref,
        mixed_ref, gain_ref, wu_ref, whid_ref, y_ref, direct_ref, hidden_ref, m0_ref, gg_ref,
        pair_keep_ref, pair_send_ref, full_ref,
    )
    for part, parts in ((1, far_part), (0, own_part)):
        value_back(
            part, hidden_ref, normed_ref, mixed_ref, probs_ref, *parts, ga_ref, gb_ref,
            *weights[4 * part : 4 * part + 4], ng_ref, mg_ref, p_ref, *packs,
        )
    third_pass(
        rows, zpre_ref, probs_ref, p_ref, qg_ref, qb_ref, kg_ref, wz_ref, mixed_ref, m0_ref,
        mg_ref, pre_ref, keep_ref, al_ref, de_ref, outs[0], dz_ref, *outs[1:], qk_ref,
    )
    width, zd = dz_ref.shape
    blocks, cols = width // (2 * zd), width // 4
    share = cols // blocks
    for r in range(4):
        pack_ref = (pair_keep_ref, pair_send_ref)[r % 2]
        for c in range(blocks):
            rows_at = pl.ds(pl.multiple_of(offs_ref[r] + c * share, 64), share)
            pack_ref[r // 2, 4 * cols : 4 * cols + share, c * zd : (c + 1) * zd] = dz_ref[
                rows_at, :
            ].astype(pack_ref.dtype)
        pack_ref[r // 2, 4 * cols + share :, :] = jnp.zeros((share, width // 2), pack_ref.dtype)


def fourth_pass(rows, pg_ref, normed_ref, im_ref, iv_ref, near_ref, far_ref, keep_ref, flag_ref, al_ref, de_ref, be_ref, eta_ref, om_ref, n0_ref, x_ref, g_ref, direct_ref, gg_ref, qk_ref, xg_ref, sums_ref, dec_ref, drv_ref, ng_ref):
    rate_tables(al_ref, de_ref, be_ref, dec_ref, drv_ref)
    dims, width = al_ref.shape
    tokens = keep_ref.shape[0]
    length = tokens // rows
    steps = length // CHUNKS
    span = rows * dims
    sums_ref[...] = jnp.zeros_like(sums_ref)

    def lane(j, carry):
        lanes = pl.ds(pl.multiple_of(j * LANES, LANES), LANES)
        omega = bcast(om_ref, 0, lanes)
        for row in range(rows):
            base = j * tokens + row * length
            grad = steps_of(pg_ref, base, steps)
            token = steps_of(normed_ref, base, steps)
            kept = steps_of(keep_ref, row * length, steps)
            reach = shifted(product(kept), -1, 1.0)
            for by in (-1, -2, -4):
                reach = reach * shifted(reach, by, 1.0)
            place = lax.broadcasted_iota(jnp.int32, (CHUNKS, LANES), 0)
            later = (steps * (CHUNKS - 1 - place)).astype(F32)
            flag = bcast(flag_ref, row, pl.ds(0, LANES))
            total = [omega * t for t in grad]
            for n in range(dims):
                d, b, e = bcast(dec_ref, n, lanes), bcast(drv_ref, n, lanes), bcast(eta_ref, n, lanes)
                chunk = power(d, steps)
                inverse = 1.0 / d
                part = power(chunk, CHUNKS) * flag
                slope = (float(length) * part) * inverse
                at = row * dims + n
                m2 = bcast(far_ref, at, lanes)
                m_in = bcast(near_ref, at, lanes) + part * m2
                v_in = bcast(near_ref, span + at, lanes) + part * bcast(far_ref, span + at, lanes) + slope * m2
                through = reach * chunk_powers(chunk, -1)
                at = pl.ds(at * CHUNKS, CHUNKS)
                m = im_ref[at, lanes] + through * m_in
                v = iv_ref[at, lanes] + through * v_in + (later * through * inverse) * m_in
                coef = e * b
                sum_m = jnp.zeros((CHUNKS, LANES), F32)
                sum_v = jnp.zeros((CHUNKS, LANES), F32)
                for k in range(steps - 1, -1, -1):
                    mu = grad[k] + m
                    sum_m = sum_m + token[k] * mu
                    sum_v = sum_v + token[k] * v
                    total[k] = total[k] + coef * mu
                    rate = kept[k] * d
                    m = rate * mu
                    v = kept[k] * mu + rate * v
                sums_ref[pl.ds(n, 1), lanes] += jnp.sum(sum_m, 0, keepdims=True)
                sums_ref[pl.ds(dims + n, 1), lanes] += jnp.sum(sum_v, 0, keepdims=True)
            for k in range(steps):
                ng_ref[pl.ds(base + k, CHUNKS, stride=steps), :] = total[k]
        return carry

    lax.fori_loop(0, width // LANES, lane, 0)
    normed_grad = from_slabs(ng_ref[...], tokens) + n0_ref[...]
    hat, scale = norm_parts(x_ref[...].astype(F32))
    at = 2 * dims
    for j in range(width // LANES):
        slab = slice(j * tokens, (j + 1) * tokens)
        sums_ref[at : at + 1, j * LANES : (j + 1) * LANES] = jnp.sum(
            pg_ref[slab, :] * normed_ref[slab, :], 0, keepdims=True
        )
    sums_ref[at + 1 : at + 2, :] = jnp.sum(normed_grad * hat, 0, keepdims=True)
    sums_ref[at + 2 : at + 3, :] = gg_ref[...]
    zd = qk_ref.shape[1]
    for i in range(3):
        sums_ref[at + 3 : at + 4, i * zd : (i + 1) * zd] = qk_ref[i : i + 1, :]
    xg_ref[...] = (direct_ref[...] + norm_back(normed_grad * g_ref[...], hat, scale)).astype(LOW)


def swap(x, axis, bit):
    size = lax.axis_size(axis)
    return lax.ppermute(x, axis, [(i, i ^ bit) for i in range(size)])


def shift(x, by):
    size = lax.axis_size("tensor")
    return lax.ppermute(
        x, "tensor", [(i, i + by) for i in range(size) if 0 <= i + by < size]
    )


def pick(first, pair):
    return jnp.where(first, *pair)


def split_rows(v):
    half = v.shape[0] // 2
    return v[:half], v[half:]


def joined(mine, other, first):
    return pick(
        first, (jnp.concatenate([mine, other], 0), jnp.concatenate([other, mine], 0))
    )


tied = lax.optimization_barrier


def rounded(v):
    return lax.reduce_precision(v, 8, 7)


def halves(v, first):
    low, high = split_rows(v)
    return pick(first, (low, high)), pick(first, (high, low)).astype(LOW)


def reduction(kind, packs, firsts):
    bits = [1 << b for b in range(lax.axis_size("dp").bit_length() - 1)]
    lead, spread, rest = {
        "x": ([1], [2], []),
        "z": ([2], [1], []),
        "y": ([], [1, 2], []),
        "w": ([], [2, 1], []),
        "X": ([1], [], [2]),
        "Z": ([2], [], [1]),
        "Y": ([], [1], [2]),
        "W": ([], [2], [1]),
    }[kind]
    near, far = yield from packs
    for bit in lead:
        near, away = halves(near, firsts[bit])
        far, far_away = halves(far, firsts[bit])
        got = yield "dp", bit, jnp.concatenate([away, far_away], 0)
        got = got.astype(F32)
        near, far = near + got[: near.shape[0]], far + got[near.shape[0] :]
    got = yield "tensor", 2, far.astype(LOW)
    total = near + got.astype(F32)
    for bit in spread:
        total, away = halves(total, firsts[bit])
        got = yield "dp", bit, away
        total = total + got.astype(F32)
    for bit in rest + bits[2:]:
        total = rounded(total)
        got = yield "dp", bit, total.astype(LOW)
        total = total + got.astype(F32)
    low = total.astype(LOW)
    for bit in reversed(lead + spread):
        got = yield "dp", bit, low
        low = joined(low, got, firsts[bit])
    return low


def one_swap(axis, bit, v):
    got = yield axis, bit, v
    return got


def everywhere(v):
    size = v.shape[0]
    for axis in ("tensor", "dp"):
        for b in range(lax.axis_size(axis).bit_length() - 1):
            high = rounded(v)
            low = rounded(v - high)
            got = yield axis, 1 << b, jnp.concatenate([high, low], 0).astype(LOW)
            got = got.astype(F32)
            v = (high + low) + (got[:size] + got[size:])
    return v


class Pump:
    def __init__(self, token):
        self.token = token
        self.flows, self.ready, self.flying, self.done = {}, {}, {}, {}

    def gate(self, v):
        v, self.token = tied((v, self.token))
        return v

    def add(self, name, flow):
        self.flows[name] = flow
        self.ready[name] = next(flow)

    def issue(self, name):
        axis, bit, v = self.ready.pop(name)
        self.flying[name] = swap(self.gate(v), axis, bit)

    def finish(self, name):
        got = self.gate(self.flying.pop(name))
        try:
            self.ready[name] = self.flows[name].send(got)
        except StopIteration as end:
            self.done[name] = end.value

    def drain(self):
        while self.ready or self.flying:
            for name in list(self.ready):
                self.issue(name)
            for name in list(self.flying):
                self.finish(name)


def side_by_side(pack):
    half = pack.shape[0] // 2
    return jnp.concatenate([pack[:half], pack[half:]], 1)


def shards(
    layer_input,
    doc_lengths,
    norm1_gain,
    alpha_raw,
    delta_raw,
    ema_beta,
    ema_eta,
    ema_omega,
    w_z,
    q_gain,
    q_bias,
    k_gain,
    w_value,
    w_reset,
    w_update,
    w_hidden,
    w_out,
    norm2_gain,
    w_ffn_in,
    w_ffn_out,
    cotangent,
):
    member = lax.axis_index("tensor")
    place = lax.axis_index("dp")
    layer_input, begin, offs, *firsts = tied(
        (
            layer_input,
            member * layer_input.shape[1],
            (member ^ jnp.arange(4, dtype=jnp.int32)) * w_hidden.shape[0],
            (place & 1) == 0,
            (place & 2) == 0,
            (member & 1) == 0,
            (member & 2) == 0,
        )
    )
    first_core, first_chip = firsts[2:]
    firsts = dict(zip((1, 2), firsts[:2], strict=True))
    rows, length, width = layer_input.shape
    tokens = rows * length
    dims = alpha_raw.shape[0]
    zd = w_z.shape[1]
    units = w_value.shape[1]
    cols = w_hidden.shape[0]
    x = layer_input.reshape(tokens, width)
    cot = cotangent.reshape(tokens, width)
    g1, g2, om = norm1_gain[None], norm2_gain[None], ema_omega[None]
    qg, qb, kg = q_gain[None], q_bias[None], k_gain[None]

    docs = doc_lengths.shape[1]
    order = jnp.arange(docs)
    ends = jnp.sum(
        jnp.where(order[:, None] <= order[None, :], doc_lengths[:, :, None], 0), 1
    ).astype(jnp.int32)
    starts = ends - doc_lengths
    starts, ends = starts - begin, ends - begin
    places = jnp.arange(length, dtype=jnp.int32)
    docid = jnp.sum((places[None, :, None] >= ends[:, None, :]).astype(jnp.int32), 2)
    keep = 1.0 - jnp.any(places[None, :, None] == starts[:, None, :], 2).astype(F32)
    keep = jnp.broadcast_to(keep.reshape(tokens, 1), (tokens, LANES))
    blocks = docid.reshape(tokens // STRETCH, STRETCH)
    spot = jnp.arange(STRETCH)
    mask = (spot[None, :] <= spot[:, None])[None] & (blocks[:, :, None] == blocks[:, None, :])
    mask = mask.astype(F32).reshape(tokens, STRETCH)

    def unbroken(part):
        low, high = part * length, (part + 1) * length
        inside = jnp.any((starts >= low) & (starts < high), 1)
        return jnp.broadcast_to(1.0 - inside.astype(F32)[:, None], (rows, LANES))

    vm = lambda shape: pltpu.VMEM(shape, F32)
    tab = (dims, width)
    wide = (tokens, width)
    mat = 2.0 * tokens * width
    ema = 8.0 * tokens * width * dims
    chunked = (rows * dims * CHUNKS, width)
    finals = (rows * dims, width)
    slabs = (tokens * width // LANES, LANES)

    w_join = jnp.concatenate([w_hidden, w_out], 0)
    shares = (w_value, w_reset, w_join, w_ffn_in, w_ffn_out)
    bits = (1, 1, 2, 1, 1)
    pump = Pump(offs)
    beside = [swap(w, "tensor", 1) for w in (w_value, w_reset, w_ffn_in, w_ffn_out)]
    half_v, half_r, half_g, half_i, half_o = (
        pick(firsts[bit], split_rows(w)) for w, bit in zip(shares, bits, strict=True)
    )

    over_v = swap(half_v, "tensor", 2)
    beside = [pump.gate(w) for w in beside]
    over_r = swap(pump.gate(half_r), "tensor", 2)
    x = pump.gate(x)

    normed, normed_low, init, last = call(
        functools.partial(first_pass, rows),
        [(slabs, F32), (wide, LOW), (chunked, F32), (finals, F32)],
        (x, g1, alpha_raw, delta_raw, ema_beta, keep),
        ema,
        [vm(tab), vm(tab)],
    )
    last = pump.gate(last)
    over_v = pump.gate(over_v)
    other_v = swap(over_v, "dp", 1)
    f1, f2 = shift(last, 1), shift(last, 2)
    over_r = pump.gate(over_r)
    other_r = swap(over_r, "dp", 1)
    f1, f2 = pump.gate(f1), pump.gate(f2)
    over_g = swap(pump.gate(half_g), "tensor", 2)
    half_i = pump.gate(half_i)
    pre, mixed_low, z_pre, gate, probs = call(
        functools.partial(second_pass, rows),
        [(slabs, F32), (wide, LOW), ((tokens, zd), F32), (wide, F32), ((tokens, STRETCH), F32)],
        (normed, init, f1, f2, keep, unbroken(-1), alpha_raw, delta_raw, ema_beta,
         ema_eta, om, w_z, w_update, qg, qb, kg, mask),
        ema + mat * width,
        [vm(tab), vm(tab)],
    )
    split = (2, tokens, units)
    mixed_low = pump.gate(mixed_low)
    over_i = swap(half_i, "tensor", 2)
    other_v = pump.gate(other_v)
    mixed_low = pump.gate(mixed_low)

    def values(weights):
        return call(
            value_part,
            [(split, F32), (split, F32), (split, F32), (split, LOW)],
            (normed_low, mixed_low, probs, *weights),
            4 * mat * units,
        )

    own_part = values((w_value, w_reset, beside[0], beside[1]))
    united0 = pump.gate(own_part[3])
    other_r = pump.gate(other_r)
    over_g, over_i = pump.gate(over_g), pump.gate(over_i)
    over_g, over_i, half_o = pump.gate(over_g), pump.gate(over_i), pump.gate(half_o)
    over_o = swap(half_o, "tensor", 2)
    other_g = swap(over_g, "dp", 2)
    other_i = swap(over_i, "dp", 1)
    other_v, other_r = pump.gate(other_v), pump.gate(other_r)
    full_v = pump.gate(joined(over_v, other_v, firsts[1]))
    both_v = swap(full_v, "tensor", 1)
    full_r = pump.gate(joined(over_r, other_r, firsts[1]))
    both_r = swap(full_r, "tensor", 1)
    both_v, both_r = pump.gate(both_v), pump.gate(both_r)
    full_v = pump.gate(full_v)
    far_part = values((full_v, full_r, both_v, both_r))
    united1 = pump.gate(far_part[3])
    over_o = pump.gate(over_o)
    other_i = pump.gate(other_i)
    other_o = swap(over_o, "dp", 1)
    other_g = pump.gate(other_g)
    near_g = pump.gate(jnp.stack([w_join, joined(over_g, other_g, firsts[2])]))
    beside_g = swap(near_g, "tensor", 1)
    full_i = pump.gate(joined(over_i, other_i, firsts[1]))
    both_i = swap(full_i, "tensor", 1)
    beside_g = pump.gate(beside_g)
    wg = (near_g, beside_g)
    wv, wr = (w_value, beside[0], full_v, both_v), (w_reset, beside[1], full_r, both_r)
    kept_parts = ((*own_part[:3], united0), (*far_part[:3], united1))
    hidden_pre, blended, second, whid = call(
        blend_part,
        [(wide, F32), (wide, F32), (wide, LOW), ((width, width), LOW)],
        (offs, x, mixed_low, gate, united0, united1, *wg, g2),
        mat * (width + 4 * units),
        smem=(0,),
    )
    second = pump.gate(second)
    ffn_rows = width + 2 * units

    def ffn_of(weights):
        return call(
            ffn_part,
            [(wide, F32), (wide, F32), ((ffn_rows, units), LOW), ((ffn_rows, units), LOW)],
            (second, cot, *weights),
            12 * mat * units,
        )

    ffn0 = ffn_of((w_ffn_in, beside[2], w_ffn_out, beside[3]))
    back0 = pump.gate(ffn0[1])
    other_o = pump.gate(other_o)
    full_o = pump.gate(joined(over_o, other_o, firsts[1]))
    both_o = swap(full_o, "tensor", 1)
    both_i, both_o = pump.gate(both_i), pump.gate(both_o)
    ffn1 = ffn_of((full_i, both_i, full_o, both_o))
    pump.add("F0", one_swap("tensor", 1, ffn0[3]))
    pump.add("F1", one_swap("tensor", 1, ffn1[3]))
    share = cols * zd // (width // 2)
    own = (2, 4 * cols + 2 * share, width // 2)
    held = {}

    def run_back():
        outs = call(
            functools.partial(back_pass, rows),
            [(wide, LOW), (wide, F32), ((1, width), F32), (own, LOW), (own, LOW), (wide, F32),
             *[((2, 2 * width, units), LOW), ((2, width, units), LOW)] * 2,
             (slabs, F32), ((8, zd), F32), (chunked, F32), (chunked, F32), (finals, F32), (finals, F32)],
            (offs, x, cot, pump.gate(blended), ffn1[1], back0, ffn0[0], ffn1[0], hidden_pre, gate,
             mixed_low, g2, w_update, whid, normed_low, probs, *kept_parts[0], *kept_parts[1], *wg,
             wv[0], wr[0], wv[1], wr[1], wv[2], wr[2], wv[3], wr[3],
             z_pre, qg, qb, kg, w_z, pre, keep, alpha_raw, delta_raw),
            (4 * width + 28 * units) * mat,
            [vm(wide), vm((tokens, STRETCH)), vm((2, tokens, zd)), vm(wide), vm((width, width)),
             pltpu.VMEM(wide, LOW), vm((width, zd))],
            smem=(0,),
        )
        held["bb"], held["v"] = outs[:5], outs[5:10]
        held["t3"] = list(outs[10:])
        pump.token, held["t3"][4] = tied((pump.token, held["t3"][4]))

    def send_back():
        back = pump.gate(jnp.concatenate([held["t3"][4], held["t3"][5]], 0))
        held["back"] = shift(back, -1), shift(back, -2)

    def take_back():
        held["back"] = [pump.gate(v) for v in held["back"]]

    def run_fourth():
        t3 = held["t3"]
        held["t4"] = call(
            functools.partial(fourth_pass, rows),
            [(wide, LOW), ((2 * dims + 8, width), F32)],
            (t3[0], normed, t3[2], t3[3], *held["back"], keep, unbroken(1), alpha_raw,
             delta_raw, ema_beta, ema_eta, om, held["v"][0], x, g1, held["bb"][1],
             held["bb"][2], t3[1]),
            2 * ema,
            [vm(tab), vm(tab), vm(slabs)],
        )
        sums = pump.gate(held["t4"][1])
        sums = jnp.concatenate([sums[:, at : at + LANES] for at in range(0, width, LANES)], 0)
        pump.add("sm", everywhere(sums))

    def packs_of(name):
        if name in "IU":
            rows_of = slice(0, width) if name == "I" else slice(width, 2 * width)
            return tuple(
                keep[rows_of].astype(F32) + pump.done[swapped][rows_of].astype(F32)
                for keep, swapped in ((ffn0[2], "F0"), (ffn1[2], "F1"))
            )
        kept, sent = held["bb"][3:] if name == "P" else held["v"]["QN".index(name) + 1 : 5 : 2]
        got = yield "tensor", 1, sent
        both = kept.astype(F32) + got.astype(F32)
        return both[0], both[1]

    def with_shared():
        low = yield from reduction(KINDS["P"], packs_of("P"), firsts)
        v = jnp.concatenate([low[: 2 * cols], low[4 * cols : 4 * cols + share]], 0)
        for bit, first in ((2, first_chip), (1, first_core)):
            got = yield "tensor", bit, v
            v = joined(v, got, first)
        v = v.reshape(2, 2, 2 * cols + share, width // 2)
        return low[2 * cols : 4 * cols], [v[core, chip] for chip in range(2) for core in range(2)]

    def add_flow(name):
        pump.add(
            name, with_shared() if name == "P" else reduction(KINDS[name], packs_of(name), firsts)
        )

    kernels = {
        "back": run_back,
        "t4": run_fourth,
    }
    last_small = max(i for i, word in enumerate(ORDER) if word == "+sm")
    for step, word in enumerate(ORDER):
        sign, name = word[0], word[1:]
        if sign == "K":
            kernels[name]()
        elif name == "E":
            (send_back if sign == "+" else take_back)()
        elif sign == "+":
            if name in KINDS and name not in pump.flows:
                add_flow(name)
            if step == last_small:
                axis, bit, v = pump.ready["sm"]
                hold = 0.0 * jnp.clip(pump.ready["N"][2][:1, :1].astype(F32), -1.0, 1.0)
                pump.ready["sm"] = axis, bit, v + hold.astype(v.dtype)
            pump.issue(name)
        else:
            pump.finish(name)
    pump.drain()
    output, input_grad = held["bb"][0], held["t4"][0]
    sums = from_slabs(pump.done["sm"], 2 * dims + 8)
    pair_sum, gate_sum, value_sum, in_sum, fout_sum = (pump.done[n] for n in "PQNIU")

    alpha, sigma = jax.nn.sigmoid(alpha_raw), jax.nn.sigmoid(delta_raw)
    with_mu, with_nu = sums[:dims], sums[dims : 2 * dims]
    drive_grad = ema_eta * with_mu
    decay_grad = ema_eta * (alpha * ema_beta) * with_nu
    at = 2 * dims
    hidden_sum, shared = pair_sum
    update_grad = jnp.concatenate([side_by_side(v[: 2 * cols]) for v in shared], 0)
    dz_sum = jnp.concatenate(
        [v[2 * cols :, at : at + zd] for v in shared for at in range(0, width // 2, zd)], 0
    )
    return (
        output.reshape(layer_input.shape),
        input_grad.reshape(layer_input.shape),
        sums[at + 1],
        (ema_beta * drive_grad - sigma * decay_grad) * alpha * (1.0 - alpha),
        -alpha * decay_grad * sigma * (1.0 - sigma),
        alpha * drive_grad,
        (alpha * ema_beta) * with_mu,
        sums[at],
        dz_sum.astype(F32),
        sums[at + 3, :zd],
        sums[at + 3, zd : 2 * zd],
        sums[at + 3, 2 * zd : 3 * zd],
        value_sum.astype(F32),
        gate_sum[:width].astype(F32),
        update_grad.astype(F32),
        side_by_side(hidden_sum).astype(F32),
        side_by_side(gate_sum[width:]).astype(F32),
        sums[at + 2],
        in_sum.astype(F32),
        side_by_side(fout_sum).astype(F32),
    )


def solution(mesh):
    whole, by_row = P(), P("dp", "tensor", None)
    by_col, by_unit = P(None, "tensor"), P("tensor", None)
    return jax.shard_map(
        shards,
        mesh=mesh,
        in_specs=(by_row, P("dp", None), *(whole,) * 10, by_col, by_col, whole, by_unit, by_unit, whole, by_col, by_unit, by_row),
        out_specs=(by_row, by_row, *(whole,) * 10, by_col, by_col, whole, by_unit, by_unit, whole, by_col, by_unit),
        check_vma=False,
    )
```
